512 devices in a mesh: sec: 2 (over z_lo), gy: 16 (over x, z_hi), gx: 16 (over y, core).
Axes of the slice: x: 4, y: 8, z: 8 (z_hi: 4, z_lo: 2; z = z_hi * 2 + z_lo), core: 2. Of those that a mesh axis runs over, the one named last changes fastest.
Arguments:
- fields: float32 [2, 4, 1, 3072, 6144], P('sec', None, None, 'gy', 'gx'), may hold values from -6 to 6
- forcing: bfloat16 [2, 4, 1, 3072, 6144], P('sec', None, None, 'gy', 'gx'), may hold values from -4 to 4
- courant: float32 [2, 1], replicated, may hold values from -0.18 to 0.18
- diffusion: float32 [4], replicated, may hold values from 0.03 to 0.08
- nest_patch: int32 [16, 16], replicated, may hold values from 0 to 143, as said below
Outputs:
- fields_out: float32 [2, 4, 1, 3072, 6144], P('sec', None, None, 'gy', 'gx')
The draws below stay inside these ranges and needn't reach their ends.
Inputs may be any that keep to these rules, and one draw needn't show every extreme that they name: Entry [i, j] names a patch of the parent device in row nest_patch[i, j] // 9 of device column j: patch row (nest_patch[i, j] % 9) // 3 and patch column nest_patch[i, j] % 3 of its 3 x 3 patches. That device row differs from i by at most one. Nests of one column lie on distinct patches; in every column some parent device lies under exactly three nests, and none under more.
All inputs are finite; a program needn't handle non-finite values.
Results may differ from the reference program's by a relative error of at most 0.0003.
Values sent between devices are 32-bit elements; how exact they have to be, the bound alone decides.
No kernel may reach another device: no remote copies, remote signals or barrier semaphores. Data moves between devices by JAX's collectives and lax.ppermute only.
A program may use at most 128 MiB of HBM per device.

```python
import math
import jax
import jax.numpy as jnp
from jax import lax

NVAR = 4
LEV = 1
CY = 192
CX = 384
NEST_ROWS = 16
NEST_COLS = 16
NY = 3072
NX = 6144


def place_value(order, wanted):
    position = jnp.arange(9, dtype=jnp.int32)
    current = order[1]
    return jnp.where(order == wanted, current, jnp.where(position == 1, wanted, order)).astype(jnp.int32)


def draw_nest_patch(key, part):
    first_key, second_key, third_key = jax.random.split(key, 3)
    offsets = jax.random.randint(first_key, (NEST_ROWS, NEST_COLS), -1, 2)
    offsets = offsets.at[NEST_ROWS - 1, 0].set(0)
    offsets = offsets.at[0, 1].set(0)
    row_index = jnp.arange(NEST_ROWS, dtype=jnp.int32)[:, None]
    target = jnp.clip(row_index + offsets, 0, NEST_ROWS - 1)
    storm = jax.random.randint(second_key, (NEST_COLS,), 1, NEST_ROWS - 1)
    storm = storm.at[0].set(1)
    storm = storm.at[1].set(NEST_ROWS - 2)
    nearby = jnp.abs(row_index - storm[None, :]) <= 1
    target = jnp.where(nearby, storm[None, :], target)
    role = row_index - target + 1
    slot_keys = jax.random.split(third_key, NEST_ROWS * NEST_COLS)
    orders = jax.vmap(lambda single: jax.random.permutation(single, 9))(slot_keys)
    orders = orders.reshape(NEST_ROWS, NEST_COLS, 9).astype(jnp.int32)
    orders = orders.at[NEST_ROWS - 1, 0].set(place_value(orders[NEST_ROWS - 1, 0], 8))
    orders = orders.at[0, 1].set(place_value(orders[0, 1], 0))
    column_index = jnp.arange(NEST_COLS, dtype=jnp.int32)[None, :]
    slot = orders[target, column_index, role]
    return (target * 9 + slot).astype(jnp.int32)


def level_of(own_key, dims, pieces, least, largest):
    loudness, own = 1.0, jax.random.fold_in(own_key, 6)
    for dim, blocks in pieces:
        heights = jnp.exp(jax.random.uniform(jax.random.fold_in(own, dim), (blocks,), jnp.float32, least / len(pieces), largest / len(pieces)))
        loudness = loudness * jnp.repeat(heights, dims[dim] // blocks).reshape([-1 if axis == dim else 1 for axis in range(len(dims))])
    return loudness


def centred(stream_key, dims, scale, reach, shards=(), kind=jnp.bfloat16):
    values = jax.random.normal(stream_key, dims, jnp.float32) * scale
    if len(shards) > 0:
        values = level_of(stream_key, dims, shards, -0.22, 0.18) * values
    return jnp.clip(values, min=-reach, max=reach).astype(kind)


def setup_inputs(seed: int = 0) -> dict:
    key_list = jax.random.split(jax.random.key(seed), 6)
    return {
        "fields": centred(key_list[0], (2, NVAR, LEV, NY, NX), 1.0, 6.0, ((0, 2), (3, 16), (4, 16)), jnp.float32),
        "forcing": centred(key_list[1], (2, NVAR, LEV, NY, NX), 0.3, 4.0, ((0, 2), (3, 16), (4, 16))),
        "courant": jnp.clip(jax.random.uniform(key_list[2], (2, LEV), jnp.float32, -0.18, 0.18), -0.18, 0.18),
        "diffusion": jnp.clip(jnp.exp(jax.random.uniform(key_list[3], (NVAR,), jnp.float32, math.log(0.03), math.log(0.08))), 0.03, 0.08),
        "nest_patch": draw_nest_patch(jax.random.fold_in(key_list[5], 71), 0),
    }


third = 1.0 / 3.0
two_thirds = 2.0 / 3.0


def as_index(value):
    return jnp.asarray(value, dtype=jnp.int32)


def stencil(padded, centre, courant, diffusion, drive):
    eastern = padded[..., 1:-1, 2:]
    western = padded[..., 1:-1, :-2]
    southern = padded[..., 2:, 1:-1]
    northern = padded[..., :-2, 1:-1]
    along_columns = courant[0].reshape(1, -1, 1, 1)
    along_rows = courant[1].reshape(1, -1, 1, 1)
    spread = diffusion.reshape(-1, 1, 1, 1)
    return (centre - 0.5 * along_columns * (eastern - western) - 0.5 * along_rows * (southern - northern)
            + spread * (eastern + western + southern + northern - 4.0 * centre) + drive)


def refine_edge(parent_rim):
    lower_part = parent_rim[..., :-2]
    centre_part = parent_rim[..., 1:-1]
    upper_part = parent_rim[..., 2:]
    first_third = third * lower_part + two_thirds * centre_part
    last_third = two_thirds * centre_part + third * upper_part
    stacked = jnp.stack([first_third, centre_part, last_third], axis=-1)
    return stacked.reshape(parent_rim.shape[:-1] + (3 * (parent_rim.shape[-1] - 2),))


def pack_rims(padded, row_start, col_start, patch_rows, patch_cols):
    field_count = padded.shape[0]
    level_count = padded.shape[1]
    zero = as_index(0)
    row_start = as_index(row_start)
    col_start = as_index(col_start)
    upper = lax.dynamic_slice(padded, (zero, zero, row_start, as_index(col_start + 1)), (field_count, level_count, 1, patch_cols))[:, :, 0]
    lower = lax.dynamic_slice(padded, (zero, zero, as_index(row_start + patch_rows + 1), as_index(col_start + 1)), (field_count, level_count, 1, patch_cols))[:, :, 0]
    western = lax.dynamic_slice(padded, (zero, zero, row_start, col_start), (field_count, level_count, patch_rows + 2, 1))[..., 0]
    eastern = lax.dynamic_slice(padded, (zero, zero, row_start, as_index(col_start + patch_cols + 1)), (field_count, level_count, patch_rows + 2, 1))[..., 0]
    lane_pad = ((0, 0), (0, 0), (0, patch_cols - patch_rows - 2))
    return jnp.stack([upper, lower, jnp.pad(western, lane_pad), jnp.pad(eastern, lane_pad)], axis=2)


def unpack(message, patch_rows):
    upper_row = jnp.concatenate([message[..., 2, 0:1], message[..., 0, :], message[..., 3, 0:1]], axis=-1)
    lower_row = jnp.concatenate([message[..., 2, patch_rows + 1:patch_rows + 2], message[..., 1, :],
                                 message[..., 3, patch_rows + 1:patch_rows + 2]], axis=-1)
    western = message[..., 2, :patch_rows + 2]
    eastern = message[..., 3, :patch_rows + 2]
    return refine_edge(upper_row), refine_edge(lower_row), refine_edge(western), refine_edge(eastern)


def border(field, upper, lower, western, eastern):
    stacked_rows = jnp.concatenate([upper[..., None, :], field, lower[..., None, :]], axis=-2)
    corner_zero = jnp.zeros(western.shape[:-1] + (1,), field.dtype)
    west_column = jnp.concatenate([corner_zero, western, corner_zero], axis=-1)
    east_column = jnp.concatenate([corner_zero, eastern, corner_zero], axis=-1)
    return jnp.concatenate([west_column[..., None], stacked_rows, east_column[..., None]], axis=-1)


def nest_steps(field, drive_fine, edges_start, edges_end, courant, diffusion):
    fine_spread = diffusion * 3.0
    fine_force = drive_fine.astype(jnp.float32) / 3.0
    for substep in range(3):
        fraction = substep / 3.0
        upper, lower, western, eastern = [start_edge + fraction * (end_edge - start_edge)
                                          for start_edge, end_edge in zip(edges_start, edges_end)]
        padded = border(field, upper, lower, western, eastern)
        field = stencil(padded, field, courant, fine_spread, fine_force)
    return field


def reference(fields, forcing, courant, diffusion, nest_patch):
    parent = fields[0]
    nest_all = fields[1]
    nest_drive = forcing[1]
    patch_rows = CY // 3
    patch_cols = CX // 3
    margin = ((0, 0), (0, 0), (1, 1), (1, 1))
    padded_before = jnp.pad(parent, margin)
    advanced = stencil(padded_before, parent, courant, diffusion, forcing[0].astype(jnp.float32))
    padded_after = jnp.pad(advanced, margin)

    def one_nest(flat):
        flat = as_index(flat)
        nest_row = as_index(flat // NEST_COLS)
        nest_col = as_index(flat % NEST_COLS)
        code = as_index(nest_patch[nest_row, nest_col])
        owner = as_index(code // 9)
        slot = as_index(code % 9)
        row_start = as_index(owner * CY + (slot // 3) * patch_rows)
        col_start = as_index(nest_col * CX + (slot % 3) * patch_cols)
        message = jnp.stack([pack_rims(padded_before, row_start, col_start, patch_rows, patch_cols),
                             pack_rims(padded_after, row_start, col_start, patch_rows, patch_cols)], axis=2)
        zero = as_index(0)
        tile_row = as_index(nest_row * CY)
        tile_col = as_index(nest_col * CX)
        own_field = lax.dynamic_slice(nest_all, (zero, zero, tile_row, tile_col), (NVAR, LEV, CY, CX))
        own_drive = lax.dynamic_slice(nest_drive, (zero, zero, tile_row, tile_col), (NVAR, LEV, CY, CX))
        finished = nest_steps(own_field, own_drive, unpack(message[:, :, 0], patch_rows),
                              unpack(message[:, :, 1], patch_rows), courant, diffusion)
        averaged = finished.reshape(NVAR, LEV, patch_rows, 3, patch_cols, 3).mean(axis=(3, 5))
        target = (owner * 3 + slot // 3) * (3 * NEST_COLS) + nest_col * 3 + slot % 3
        return finished, averaged, as_index(target)

    finished_all, averaged_all, targets = lax.map(one_nest, jnp.arange(NEST_ROWS * NEST_COLS, dtype=jnp.int32))
    blocks = advanced.reshape(NVAR, LEV, 3 * NEST_ROWS, patch_rows, 3 * NEST_COLS, patch_cols)
    blocks = blocks.transpose(2, 4, 0, 1, 3, 5).reshape(9 * NEST_ROWS * NEST_COLS, NVAR, LEV, patch_rows, patch_cols)
    blocks = blocks.at[targets].set(averaged_all)
    corrected = blocks.reshape(3 * NEST_ROWS, 3 * NEST_COLS, NVAR, LEV, patch_rows, patch_cols)
    corrected = corrected.transpose(2, 3, 0, 4, 1, 5).reshape(NVAR, LEV, NY, NX)
    nest_final = finished_all.reshape(NEST_ROWS, NEST_COLS, NVAR, LEV, CY, CX)
    nest_final = nest_final.transpose(2, 3, 0, 4, 1, 5).reshape(NVAR, LEV, NY, NX)
    return jnp.stack([corrected, nest_final])
```

```python
import functools

import jax
import jax.numpy as jnp
from jax import lax
from jax.experimental import pallas as pl
from jax.experimental.pallas import tpu as pltpu
from jax.sharding import PartitionSpec as P


F32 = jnp.float32
BF16 = jnp.bfloat16
V, H, W = 4, 192, 384
PH, PW = H // 3, W // 3
CHUNK = 16
OFF = 160
X_ROWS = (0, PH - 1, PH, 2 * PH - 1, 2 * PH, H - 1)
Y_ROWS = (PH - 1, PH, 2 * PH - 1, 2 * PH)
X_COLS = (0, 1, PW - 1, PW, 2 * PW - 1, 2 * PW, W - 2, W - 1)
Y_COLS = (PW - 1, PW, 2 * PW - 1, 2 * PW)
AXES = ("sec", "gy", "gx")
SMEM = pl.BlockSpec(memory_space=pltpu.SMEM)


def iota(shape, dim):
    return lax.broadcasted_iota(jnp.int32, shape, dim)


def split3(a):
    high = a.astype(BF16)
    rest = a - high.astype(F32)
    middle = rest.astype(BF16)
    low = (rest - middle.astype(F32)).astype(BF16)
    return high, middle, low


def dot_right(a, m):
    return sum(jnp.dot(part, m, preferred_element_type=F32) for part in split3(a))


def dot_nt(m, a):
    dims = (((1,), (1,)), ((), ()))
    return sum(lax.dot_general(m, part, dims, preferred_element_type=F32) for part in split3(a))


def dot_left(m, a):
    return sum(jnp.dot(m, part, preferred_element_type=F32) for part in split3(a))


def select_rows(picks, width):
    row, lane = iota((8, width), 0), iota((8, width), 1)
    wanted = jnp.full((8, width), -1, jnp.int32)
    for i, pick in enumerate(picks):
        wanted = jnp.where(row == i, pick, wanted)
    return jnp.where(lane == wanted, 1.0, 0.0).astype(BF16)


def weights(k, courant):
    half_x = 0.5 * courant[0, 0]
    half_y = 0.5 * courant[1, 0]
    return 1.0 - 4.0 * k, k - half_x, k + half_x, k - half_y, k + half_y


def per_field(diffusion, scale, shape, dim, groups):
    index = iota(shape, dim)
    out = jnp.zeros(shape, F32)
    for g in range(groups):
        for f in range(V):
            out = jnp.where(index == g * V + f, scale * diffusion[f], out)
    return out


def first_kernel(ids, courant, diffusion, x, drive, y, mean, rows, cols, one, two, force, thirds):
    f = pl.program_id(0)
    parent = ids[0] == 0
    scale = jnp.where(parent, 1.0, 3.0)
    a0, ae, aw, as_, an = weights(diffusion[f] * scale, courant)
    lane = iota((1, W), 1)
    east = jnp.where(lane == W - 1, 0.0, ae)
    west = jnp.where(lane == 0, 0.0, aw)

    @pl.when(f == 0)
    def _():
        for buffer in (one, two):
            buffer[0:8, :] = jnp.zeros((8, W), F32)
            buffer[H + 8 : H + 16, :] = jnp.zeros((8, W), F32)
        cols[...] = jnp.zeros(cols.shape, F32)

    def step(source, store):
        for r in range(0, H, CHUNK):
            centre = source[8 + r : 8 + r + CHUNK, :]
            north = source[7 + r : 7 + r + CHUNK, :]
            south = source[9 + r : 9 + r + CHUNK, :]
            value = (
                a0 * centre
                + east * pltpu.roll(centre, W - 1, 1)
                + west * pltpu.roll(centre, 1, 1)
                + as_ * south
                + an * north
                + force[r : r + CHUNK, :]
            )
            store(r, value)

    def into(buffer):
        def store(r, value):
            buffer[8 + r : 8 + r + CHUNK, :] = value

        return store

    def finish(r, value):
        y[0, r : r + CHUNK, :] = value

    force[...] = drive[0].astype(F32) * jnp.where(parent, 1.0, 1.0 / 3.0)
    one[8 : 8 + H, :] = x[0]

    @pl.when(parent)
    def _():
        step(one, finish)
        for i, r in enumerate(X_ROWS):
            rows[i, pl.ds(f, 1), :] = x[0, r : r + 1, :]
        for i, r in enumerate(Y_ROWS):
            rows[6 + i, pl.ds(f, 1), :] = y[0, r : r + 1, :]
        from_x = dot_nt(select_rows(X_COLS, W), x[0])
        from_y = dot_nt(select_rows(Y_COLS, W), y[0])
        dims = (((1,), (1,)), ((), ()))
        from_drive = lax.dot_general(
            select_rows((0, W - 1), W), drive[0], dims, preferred_element_type=F32
        )
        for i in range(8):
            cols[i, pl.ds(f, 1), 0:H] = from_x[i : i + 1]
        for i in range(4):
            cols[8 + i, pl.ds(f, 1), 0:H] = from_y[i : i + 1]
        for i in range(2):
            cols[12 + i, pl.ds(f, 1), 0:H] = from_drive[i : i + 1]

    @pl.when(jnp.logical_not(parent))
    def _():
        step(one, into(two))
        step(two, into(one))
        step(one, finish)
        thirds[...] = dot_right(y[0], mean_matrix())
        total = (
            thirds[pl.ds(0, PH, stride=3), :]
            + thirds[pl.ds(1, PH, stride=3), :]
            + thirds[pl.ds(2, PH, stride=3), :]
        )
        mean[0] = total * (1.0 / 9.0)


def mean_matrix():
    gap = iota((W, PW), 0) - 3 * iota((W, PW), 1)
    return jnp.where((gap >= 0) & (gap <= 2), 1.0, 0.0).astype(BF16)


def first(ids, courant, diffusion, x, drive):
    tile = pl.BlockSpec((1, H, W), lambda f: (f, 0, 0))
    return pl.pallas_call(
        first_kernel,
        grid=(V,),
        in_specs=[SMEM, SMEM, SMEM, tile, tile],
        out_specs=[
            tile,
            pl.BlockSpec((1, PH, PW), lambda f: (f, 0, 0)),
            pl.BlockSpec((10, V, W), lambda f: (0, 0, 0)),
            pl.BlockSpec((14, V, 256), lambda f: (0, 0, 0)),
        ],
        out_shape=[
            jax.ShapeDtypeStruct((V, H, W), F32),
            jax.ShapeDtypeStruct((V, PH, PW), F32),
            jax.ShapeDtypeStruct((10, V, W), F32),
            jax.ShapeDtypeStruct((14, V, 256), F32),
        ],
        scratch_shapes=[
            pltpu.VMEM((H + 16, W), F32),
            pltpu.VMEM((H + 16, W), F32),
            pltpu.VMEM((H, W), F32),
            pltpu.VMEM((H, PW), F32),
        ],
        name="first",
    )(ids, courant, diffusion, x, drive)


def pack_kernel(cols, north, south, to_west, to_east):
    for out, picks, lo in ((to_west, (0, 1, 12), 0), (to_east, (7, 6, 13), W - 128)):
        for i, pick in enumerate(picks):
            out[i] = cols[pick]
        out[3, :, 0:128] = north[0, :, lo : lo + 128]
        out[3, :, 128:256] = north[1, :, lo : lo + 128]
        out[4, :, 0:128] = north[2, :, lo : lo + 128]
        out[4, :, 128:256] = south[2, :, lo : lo + 128]
        out[5, :, 0:128] = south[0, :, lo : lo + 128]
        out[5, :, 128:256] = south[1, :, lo : lo + 128]


def pack(cols, north, south):
    shape = jax.ShapeDtypeStruct((6, V, 256), F32)
    return pl.pallas_call(pack_kernel, out_shape=[shape, shape], name="pack")(cols, north, south)


def role_slot(nest_patch, row, column, member, count):
    nest = jnp.clip(row + member - 1, 0, count - 1)
    return nest_patch[nest, column]


def rims_kernel(
    ids, courant, diffusion, nest_patch, rows, cols, north, south, west, east, out, bank, side
):
    row, column = ids[1], ids[2]

    @pl.when(ids[0] == 0)
    def _():
        k = per_field(diffusion, 1.0, (V, 1), 0, 1)
        a0, ae, aw, as_, an = weights(k, courant)
        has_n = jnp.where(row > 0, 1.0, 0.0)
        has_s = jnp.where(row < ids[3] - 1, 1.0, 0.0)
        has_w = jnp.where(column > 0, 1.0, 0.0)
        has_e = jnp.where(column < ids[4] - 1, 1.0, 0.0)
        lane128 = iota((V, 128), 1)
        lane256 = iota((V, 256), 1)
        wide = W + 256
        lane_wide = iota((V, wide), 1)
        keep = jnp.where(lane_wide < 128, has_w, jnp.where(lane_wide >= 128 + W, has_e, 1.0))
        near_w, near_e = west[0], east[0]

        def join(before, middle, after):
            return jnp.concatenate([before, middle, after], axis=1)

        def with_sides(middle, left, right):
            return join(
                jnp.where(lane128 == 127, left, 0.0), middle, jnp.where(lane128 == 0, right, 0.0)
            )

        def lanes(value, at):
            return value[:, at : at + 1]

        def halo_row(near, far, force, inner, a_far, a_inner, exists):
            value = (
                a0 * near
                + ae * pltpu.roll(near, wide - 1, 1)
                + aw * pltpu.roll(near, 1, 1)
                + a_far * far
                + a_inner * inner
                + force
            )
            return value * keep * exists

        north_1 = join(west[3, :, 0:128], north[0], east[3, :, 0:128])
        north_2 = join(west[3, :, 128:256], north[1], east[3, :, 128:256])
        north_f = join(west[4, :, 0:128], north[2], east[4, :, 0:128])
        south_1 = join(west[5, :, 0:128], south[0], east[5, :, 0:128])
        south_2 = join(west[5, :, 128:256], south[1], east[5, :, 128:256])
        south_f = join(west[4, :, 128:256], south[2], east[4, :, 128:256])
        top = with_sides(rows[0], lanes(near_w, 0), lanes(near_e, 0))
        bottom = with_sides(rows[5], lanes(near_w, H - 1), lanes(near_e, H - 1))
        new_north = halo_row(north_1, north_2, north_f, top, an, as_, has_n)
        new_south = halo_row(south_1, south_2, south_f, bottom, as_, an, has_s)

        def with_ends(column_values, before, after):
            return jnp.where(
                lane256 == 255, before, jnp.where(lane256 == H, after, column_values)
            )

        def halo_column(near, far, force, inner, a_far, a_inner, exists, at):
            full = with_ends(near, lanes(north_1, at), lanes(south_1, at))
            value = (
                a0 * full
                + as_ * pltpu.roll(full, 255, 1)
                + an * pltpu.roll(full, 1, 1)
                + a_far * far
                + a_inner * inner
                + force
            )
            new = with_ends(value * exists, lanes(new_north, at), lanes(new_south, at))
            return full, new

        at_w, at_e = 127, 128 + W
        old_west, new_west = halo_column(near_w, west[1], west[2], cols[0], aw, ae, has_w, at_w)
        old_east, new_east = halo_column(near_e, east[1], east[2], cols[7], ae, aw, has_e, at_e)

        bank[0, 0] = north_1
        bank[1, 0] = new_north
        bank[0, 5] = south_1
        bank[1, 5] = new_south
        lane_w = iota((V, W), 1)
        for i, r in enumerate(Y_ROWS):
            place = (1, 3, 2, 4)[i]
            left, right = lanes(near_w, r), lanes(near_e, r)
            bank[0, place] = with_sides(rows[1 + i], left, right)
            fixed = (
                rows[6 + i]
                + jnp.where(lane_w == 0, aw * left, 0.0)
                + jnp.where(lane_w == W - 1, ae * right, 0.0)
            )
            bank[1, place] = with_sides(fixed, lanes(new_west, r), lanes(new_east, r))
        side[0, 0] = old_west
        side[1, 0] = new_west
        side[0, 5] = old_east
        side[1, 5] = new_east
        for i, c in enumerate(Y_COLS):
            place = (1, 3, 2, 4)[i]
            before, after = lanes(north_1, 128 + c), lanes(south_1, 128 + c)
            side[0, place] = with_ends(cols[2 + i], before, after)
            fixed = (
                cols[8 + i]
                + jnp.where(lane256 == 0, an * before, 0.0)
                + jnp.where(lane256 == H - 1, as_ * after, 0.0)
            )
            side[1, place] = with_ends(
                fixed, lanes(new_north, 128 + c), lanes(new_south, 128 + c)
            )

        for member in range(3):
            slot = lax.rem(role_slot(nest_patch, row, column, member, ids[3]), 9)
            patch_row, patch_col = lax.div(slot, 3), lax.rem(slot, 3)
            start = pl.multiple_of(patch_col * PW, PW)
            shift = OFF + 1 - PH * patch_row
            for time in range(2):
                for half in range(2):
                    rim = bank[time, patch_row + 3 * half, :, pl.ds(start, 384)]
                    rim = pltpu.roll(rim, 384 - 127, 1)[:, 0:256]
                    flank = pltpu.roll(side[time, patch_col + 3 * half], shift, 1)
                    flank = jnp.where((lane256 >= OFF) & (lane256 < OFF + PH + 2), flank, 0.0)
                    place = (2 * time + half) * V
                    out[member, place : place + V, :] = jnp.where(lane256 < PW + 2, rim, flank)


def rims(ids, courant, diffusion, nest_patch, rows, cols, north, south, west, east):
    return pl.pallas_call(
        rims_kernel,
        in_specs=[SMEM] * 4 + [pl.BlockSpec(memory_space=pltpu.VMEM)] * 6,
        out_shape=jax.ShapeDtypeStruct((3, 4 * V, 256), F32),
        scratch_shapes=[pltpu.VMEM((2, 6, V, W + 256), F32), pltpu.VMEM((2, 6, V, 256), F32)],
        name="rims",
    )(ids, courant, diffusion, nest_patch, rows, cols, north, south, west, east)


def edge_effect(u, courant, diffusion):
    k_row = per_field(diffusion, 3.0, (2 * V, 1), 0, 2)
    a0, ae, aw, as_, an = weights(k_row, courant)
    upper = iota((2 * V, 1), 0) < V
    outer, inner = jnp.where(upper, an, as_), jnp.where(upper, as_, an)
    lane = iota((2 * V, W), 1)
    east = jnp.where(lane == W - 1, 0.0, ae)
    west = jnp.where(lane == 0, 0.0, aw)
    tent = jnp.maximum(3 - jnp.abs(iota((256, W), 1) - 3 * iota((256, W), 0) + 2), 0)
    edges = dot_right(u, tent.astype(F32).astype(BF16)) * (1.0 / 3.0)
    old, new = edges[0 : 2 * V], edges[2 * V : 4 * V]

    def along_row(v):
        return a0 * v + east * pltpu.roll(v, W - 1, 1) + west * pltpu.roll(v, 1, 1)

    row_effect = depths(old, new, outer, inner, along_row)

    k_col = per_field(diffusion, 3.0, (1, 2 * V), 1, 2)
    a0, ae, aw, as_, an = weights(k_col, courant)
    left = iota((1, 2 * V), 1) < V
    outer, inner = jnp.where(left, aw, ae), jnp.where(left, ae, aw)
    down = iota((H, 2 * V), 0)
    south = jnp.where(down == H - 1, 0.0, as_)
    north = jnp.where(down == 0, 0.0, an)
    tent = jnp.maximum(3 - jnp.abs(iota((H, 256), 0) - 3 * (iota((H, 256), 1) - OFF) + 2), 0)
    tent = tent.astype(F32).astype(BF16)
    old = dot_nt(tent, u[0 : 2 * V]) * (1.0 / 3.0)
    new = dot_nt(tent, u[2 * V : 4 * V]) * (1.0 / 3.0)

    def along_column(v):
        return a0_col * v + south * pltpu.roll(v, H - 1, 0) + north * pltpu.roll(v, 1, 0)

    a0_col = a0
    return row_effect, depths(old, new, outer, inner, along_column)


def depths(old, new, outer, inner, along):
    third = (new - old) * (1.0 / 3.0)
    first_0 = outer * old
    second_0 = along(first_0) + outer * (old + third)
    second_1 = outer * first_0
    third_0 = along(second_0) + inner * second_1 + outer * (old + 2.0 * third)
    third_1 = along(second_1) + outer * second_0
    third_2 = outer * second_1
    return third_0, third_1, third_2


def last_kernel(
    ids, courant, diffusion, nest_patch, y, north, south, west, east, sent,
    got_0, got_1, got_2, mean_0, mean_1, mean_2, out, by_row, by_mean, by_col, fix_col,
):
    f = pl.program_id(0)
    row, column, count = ids[1], ids[2], ids[3]
    parent = ids[0] == 0
    got = (got_0, got_1, got_2)
    means = (mean_0, mean_1, mean_2)

    @pl.when((f == 0) & parent)
    def _():
        eye = jnp.where(iota((H, 256), 0) == iota((H, 256), 1), 1.0, 0.0).astype(BF16)
        sides = jnp.concatenate([west[0], east[0]], axis=0)
        fix_col[...] = dot_nt(eye, sides)
        rows_matrix = iota((PH, H), 1) - 3 * iota((PH, H), 0)
        rows_matrix = jnp.where((rows_matrix >= 0) & (rows_matrix <= 2), 1.0, 0.0).astype(BF16)
        for member in range(3):
            row_effect, col_effect = edge_effect(sent[member], courant, diffusion)
            by_mean[member] = dot_right(sum(row_effect), mean_matrix()) * (1.0 / 9.0)
            by_col[member, 0:PH, :] = dot_left(rows_matrix, sum(col_effect)) * (1.0 / 9.0)

    @pl.when((f == 0) & jnp.logical_not(parent))
    def _():
        member = row - lax.div(nest_patch[row, column], 9) + 1
        u = jnp.where(member == 0, got[0][...], jnp.where(member == 1, got[1][...], got[2][...]))
        row_effect, col_effect = edge_effect(u, courant, diffusion)
        for depth in range(3):
            by_row[depth] = row_effect[depth]
            by_col[depth] = col_effect[depth]

    def pick_lane(value, index):
        lane = iota(value.shape, 1)
        return jnp.sum(jnp.where(lane == index, value, 0.0), axis=1, keepdims=True)

    @pl.when(parent)
    def _():
        _, ae, aw, as_, an = weights(diffusion[f], courant)
        out[...] = y[...]
        out[0, 0:1, :] = out[0, 0:1, :] + an * north[0, pl.ds(f, 1), :]
        out[0, H - 1 : H, :] = out[0, H - 1 : H, :] + as_ * south[0, pl.ds(f, 1), :]
        lane = iota((H, 128), 1)
        left = aw * pick_lane(fix_col[...], f)
        right = ae * pick_lane(fix_col[...], V + f)
        out[0, :, 0:128] = out[0, :, 0:128] + jnp.where(lane == 0, left, 0.0)
        out[0, :, W - 128 : W] = out[0, :, W - 128 : W] + jnp.where(lane == 127, right, 0.0)
        patch_line, patch_lane = iota((PH, PW), 0), iota((PH, PW), 1)
        for member in range(3):
            nest = row + member - 1
            entry = role_slot(nest_patch, row, column, member, count)
            slot = lax.rem(entry, 9)
            valid = (nest >= 0) & (nest < count) & (lax.div(entry, 9) == row)

            @pl.when(valid)
            def _(member=member, slot=slot):
                at_row = pl.multiple_of(lax.div(slot, 3) * PH, PH)
                at_col = pl.multiple_of(lax.rem(slot, 3) * PW, PW)
                above = by_mean[member, pl.ds(f, 1), :]
                below = by_mean[member, pl.ds(V + f, 1), :]
                before = pick_lane(by_col[member, 0:PH, :], f)
                after = pick_lane(by_col[member, 0:PH, :], V + f)
                patch = (
                    means[member][0]
                    + jnp.where(patch_line == 0, above, 0.0)
                    + jnp.where(patch_line == PH - 1, below, 0.0)
                    + jnp.where(patch_lane == 0, before, 0.0)
                    + jnp.where(patch_lane == PW - 1, after, 0.0)
                )
                out[0, pl.ds(at_row, PH), pl.ds(at_col, PW)] = patch

    @pl.when(jnp.logical_not(parent))
    def _():
        out[...] = y[...]
        lane = iota((H, 128), 1)
        left = jnp.zeros((H, 128), F32)
        right = jnp.zeros((H, 128), F32)
        for depth in range(3):
            bottom = H - 1 - depth
            out[0, depth : depth + 1, :] = (
                out[0, depth : depth + 1, :] + by_row[depth, pl.ds(f, 1), :]
            )
            out[0, bottom : bottom + 1, :] = (
                out[0, bottom : bottom + 1, :] + by_row[depth, pl.ds(V + f, 1), :]
            )
            left = left + jnp.where(lane == depth, pick_lane(by_col[depth], f), 0.0)
            right = right + jnp.where(lane == 127 - depth, pick_lane(by_col[depth], V + f), 0.0)
        out[0, :, 0:128] = out[0, :, 0:128] + left
        out[0, :, W - 128 : W] = out[0, :, W - 128 : W] + right


def last(ids, courant, diffusion, nest_patch, y, north, south, west, east, sent, got, means):
    tile = pl.BlockSpec((1, H, W), lambda f: (f, 0, 0))
    patch = pl.BlockSpec((1, PH, PW), lambda f: (f, 0, 0))
    halo = pl.BlockSpec((3, V, W), lambda f: (0, 0, 0))
    flank = pl.BlockSpec((6, V, 256), lambda f: (0, 0, 0))
    message = pl.BlockSpec((4 * V, 256), lambda f: (0, 0))
    messages = pl.BlockSpec((3, 4 * V, 256), lambda f: (0, 0, 0))
    return pl.pallas_call(
        last_kernel,
        grid=(V,),
        in_specs=[SMEM] * 4
        + [tile, halo, halo, flank, flank, messages]
        + [message] * 3
        + [patch] * 3,
        out_specs=tile,
        out_shape=jax.ShapeDtypeStruct((V, H, W), F32),
        scratch_shapes=[
            pltpu.VMEM((3, 2 * V, W), F32),
            pltpu.VMEM((3, 2 * V, PW), F32),
            pltpu.VMEM((3, H, 2 * V), F32),
            pltpu.VMEM((H, 2 * V), F32),
        ],
        name="last",
    )(ids, courant, diffusion, nest_patch, y, north, south, west, east, sent, *got, *means)


def routes(sizes, source, move):
    _, n_rows, n_cols = sizes
    out = []
    for r in range(n_rows):
        for c in range(n_cols):
            to_sec, to_r, to_c = move(r, c)
            if 0 <= to_r < n_rows and 0 <= to_c < n_cols:
                out.append(
                    (
                        (source * n_rows + r) * n_cols + c,
                        (to_sec * n_rows + to_r) * n_cols + to_c,
                    )
                )
    return out


def on_device(sizes, fields, forcing, courant, diffusion, nest_patch):
    x = fields.reshape(V, H, W)
    drive = forcing.reshape(V, H, W)
    ids = jnp.stack(
        [
            lax.axis_index("sec"),
            lax.axis_index("gy"),
            lax.axis_index("gx"),
            jnp.int32(sizes[1]),
            jnp.int32(sizes[2]),
        ]
    ).astype(jnp.int32)

    def shift(value, source, move):
        return lax.ppermute(value, AXES, routes(sizes, source, move))

    downward = jnp.stack([x[:, H - 1], x[:, H - 2], drive[:, H - 1].astype(F32)])
    upward = jnp.stack([x[:, 0], x[:, 1], drive[:, 0].astype(F32)])
    north = shift(downward, 0, lambda r, c: (0, r + 1, c))
    south = shift(upward, 0, lambda r, c: (0, r - 1, c))
    y, mean, rows, cols = first(ids, courant, diffusion, x, drive)
    to_west, to_east = pack(cols, north, south)
    west = shift(to_east, 0, lambda r, c: (0, r, c + 1))
    east = shift(to_west, 0, lambda r, c: (0, r, c - 1))
    means = [shift(mean, 1, lambda r, c, m=m: (0, r + 1 - m, c)) for m in range(3)]
    sent = rims(ids, courant, diffusion, nest_patch, rows, cols, north, south, west, east)
    got = [shift(sent[m], 0, lambda r, c, m=m: (1, r + m - 1, c)) for m in range(3)]
    out = last(
        ids, courant, diffusion, nest_patch, y, north, south, west, east, sent, got, means
    )
    return out.reshape(fields.shape)


def solution(mesh):
    sizes = tuple(mesh.shape[axis] for axis in AXES)
    spec = P("sec", None, None, "gy", "gx")
    return jax.shard_map(
        functools.partial(on_device, sizes),
        mesh=mesh,
        in_specs=(spec, spec, P(), P(), P()),
        out_specs=spec,
        check_vma=False,
    )
```

```python
import functools

import jax
import jax.numpy as jnp
from jax import lax
from jax.experimental import pallas as pl
from jax.experimental.pallas import tpu as pltpu
from jax.sharding import PartitionSpec as P


F32 = jnp.float32
BF16 = jnp.bfloat16
V, H, W = 4, 192, 384
PH, PW = H // 3, W // 3
CHUNK = 16
OFF = 160


def beside(n):
    inner = (n - 1, n, 2 * n - 1, 2 * n)
    return inner, (0, 1, n - 2, n - 1, n, n + 1, 2 * n - 2, 2 * n - 1, 2 * n, 2 * n + 1, 3 * n - 2, 3 * n - 1)


IN_ROWS, BANK_ROWS = beside(PH)
IN_COLS, BANK_COLS = beside(PW)
FORCE_COLS = (0, *IN_COLS, W - 1)
AXES = ("sec", "gy", "gx")
SMEM = pl.BlockSpec(memory_space=pltpu.SMEM)
VMEM = pl.BlockSpec(memory_space=pltpu.VMEM)
ANY = pl.BlockSpec(memory_space=pl.ANY)


def iota(shape, dim):
    return lax.broadcasted_iota(jnp.int32, shape, dim)


def split3(a):
    high = a.astype(BF16)
    rest = a - high.astype(F32)
    middle = rest.astype(BF16)
    low = (rest - middle.astype(F32)).astype(BF16)
    return high, middle, low


def dot_right(a, m):
    return sum(jnp.dot(part, m, preferred_element_type=F32) for part in split3(a))


def dot_nt(m, a):
    dims = (((1,), (1,)), ((), ()))
    return sum(lax.dot_general(m, part, dims, preferred_element_type=F32) for part in split3(a))


def dot_left(m, a):
    return sum(jnp.dot(m, part, preferred_element_type=F32) for part in split3(a))


def select_rows(picks, width):
    row, lane = iota((16, width), 0), iota((16, width), 1)
    wanted = jnp.full((16, width), -1, jnp.int32)
    for i, pick in enumerate(picks):
        wanted = jnp.where(row == i, pick, wanted)
    return jnp.where(lane == wanted, 1.0, 0.0).astype(BF16)


def weights(k, courant):
    half_x = 0.5 * courant[0]
    half_y = 0.5 * courant[1]
    return 1.0 - 4.0 * k, k - half_x, k + half_x, k - half_y, k + half_y


def per_field(diffusion, scale, shape, dim, groups):
    index = iota(shape, dim)
    out = jnp.zeros(shape, F32)
    for g in range(groups):
        for f in range(V):
            out = jnp.where(index == g * V + f, scale * diffusion[f], out)
    return out


def near(*values):
    return [pltpu.with_memory_space_constraint(v, pltpu.VMEM) for v in values]


def position():
    return [lax.axis_index(axis) for axis in AXES]


def edge_kernel(x, drive, down, up, x_top, x_bottom, d_top, d_bottom, sems):
    copies = [
        pltpu.make_async_copy(x.at[:, 0:8, :], x_top, sems.at[0]),
        pltpu.make_async_copy(x.at[:, H - 8 : H, :], x_bottom, sems.at[1]),
        pltpu.make_async_copy(drive.at[:, 0:16, :], d_top, sems.at[2]),
        pltpu.make_async_copy(drive.at[:, H - 16 : H, :], d_bottom, sems.at[3]),
    ]
    for copy in copies:
        copy.start()
    for copy in copies:
        copy.wait()
    for f in range(V):
        down[0, f : f + 1] = x_bottom[f, 7:8, :]
        down[1, f : f + 1] = x_bottom[f, 6:7, :]
        down[2, f : f + 1] = d_bottom[f].astype(F32)[15:16]
        up[0, f : f + 1] = x_top[f, 0:1, :]
        up[1, f : f + 1] = x_top[f, 1:2, :]
        up[2, f : f + 1] = d_top[f].astype(F32)[0:1]


def edge(x, drive):
    shape = pltpu.VMEM((3, V, W), F32)
    return pl.pallas_call(
        edge_kernel,
        in_specs=[ANY, ANY],
        out_specs=[VMEM, VMEM],
        out_shape=[shape, shape],
        scratch_shapes=[
            pltpu.VMEM((V, 8, W), F32),
            pltpu.VMEM((V, 8, W), F32),
            pltpu.VMEM((V, 16, W), BF16),
            pltpu.VMEM((V, 16, W), BF16),
            pltpu.SemaphoreType.DMA((4,)),
        ],
        name="edge",
    )(x, drive)


def first_kernel(
    courant, diffusion, x, drive, y, mean, rows, cols, one, two, source, force, thirds, sems
):
    parent = position()[0] == 0
    scale = jnp.where(parent, 1.0, 3.0)
    lane = iota((1, W), 1)

    def load(f):
        return (
            pltpu.make_async_copy(x.at[f], one.at[f, 8 : 8 + H, :], sems.at[0, f]),
            pltpu.make_async_copy(drive.at[f], source.at[f], sems.at[1, f]),
        )

    for f in range(V):
        for copy in load(f):
            copy.start()
    for f in range(V):
        one[f, 0:8, :] = jnp.zeros((8, W), F32)
        one[f, H + 8 : H + 16, :] = jnp.zeros((8, W), F32)
    two[0:8, :] = jnp.zeros((8, W), F32)
    two[H + 8 : H + 16, :] = jnp.zeros((8, W), F32)

    def field(f, steps):
        a0, ae, aw, as_, an = weights(diffusion[f] * scale, courant)
        east = jnp.where(lane == W - 1, 0.0, ae)
        west = jnp.where(lane == 0, 0.0, aw)

        def step(old, new, at):
            for r in range(0, H, CHUNK):
                centre = old[8 + r : 8 + r + CHUNK, :]
                north = old[7 + r : 7 + r + CHUNK, :]
                south = old[9 + r : 9 + r + CHUNK, :]
                new[at + r : at + r + CHUNK, :] = (
                    a0 * centre
                    + east * pltpu.roll(centre, W - 1, 1)
                    + west * pltpu.roll(centre, 1, 1)
                    + as_ * south
                    + an * north
                    + force[r : r + CHUNK, :]
                )

        force[...] = source[f].astype(F32) * jnp.where(parent, 1.0, 1.0 / 3.0)
        mine = one.at[f]
        if steps == 3:
            step(mine, two, 8)
            step(two, mine, 8)
        step(mine, y.at[f], 0)

    @pl.when(parent)
    def _():
        cols[...] = jnp.zeros(cols.shape, F32)
        picks, force_picks = select_rows(BANK_COLS, W), select_rows(FORCE_COLS, W)
        dims = (((1,), (1,)), ((), ()))
        for f in range(V):
            for copy in load(f):
                copy.wait()
            for i, r in enumerate(BANK_ROWS):
                rows[i, f : f + 1] = one[f, 8 + r : 9 + r, :]
            for i, r in enumerate(IN_ROWS):
                band = source[f, r // 16 * 16 : r // 16 * 16 + 16, :].astype(F32)
                rows[12 + i, f : f + 1] = band[r % 16 : r % 16 + 1]
            from_x = dot_nt(picks, one[f, 8 : 8 + H, :])
            from_drive = lax.dot_general(
                force_picks, source[f], dims, preferred_element_type=F32
            )
            for i in range(12):
                cols[i, f : f + 1, 0:H] = from_x[i : i + 1]
            for i in range(6):
                cols[12 + i, f : f + 1, 0:H] = from_drive[i : i + 1]

        @pl.loop(0, V)
        def _(f):
            field(f, 1)

    @pl.when(jnp.logical_not(parent))
    def _():
        blocks = mean_matrix()

        @pl.loop(0, V)
        def _(f):
            for copy in load(f):
                copy.wait()
            field(f, 3)
            thirds[...] = dot_right(y[f], blocks)
            total = (
                thirds[pl.ds(0, PH, stride=3), :]
                + thirds[pl.ds(1, PH, stride=3), :]
                + thirds[pl.ds(2, PH, stride=3), :]
            )
            mean[f] = total * (1.0 / 9.0)


def mean_matrix():
    gap = iota((W, PW), 0) - 3 * iota((W, PW), 1)
    return jnp.where((gap >= 0) & (gap <= 2), 1.0, 0.0).astype(BF16)


def first(courant, diffusion, x, drive):
    return pl.pallas_call(
        first_kernel,
        in_specs=[SMEM, SMEM, ANY, ANY],
        out_specs=[VMEM] * 4,
        out_shape=[
            pltpu.VMEM((V, H, W), F32),
            pltpu.VMEM((V, PH, PW), F32),
            pltpu.VMEM((16, V, W), F32),
            pltpu.VMEM((18, V, 256), F32),
        ],
        scratch_shapes=[
            pltpu.VMEM((V, H + 16, W), F32),
            pltpu.VMEM((H + 16, W), F32),
            pltpu.VMEM((V, H, W), BF16),
            pltpu.VMEM((H, W), F32),
            pltpu.VMEM((H, PW), F32),
            pltpu.SemaphoreType.DMA((2, V)),
        ],
        cost_estimate=pl.CostEstimate(flops=40_000_000, transcendentals=0, bytes_accessed=20_000_000),
        name="first",
    )(courant, diffusion, x, drive)


def pack_kernel(cols, north, south, to_west, to_east):
    for out, picks, lo in ((to_west, (0, 1, 12), 0), (to_east, (11, 10, 17), W - 128)):
        for i, pick in enumerate(picks):
            out[i] = cols[pick]
        out[3, :, 0:128] = north[0, :, lo : lo + 128]
        out[3, :, 128:256] = north[1, :, lo : lo + 128]
        out[4, :, 0:128] = north[2, :, lo : lo + 128]
        out[4, :, 128:256] = south[2, :, lo : lo + 128]
        out[5, :, 0:128] = south[0, :, lo : lo + 128]
        out[5, :, 128:256] = south[1, :, lo : lo + 128]


def pack(cols, north, south):
    shape = pltpu.VMEM((6, V, 256), F32)
    return pl.pallas_call(
        pack_kernel,
        in_specs=[VMEM] * 3,
        out_specs=[VMEM] * 2,
        out_shape=[shape, shape],
        name="pack",
    )(*near(cols, north, south))


def role_slot(nest_patch, row, column, member, count):
    nest = jnp.clip(row + member - 1, 0, count - 1)
    return nest_patch[nest, column]


def rims_kernel(
    courant, diffusion, nest_patch, rows, cols, north, south, west, east, *out_bank_side
):
    *out, bank, side = out_bank_side
    section, row, column = position()
    count, columns = nest_patch.shape

    @pl.when(section == 0)
    def _():
        k = per_field(diffusion, 1.0, (V, 1), 0, 1)
        a0, ae, aw, as_, an = weights(k, courant)
        has_n = jnp.where(row > 0, 1.0, 0.0)
        has_s = jnp.where(row < count - 1, 1.0, 0.0)
        has_w = jnp.where(column > 0, 1.0, 0.0)
        has_e = jnp.where(column < columns - 1, 1.0, 0.0)
        lane128 = iota((V, 128), 1)
        lane256 = iota((V, 256), 1)
        wide = W + 256
        lane_wide = iota((V, wide), 1)
        keep = jnp.where(lane_wide < 128, has_w, jnp.where(lane_wide >= 128 + W, has_e, 1.0))
        near_w, near_e = west[0], east[0]

        def join(before, middle, after):
            return jnp.concatenate([before, middle, after], axis=1)

        def with_sides(middle, left, right):
            return join(
                jnp.where(lane128 == 127, left, 0.0), middle, jnp.where(lane128 == 0, right, 0.0)
            )

        def lanes(value, at):
            return value[:, at : at + 1]

        def halo_row(near, far, force, inner, a_far, a_inner, exists):
            value = (
                a0 * near
                + ae * pltpu.roll(near, wide - 1, 1)
                + aw * pltpu.roll(near, 1, 1)
                + a_far * far
                + a_inner * inner
                + force
            )
            return value * keep * exists

        north_1 = join(west[3, :, 0:128], north[0], east[3, :, 0:128])
        north_2 = join(west[3, :, 128:256], north[1], east[3, :, 128:256])
        north_f = join(west[4, :, 0:128], north[2], east[4, :, 0:128])
        south_1 = join(west[5, :, 0:128], south[0], east[5, :, 0:128])
        south_2 = join(west[5, :, 128:256], south[1], east[5, :, 128:256])
        south_f = join(west[4, :, 128:256], south[2], east[4, :, 128:256])
        top = with_sides(rows[0], lanes(near_w, 0), lanes(near_e, 0))
        bottom = with_sides(rows[11], lanes(near_w, H - 1), lanes(near_e, H - 1))
        new_north = halo_row(north_1, north_2, north_f, top, an, as_, has_n)
        new_south = halo_row(south_1, south_2, south_f, bottom, as_, an, has_s)

        def with_ends(column_values, before, after):
            return jnp.where(
                lane256 == 255, before, jnp.where(lane256 == H, after, column_values)
            )

        def halo_column(near, far, force, inner, a_far, a_inner, exists, at):
            full = with_ends(near, lanes(north_1, at), lanes(south_1, at))
            value = (
                a0 * full
                + as_ * pltpu.roll(full, 255, 1)
                + an * pltpu.roll(full, 1, 1)
                + a_far * far
                + a_inner * inner
                + force
            )
            new = with_ends(value * exists, lanes(new_north, at), lanes(new_south, at))
            return full, new

        at_w, at_e = 127, 128 + W
        old_west, new_west = halo_column(near_w, west[1], west[2], cols[0], aw, ae, has_w, at_w)
        old_east, new_east = halo_column(near_e, east[1], east[2], cols[11], ae, aw, has_e, at_e)

        bank[0, 0] = north_1
        bank[1, 0] = new_north
        bank[0, 5] = south_1
        bank[1, 5] = new_south
        blank = jnp.zeros((V, 128), F32)
        for i, r in enumerate(IN_ROWS):
            place, at = (1, 3, 2, 4)[i], BANK_ROWS.index(r)
            old = with_sides(rows[at], lanes(near_w, r), lanes(near_e, r))
            bank[0, place] = old
            new = (
                a0 * old
                + ae * pltpu.roll(old, wide - 1, 1)
                + aw * pltpu.roll(old, 1, 1)
                + join(blank, an * rows[at - 1] + as_ * rows[at + 1] + rows[12 + i], blank)
            )
            bank[1, place] = jnp.where(
                lane_wide == 127,
                lanes(new_west, r),
                jnp.where(lane_wide == 128 + W, lanes(new_east, r), new),
            )
        side[0, 0] = old_west
        side[1, 0] = new_west
        side[0, 5] = old_east
        side[1, 5] = new_east
        for i, c in enumerate(IN_COLS):
            place, at = (1, 3, 2, 4)[i], BANK_COLS.index(c)
            old, new = halo_column(
                cols[at], cols[at - 1], cols[12 + FORCE_COLS.index(c)], cols[at + 1], aw, ae, 1.0, 128 + c
            )
            side[0, place] = old
            side[1, place] = new

        for member in range(3):
            slot = lax.rem(role_slot(nest_patch, row, column, member, count), 9)
            patch_row, patch_col = lax.div(slot, 3), lax.rem(slot, 3)
            start = pl.multiple_of(patch_col * PW, PW)
            shift = OFF + 1 - PH * patch_row
            for time in range(2):
                for half in range(2):
                    rim = bank[time, patch_row + 3 * half, :, pl.ds(start, 384)]
                    rim = pltpu.roll(rim, 384 - 127, 1)[:, 0:256]
                    flank = pltpu.roll(side[time, patch_col + 3 * half], shift, 1)
                    flank = jnp.where((lane256 >= OFF) & (lane256 < OFF + PH + 2), flank, 0.0)
                    place = (2 * time + half) * V
                    out[member][place : place + V, :] = jnp.where(lane256 < PW + 2, rim, flank)


def rims(courant, diffusion, nest_patch, rows, cols, north, south, west, east):
    return pl.pallas_call(
        rims_kernel,
        in_specs=[SMEM] * 3 + [VMEM] * 6,
        out_specs=[VMEM] * 3,
        out_shape=[pltpu.VMEM((4 * V, 256), F32)] * 3,
        scratch_shapes=[pltpu.VMEM((2, 6, V, W + 256), F32), pltpu.VMEM((2, 6, V, 256), F32)],
        name="rims",
    )(courant, diffusion, nest_patch, *near(rows, cols, north, south, west, east))


def edge_effect(u, courant, diffusion):
    k_row = per_field(diffusion, 3.0, (2 * V, 1), 0, 2)
    a0, ae, aw, as_, an = weights(k_row, courant)
    upper = iota((2 * V, 1), 0) < V
    outer, inner = jnp.where(upper, an, as_), jnp.where(upper, as_, an)
    lane = iota((2 * V, W), 1)
    east = jnp.where(lane == W - 1, 0.0, ae)
    west = jnp.where(lane == 0, 0.0, aw)
    tent = jnp.maximum(3 - jnp.abs(iota((256, W), 1) - 3 * iota((256, W), 0) + 2), 0)
    edges = dot_right(u, tent.astype(F32).astype(BF16)) * (1.0 / 3.0)
    old, new = edges[0 : 2 * V], edges[2 * V : 4 * V]

    def along_row(v):
        return a0 * v + east * pltpu.roll(v, W - 1, 1) + west * pltpu.roll(v, 1, 1)

    row_effect = depths(old, new, outer, inner, along_row)

    k_col = per_field(diffusion, 3.0, (1, 2 * V), 1, 2)
    a0, ae, aw, as_, an = weights(k_col, courant)
    left = iota((1, 2 * V), 1) < V
    outer, inner = jnp.where(left, aw, ae), jnp.where(left, ae, aw)
    down = iota((H, 2 * V), 0)
    south = jnp.where(down == H - 1, 0.0, as_)
    north = jnp.where(down == 0, 0.0, an)
    tent = jnp.maximum(3 - jnp.abs(iota((H, 256), 0) - 3 * (iota((H, 256), 1) - OFF) + 2), 0)
    tent = tent.astype(F32).astype(BF16)
    old = dot_nt(tent, u[0 : 2 * V]) * (1.0 / 3.0)
    new = dot_nt(tent, u[2 * V : 4 * V]) * (1.0 / 3.0)

    def along_column(v):
        return a0_col * v + south * pltpu.roll(v, H - 1, 0) + north * pltpu.roll(v, 1, 0)

    a0_col = a0
    return row_effect, depths(old, new, outer, inner, along_column)


def depths(old, new, outer, inner, along):
    third = (new - old) * (1.0 / 3.0)
    first_0 = outer * old
    second_0 = along(first_0) + outer * (old + third)
    second_1 = outer * first_0
    third_0 = along(second_0) + inner * second_1 + outer * (old + 2.0 * third)
    third_1 = along(second_1) + outer * second_0
    third_2 = outer * second_1
    return third_0, third_1, third_2


def spread(values, depth):
    block, lane = iota((2 * V, 2 * V * 128), 0), iota((2 * V, 2 * V * 128), 1)
    target = block * 128 + jnp.where(block < V, depth, 127 - depth)
    return dot_right(values, jnp.where(lane == target, 1.0, 0.0).astype(BF16))


def last_kernel(
    courant, diffusion, nest_patch, y, north, south, west, east,
    sent_0, sent_1, sent_2, got_0, got_1, got_2, mean_0, mean_1, mean_2, out, tile, sems,
):
    section, row, column = position()
    count = nest_patch.shape[0]
    parent = section == 0
    sent, got, means = (sent_0, sent_1, sent_2), (got_0, got_1, got_2), (mean_0, mean_1, mean_2)

    def sides(f, both):
        tile[f, :, 0:128] = y[f, :, 0:128] + both[:, f * 128 : (f + 1) * 128]
        tile[f, :, 128 : W - 128] = y[f, :, 128 : W - 128]
        right = (V + f) * 128
        tile[f, :, W - 128 : W] = y[f, :, W - 128 : W] + both[:, right : right + 128]

    def send(f):
        return pltpu.make_async_copy(tile.at[f], out.at[f], sems.at[f])

    @pl.when(parent)
    def _():
        _, ae, aw, _, _ = weights(per_field(diffusion, 1.0, (1, 2 * V), 1, 2), courant)
        eye = jnp.where(iota((H, H), 0) == iota((H, H), 1), 1.0, 0.0).astype(BF16)
        beyond = jnp.concatenate([west[0, :, 0:H], east[0, :, 0:H]], axis=0)
        outer = jnp.where(iota((1, 2 * V), 1) < V, aw, ae)
        both = spread(dot_nt(eye, beyond) * outer, 0)
        for f in range(V):
            _, _, _, as_, an = weights(diffusion[f], courant)
            sides(f, both)
            tile[f, 0:1, :] = tile[f, 0:1, :] + an * north[0, f : f + 1, :]
            tile[f, H - 1 : H, :] = tile[f, H - 1 : H, :] + as_ * south[0, f : f + 1, :]
        thirds = iota((PH, H), 1) - 3 * iota((PH, H), 0)
        thirds = jnp.where((thirds >= 0) & (thirds <= 2), 1.0, 0.0).astype(BF16)
        line = iota((PH, PW), 0)
        for member in range(3):
            nest = row + member - 1
            entry = role_slot(nest_patch, row, column, member, count)
            slot = lax.rem(entry, 9)

            @pl.when((nest >= 0) & (nest < count) & (lax.div(entry, 9) == row))
            def _(member=member, slot=slot):
                at_row = pl.multiple_of(lax.div(slot, 3) * PH, PH)
                at_col = pl.multiple_of(lax.rem(slot, 3) * PW, PW)
                row_effect, col_effect = edge_effect(sent[member][...], courant, diffusion)
                by_row = dot_right(sum(row_effect), mean_matrix()) * (1.0 / 9.0)
                by_col = spread(dot_left(thirds, sum(col_effect)) * (1.0 / 9.0), 0)
                for f in range(V):
                    right = (V + f) * 128
                    tile[f, pl.ds(at_row, PH), pl.ds(at_col, PW)] = (
                        means[member][f]
                        + jnp.where(line == 0, by_row[f : f + 1], 0.0)
                        + jnp.where(line == PH - 1, by_row[V + f : V + f + 1], 0.0)
                        + by_col[:, f * 128 : (f + 1) * 128]
                        + by_col[:, right : right + 128]
                    )

        for f in range(V):
            send(f).start()

    @pl.when(jnp.logical_not(parent))
    def _():
        member = row - lax.div(nest_patch[row, column], 9) + 1
        u = jnp.where(member == 0, got[0][...], jnp.where(member == 1, got[1][...], got[2][...]))
        row_effect, col_effect = edge_effect(u, courant, diffusion)
        both = sum(spread(col_effect[depth], depth) for depth in range(3))
        for f in range(V):
            sides(f, both)
            for depth in range(3):
                bottom = H - 1 - depth
                tile[f, depth : depth + 1, :] = (
                    tile[f, depth : depth + 1, :] + row_effect[depth][f : f + 1]
                )
                tile[f, bottom : bottom + 1, :] = (
                    tile[f, bottom : bottom + 1, :] + row_effect[depth][V + f : V + f + 1]
                )
            send(f).start()

    for f in range(V):
        send(f).wait()


def last(courant, diffusion, nest_patch, y, north, south, west, east, sent, got, means):
    return pl.pallas_call(
        last_kernel,
        in_specs=[SMEM] * 3 + [VMEM] * 14,
        out_specs=ANY,
        out_shape=jax.ShapeDtypeStruct((V, H, W), F32),
        scratch_shapes=[pltpu.VMEM((V, H, W), F32), pltpu.SemaphoreType.DMA((V,))],
        name="last",
    )(
        courant, diffusion, nest_patch,
        *near(y, north, south, west, east, *sent, *got, *means),
    )


def routes(sizes, source, move):
    _, n_rows, n_cols = sizes
    out = []
    for r in range(n_rows):
        for c in range(n_cols):
            to_sec, to_r, to_c = move(r, c)
            if 0 <= to_r < n_rows and 0 <= to_c < n_cols:
                out.append(
                    (
                        (source * n_rows + r) * n_cols + c,
                        (to_sec * n_rows + to_r) * n_cols + to_c,
                    )
                )
    return out


def on_device(sizes, *arrays):
    return compute(sizes, *arrays)


def compute(sizes, fields, forcing, courant, diffusion, nest_patch):
    x = fields.reshape(V, H, W)
    drive = forcing.reshape(V, H, W)
    courant = courant.reshape(2)

    def shift(value, source, move):
        return lax.ppermute(value, AXES, routes(sizes, source, move))

    downward, upward = edge(x, drive)
    north = shift(downward, 0, lambda r, c: (0, r + 1, c))
    south = shift(upward, 0, lambda r, c: (0, r - 1, c))
    y, mean, rows, cols = first(courant, diffusion, x, drive)
    to_west, to_east = pack(cols, north, south)
    west = shift(to_east, 0, lambda r, c: (0, r, c + 1))
    east = shift(to_west, 0, lambda r, c: (0, r, c - 1))
    means = [shift(mean, 1, lambda r, c, m=m: (0, r + 1 - m, c)) for m in range(3)]
    sent = rims(courant, diffusion, nest_patch, rows, cols, north, south, west, east)
    got = [shift(sent[m], 0, lambda r, c, m=m: (1, r + m - 1, c)) for m in range(3)]
    out = last(courant, diffusion, nest_patch, y, north, south, west, east, sent, got, means)
    return out.reshape(fields.shape)


def solution(mesh):
    sizes = tuple(mesh.shape[axis] for axis in AXES)
    spec = P("sec", None, None, "gy", "gx")
    return jax.shard_map(
        functools.partial(on_device, sizes),
        mesh=mesh,
        in_specs=(spec, spec, P(), P(), P()),
        out_specs=spec,
        check_vma=False,
    )
```

```python
import functools

import jax
import jax.numpy as jnp
from jax import lax
from jax.experimental import pallas as pl
from jax.experimental.pallas import tpu as pltpu
from jax.sharding import PartitionSpec as P


F32 = jnp.float32
BF16 = jnp.bfloat16
V, H, W = 4, 192, 384
PH, PW = H // 3, W // 3
CHUNK = 16
OFF = 160


def beside(n):
    inner = (n - 1, n, 2 * n - 1, 2 * n)
    return inner, (0, 1, n - 2, n - 1, n, n + 1, 2 * n - 2, 2 * n - 1, 2 * n, 2 * n + 1, 3 * n - 2, 3 * n - 1)


IN_ROWS, BANK_ROWS = beside(PH)
IN_COLS, BANK_COLS = beside(PW)
FORCE_COLS = (0, *IN_COLS, W - 1)
AXES = ("sec", "gy", "gx")
SMEM = pl.BlockSpec(memory_space=pltpu.SMEM)
VMEM = pl.BlockSpec(memory_space=pltpu.VMEM)
ANY = pl.BlockSpec(memory_space=pl.ANY)
SMALL = pltpu.CompilerParams(vmem_limit_bytes=16 << 20)


def iota(shape, dim):
    return lax.broadcasted_iota(jnp.int32, shape, dim)


def split2(a):
    high = a.astype(BF16)
    return high, (a - high.astype(F32)).astype(BF16)


def dot_right(a, m):
    return sum(jnp.dot(part, m, preferred_element_type=F32) for part in split2(a))


def dot_nt(m, a):
    dims = (((1,), (1,)), ((), ()))
    return sum(lax.dot_general(m, part, dims, preferred_element_type=F32) for part in split2(a))


def dot_left(m, a):
    return sum(jnp.dot(m, part, preferred_element_type=F32) for part in split2(a))


def select_rows(picks, width):
    row, lane = iota((16, width), 0), iota((16, width), 1)
    wanted = jnp.full((16, width), -1, jnp.int32)
    for i, pick in enumerate(picks):
        wanted = jnp.where(row == i, pick, wanted)
    return jnp.where(lane == wanted, 1.0, 0.0).astype(BF16)


def weights(k, courant):
    half_x = 0.5 * courant[0]
    half_y = 0.5 * courant[1]
    return 1.0 - 4.0 * k, k - half_x, k + half_x, k - half_y, k + half_y


def per_field(diffusion, scale, shape, dim):
    index = iota(shape, dim) & (V - 1)
    out = jnp.full(shape, scale * diffusion[0], F32)
    for f in range(1, V):
        out = jnp.where(index == f, scale * diffusion[f], out)
    return out


def step_rows(old, r, coefs, force):
    a0, east, west, south, north = coefs
    centre = old[8 + r : 8 + r + CHUNK, :]
    return (
        a0 * centre
        + east * pltpu.roll(centre, W - 1, 1)
        + west * pltpu.roll(centre, 1, 1)
        + south * old[9 + r : 9 + r + CHUNK, :]
        + north * old[7 + r : 7 + r + CHUNK, :]
        + force
    )


def closed(k, courant):
    a0, east, west, south, north = weights(k, courant)
    lane = iota((1, W), 1)
    return a0, jnp.where(lane == W - 1, 0.0, east), jnp.where(lane == 0, 0.0, west), south, north


def near(*values):
    return [pltpu.with_memory_space_constraint(v, pltpu.VMEM) for v in values]


def position():
    return [lax.axis_index(axis) for axis in AXES]


def edge_kernel(x, drive, down, up, x_top, x_bottom, d_top, d_bottom, sems):
    copies = [
        pltpu.make_async_copy(x.at[:, 0:8, :], x_top, sems.at[0]),
        pltpu.make_async_copy(x.at[:, H - 8 : H, :], x_bottom, sems.at[1]),
        pltpu.make_async_copy(drive.at[:, 0:16, :], d_top, sems.at[2]),
        pltpu.make_async_copy(drive.at[:, H - 16 : H, :], d_bottom, sems.at[3]),
    ]
    for copy in copies:
        copy.start()
    for copy in copies:
        copy.wait()
    for f in range(V):
        down[0, f : f + 1] = x_bottom[f, 7:8, :]
        down[1, f : f + 1] = x_bottom[f, 6:7, :]
        down[2, f : f + 1] = d_bottom[f].astype(F32)[15:16]
        up[0, f : f + 1] = x_top[f, 0:1, :]
        up[1, f : f + 1] = x_top[f, 1:2, :]
        up[2, f : f + 1] = d_top[f].astype(F32)[0:1]


def edge(x, drive):
    shape = pltpu.VMEM((3, V, W), F32)
    return pl.pallas_call(
        edge_kernel,
        in_specs=[ANY, ANY],
        out_specs=[VMEM, VMEM],
        out_shape=[shape, shape],
        scratch_shapes=[
            pltpu.VMEM((V, 8, W), F32),
            pltpu.VMEM((V, 8, W), F32),
            pltpu.VMEM((V, 16, W), BF16),
            pltpu.VMEM((V, 16, W), BF16),
            pltpu.SemaphoreType.DMA((4,)),
        ],
        compiler_params=SMALL,
        name="edge",
    )(x, drive)


def first_kernel(
    courant, diffusion, x, drive, one, source, y, mean, rows, cols, two, force, thirds, sems
):
    parent = position()[0] == 0

    def load(f):
        return (
            pltpu.make_async_copy(x.at[f], one.at[f, 8 : 8 + H, :], sems.at[0, f]),
            pltpu.make_async_copy(drive.at[f], source.at[f], sems.at[1, f]),
        )

    for f in range(V):
        for copy in load(f):
            copy.start()
    for f in range(V):
        one[f, 0:8, :] = jnp.zeros((8, W), F32)
        one[f, H + 8 : H + 16, :] = jnp.zeros((8, W), F32)

    @pl.when(parent)
    def _():
        cols[...] = jnp.zeros(cols.shape, F32)
        picks, force_picks = select_rows(BANK_COLS, W), select_rows(FORCE_COLS, W)
        dims = (((1,), (1,)), ((), ()))
        for f in range(V):
            for copy in load(f):
                copy.wait()
            for i, r in enumerate(BANK_ROWS):
                rows[i, f : f + 1] = one[f, 8 + r : 9 + r, :]
            for i, r in enumerate(IN_ROWS):
                band = source[f, r // 16 * 16 : r // 16 * 16 + 16, :].astype(F32)
                rows[12 + i, f : f + 1] = band[r % 16 : r % 16 + 1]
            from_x = dot_nt(picks, one[f, 8 : 8 + H, :])
            from_drive = lax.dot_general(
                force_picks, source[f], dims, preferred_element_type=F32
            )
            for i in range(12):
                cols[i, f : f + 1, 0:H] = from_x[i : i + 1]
            for i in range(6):
                cols[12 + i, f : f + 1, 0:H] = from_drive[i : i + 1]

    @pl.when(jnp.logical_not(parent))
    def _():
        two[0:8, :] = jnp.zeros((8, W), F32)
        two[H + 8 : H + 16, :] = jnp.zeros((8, W), F32)
        blocks = mean_matrix()

        @pl.loop(0, V)
        def _(f):
            for copy in load(f):
                copy.wait()
            coefs = closed(diffusion[f] * 3.0, courant)
            mine = one.at[f]

            def step(old, new, at):
                for r in range(0, H, CHUNK):
                    new[at + r : at + r + CHUNK, :] = step_rows(
                        old, r, coefs, force[r : r + CHUNK, :]
                    )

            force[...] = source[f].astype(F32) * (1.0 / 3.0)
            step(mine, two, 8)
            step(two, mine, 8)
            step(mine, y.at[f], 0)
            thirds[...] = dot_right(y[f], blocks)
            total = (
                thirds[pl.ds(0, PH, stride=3), :]
                + thirds[pl.ds(1, PH, stride=3), :]
                + thirds[pl.ds(2, PH, stride=3), :]
            )
            mean[f] = total * (1.0 / 9.0)


def mean_matrix():
    gap = iota((W, PW), 0) - 3 * iota((W, PW), 1)
    return jnp.where((gap >= 0) & (gap <= 2), 1.0, 0.0).astype(BF16)


def first(courant, diffusion, x, drive):
    return pl.pallas_call(
        first_kernel,
        in_specs=[SMEM, SMEM, ANY, ANY],
        out_specs=[VMEM] * 6,
        out_shape=[
            pltpu.VMEM((V, H + 16, W), F32),
            pltpu.VMEM((V, H, W), BF16),
            pltpu.VMEM((V, H, W), F32),
            pltpu.VMEM((V, PH, PW), F32),
            pltpu.VMEM((16, V, W), F32),
            pltpu.VMEM((18, V, 256), F32),
        ],
        scratch_shapes=[
            pltpu.VMEM((H + 16, W), F32),
            pltpu.VMEM((H, W), F32),
            pltpu.VMEM((H, PW), F32),
            pltpu.SemaphoreType.DMA((2, V)),
        ],
        cost_estimate=pl.CostEstimate(flops=40_000_000, transcendentals=0, bytes_accessed=20_000_000),
        compiler_params=SMALL,
        name="first",
    )(courant, diffusion, x, drive)


def pack_kernel(cols, north, south, to_west, to_east):
    for out, picks, lo in ((to_west, (0, 1, 12), 0), (to_east, (11, 10, 17), W - 128)):
        for i, pick in enumerate(picks):
            out[i] = cols[pick]
        out[3, :, 0:128] = north[0, :, lo : lo + 128]
        out[3, :, 128:256] = north[1, :, lo : lo + 128]
        out[4, :, 0:128] = north[2, :, lo : lo + 128]
        out[4, :, 128:256] = south[2, :, lo : lo + 128]
        out[5, :, 0:128] = south[0, :, lo : lo + 128]
        out[5, :, 128:256] = south[1, :, lo : lo + 128]


def pack(cols, north, south):
    shape = pltpu.VMEM((6, V, 256), F32)
    return pl.pallas_call(
        pack_kernel,
        in_specs=[VMEM] * 3,
        out_specs=[VMEM] * 2,
        out_shape=[shape, shape],
        compiler_params=SMALL,
        name="pack",
    )(*near(cols, north, south))


def role_slot(nest_patch, row, column, member, count):
    nest = jnp.clip(row + member - 1, 0, count - 1)
    return nest_patch[nest, column]


def rims_kernel(
    courant, diffusion, nest_patch, rows, cols, north, south, west, east, *out_bank_side
):
    *out, bank, side = out_bank_side
    section, row, column = position()
    count, columns = nest_patch.shape

    @pl.when(section == 0)
    def _():
        k = per_field(diffusion, 1.0, (V, 1), 0)
        a0, ae, aw, as_, an = weights(k, courant)
        has_n = jnp.where(row > 0, 1.0, 0.0)
        has_s = jnp.where(row < count - 1, 1.0, 0.0)
        has_w = jnp.where(column > 0, 1.0, 0.0)
        has_e = jnp.where(column < columns - 1, 1.0, 0.0)
        lane128 = iota((V, 128), 1)
        lane256 = iota((V, 256), 1)
        wide = W + 256
        lane_wide = iota((V, wide), 1)
        keep = jnp.where(lane_wide < 128, has_w, jnp.where(lane_wide >= 128 + W, has_e, 1.0))
        near_w, near_e = west[0], east[0]

        def join(before, middle, after):
            return jnp.concatenate([before, middle, after], axis=1)

        def with_sides(middle, left, right):
            return join(
                jnp.where(lane128 == 127, left, 0.0), middle, jnp.where(lane128 == 0, right, 0.0)
            )

        def lanes(value, at):
            return value[:, at : at + 1]

        def halo_row(near, far, force, inner, a_far, a_inner, exists):
            value = (
                a0 * near
                + ae * pltpu.roll(near, wide - 1, 1)
                + aw * pltpu.roll(near, 1, 1)
                + a_far * far
                + a_inner * inner
                + force
            )
            return value * keep * exists

        north_1 = join(west[3, :, 0:128], north[0], east[3, :, 0:128])
        north_2 = join(west[3, :, 128:256], north[1], east[3, :, 128:256])
        north_f = join(west[4, :, 0:128], north[2], east[4, :, 0:128])
        south_1 = join(west[5, :, 0:128], south[0], east[5, :, 0:128])
        south_2 = join(west[5, :, 128:256], south[1], east[5, :, 128:256])
        south_f = join(west[4, :, 128:256], south[2], east[4, :, 128:256])
        top = with_sides(rows[0], lanes(near_w, 0), lanes(near_e, 0))
        bottom = with_sides(rows[11], lanes(near_w, H - 1), lanes(near_e, H - 1))
        new_north = halo_row(north_1, north_2, north_f, top, an, as_, has_n)
        new_south = halo_row(south_1, south_2, south_f, bottom, as_, an, has_s)

        def with_ends(column_values, before, after):
            return jnp.where(
                lane256 == 255, before, jnp.where(lane256 == H, after, column_values)
            )

        def halo_column(near, far, force, inner, a_far, a_inner, exists, at):
            full = with_ends(near, lanes(north_1, at), lanes(south_1, at))
            value = (
                a0 * full
                + as_ * pltpu.roll(full, 255, 1)
                + an * pltpu.roll(full, 1, 1)
                + a_far * far
                + a_inner * inner
                + force
            )
            new = with_ends(value * exists, lanes(new_north, at), lanes(new_south, at))
            return full, new

        at_w, at_e = 127, 128 + W
        old_west, new_west = halo_column(near_w, west[1], west[2], cols[0], aw, ae, has_w, at_w)
        old_east, new_east = halo_column(near_e, east[1], east[2], cols[11], ae, aw, has_e, at_e)

        bank[0, 0] = north_1
        bank[1, 0] = new_north
        bank[0, 5] = south_1
        bank[1, 5] = new_south
        blank = jnp.zeros((V, 128), F32)
        for i, r in enumerate(IN_ROWS):
            place, at = (1, 3, 2, 4)[i], BANK_ROWS.index(r)
            old = with_sides(rows[at], lanes(near_w, r), lanes(near_e, r))
            bank[0, place] = old
            new = (
                a0 * old
                + ae * pltpu.roll(old, wide - 1, 1)
                + aw * pltpu.roll(old, 1, 1)
                + join(blank, an * rows[at - 1] + as_ * rows[at + 1] + rows[12 + i], blank)
            )
            bank[1, place] = jnp.where(
                lane_wide == 127,
                lanes(new_west, r),
                jnp.where(lane_wide == 128 + W, lanes(new_east, r), new),
            )
        side[0, 0] = old_west
        side[1, 0] = new_west
        side[0, 5] = old_east
        side[1, 5] = new_east
        for i, c in enumerate(IN_COLS):
            place, at = (1, 3, 2, 4)[i], BANK_COLS.index(c)
            old, new = halo_column(
                cols[at], cols[at - 1], cols[12 + FORCE_COLS.index(c)], cols[at + 1], aw, ae, 1.0, 128 + c
            )
            side[0, place] = old
            side[1, place] = new

        for member in range(3):
            slot = lax.rem(role_slot(nest_patch, row, column, member, count), 9)
            patch_row, patch_col = lax.div(slot, 3), lax.rem(slot, 3)
            start = pl.multiple_of(patch_col * PW, PW)
            shift = OFF + 1 - PH * patch_row
            for time in range(2):
                for half in range(2):
                    rim = bank[time, patch_row + 3 * half, :, pl.ds(start, 384)]
                    rim = pltpu.roll(rim, 384 - 127, 1)[:, 0:256]
                    flank = pltpu.roll(side[time, patch_col + 3 * half], shift, 1)
                    flank = jnp.where((lane256 >= OFF) & (lane256 < OFF + PH + 2), flank, 0.0)
                    place = (2 * time + half) * V
                    out[member][place : place + V, :] = jnp.where(lane256 < PW + 2, rim, flank)


def rims(courant, diffusion, nest_patch, rows, cols, north, south, west, east):
    return pl.pallas_call(
        rims_kernel,
        in_specs=[SMEM] * 3 + [VMEM] * 6,
        out_specs=[VMEM] * 3,
        out_shape=[pltpu.VMEM((4 * V, 256), F32)] * 3,
        scratch_shapes=[pltpu.VMEM((2, 6, V, W + 256), F32), pltpu.VMEM((2, 6, V, 256), F32)],
        compiler_params=SMALL,
        name="rims",
    )(courant, diffusion, nest_patch, *near(rows, cols, north, south, west, east))


def edge_effect(old, new, courant, diffusion):
    n = old.shape[0]
    k_row = per_field(diffusion, 3.0, (n, 1), 0)
    a0_row, ae, aw, as_, an = weights(k_row, courant)
    upper = (iota((n, 1), 0) & V) == 0
    outer, inner = jnp.where(upper, an, as_), jnp.where(upper, as_, an)
    lane = iota((n, W), 1)
    east = jnp.where(lane == W - 1, 0.0, ae)
    west = jnp.where(lane == 0, 0.0, aw)
    tent = jnp.maximum(3 - jnp.abs(iota((256, W), 1) - 3 * iota((256, W), 0) + 2), 0)
    tent = tent.astype(F32).astype(BF16)

    def along_row(v):
        return a0_row * v + east * pltpu.roll(v, W - 1, 1) + west * pltpu.roll(v, 1, 1)

    row_effect = depths(
        dot_right(old, tent) * (1.0 / 3.0), dot_right(new, tent) * (1.0 / 3.0), outer, inner, along_row
    )

    k_col = per_field(diffusion, 3.0, (1, n), 1)
    a0_col, ae, aw, as_, an = weights(k_col, courant)
    left = (iota((1, n), 1) & V) == 0
    outer, inner = jnp.where(left, aw, ae), jnp.where(left, ae, aw)
    down = iota((H, n), 0)
    south = jnp.where(down == H - 1, 0.0, as_)
    north = jnp.where(down == 0, 0.0, an)
    tent = jnp.maximum(3 - jnp.abs(iota((H, 256), 0) - 3 * (iota((H, 256), 1) - OFF) + 2), 0)
    tent = tent.astype(F32).astype(BF16)

    def along_column(v):
        return a0_col * v + south * pltpu.roll(v, H - 1, 0) + north * pltpu.roll(v, 1, 0)

    col_effect = depths(
        dot_nt(tent, old) * (1.0 / 3.0), dot_nt(tent, new) * (1.0 / 3.0), outer, inner, along_column
    )
    return row_effect, col_effect


def depths(old, new, outer, inner, along):
    third = (new - old) * (1.0 / 3.0)
    first_0 = outer * old
    second_0 = along(first_0) + outer * (old + third)
    second_1 = outer * first_0
    third_0 = along(second_0) + inner * second_1 + outer * (old + 2.0 * third)
    third_1 = along(second_1) + outer * second_0
    third_2 = outer * second_1
    return third_0, third_1, third_2


def spread(values, depth, first=0):
    shape = (values.shape[1], 2 * V * 128)
    block, lane = iota(shape, 0) - first, iota(shape, 1)
    target = block * 128 + jnp.where(block < V, depth, 127 - depth)
    return dot_right(values, jnp.where(lane == target, 1.0, 0.0).astype(BF16))


def last_kernel(
    courant, diffusion, nest_patch, one, source, y, north, south, west, east,
    sent_0, sent_1, sent_2, got_0, got_1, got_2, mean_0, mean_1, mean_2, out, tile, sems,
):
    section, row, column = position()
    count = nest_patch.shape[0]
    parent = section == 0
    sent, got, means = (sent_0, sent_1, sent_2), (got_0, got_1, got_2), (mean_0, mean_1, mean_2)
    n = 2 * V

    def send(f):
        return pltpu.make_async_copy(tile.at[f], out.at[f], sems.at[f])

    @pl.when(parent)
    def _():
        _, ae, aw, _, _ = weights(per_field(diffusion, 1.0, (1, n), 1), courant)
        eye = jnp.where(iota((H, H), 0) == iota((H, H), 1), 1.0, 0.0).astype(BF16)
        beyond = jnp.concatenate([west[0, :, 0:H], east[0, :, 0:H]], axis=0)
        outer = jnp.where(iota((1, n), 1) < V, aw, ae)
        both = spread(dot_nt(eye, beyond) * outer, 0)
        for f in range(V):
            coefs = closed(diffusion[f], courant)
            left, right = f * 128, (V + f) * 128
            for r in range(0, H, CHUNK):
                end = r + CHUNK
                value = step_rows(one.at[f], r, coefs, source[f, r:end, :].astype(F32))
                tile[f, r:end, 0:128] = value[:, 0:128] + both[r:end, left : left + 128]
                tile[f, r:end, 128 : W - 128] = value[:, 128 : W - 128]
                tile[f, r:end, W - 128 : W] = (
                    value[:, W - 128 : W] + both[r:end, right : right + 128]
                )
            tile[f, 0:1, :] = tile[f, 0:1, :] + coefs[4] * north[0, f : f + 1, :]
            tile[f, H - 1 : H, :] = tile[f, H - 1 : H, :] + coefs[3] * south[0, f : f + 1, :]
        old = jnp.concatenate([s[0:n, :] for s in sent], axis=0)
        new = jnp.concatenate([s[n : 2 * n, :] for s in sent], axis=0)
        row_effect, col_effect = edge_effect(old, new, courant, diffusion)
        by_row = dot_right(sum(row_effect), mean_matrix()) * (1.0 / 9.0)
        thirds = iota((PH, H), 1) - 3 * iota((PH, H), 0)
        thirds = jnp.where((thirds >= 0) & (thirds <= 2), 1.0, 0.0).astype(BF16)
        by_col = dot_left(thirds, sum(col_effect)) * (1.0 / 9.0)
        line = iota((PH, PW), 0)
        for member in range(3):
            nest = row + member - 1
            entry = role_slot(nest_patch, row, column, member, count)
            slot = lax.rem(entry, 9)

            @pl.when((nest >= 0) & (nest < count) & (lax.div(entry, 9) == row))
            def _(member=member, slot=slot):
                at_row = pl.multiple_of(lax.div(slot, 3) * PH, PH)
                at_col = pl.multiple_of(lax.rem(slot, 3) * PW, PW)
                beside = spread(by_col, 0, member * n)
                for f in range(V):
                    left, right, up = f * 128, (V + f) * 128, member * n + f
                    tile[f, pl.ds(at_row, PH), pl.ds(at_col, PW)] = (
                        means[member][f]
                        + jnp.where(line == 0, by_row[up : up + 1], 0.0)
                        + jnp.where(line == PH - 1, by_row[up + V : up + V + 1], 0.0)
                        + beside[:, left : left + 128]
                        + beside[:, right : right + 128]
                    )

        for f in range(V):
            send(f).start()

    @pl.when(jnp.logical_not(parent))
    def _():
        member = row - lax.div(nest_patch[row, column], 9) + 1
        u = jnp.where(member == 0, got[0][...], jnp.where(member == 1, got[1][...], got[2][...]))
        row_effect, col_effect = edge_effect(u[0:n], u[n : 2 * n], courant, diffusion)
        both = sum(spread(col_effect[depth], depth) for depth in range(3))
        for f in range(V):
            left, right = f * 128, (V + f) * 128
            tile[f, :, 0:128] = y[f, :, 0:128] + both[:, left : left + 128]
            tile[f, :, 128 : W - 128] = y[f, :, 128 : W - 128]
            tile[f, :, W - 128 : W] = y[f, :, W - 128 : W] + both[:, right : right + 128]
            for depth in range(3):
                bottom = H - 1 - depth
                tile[f, depth : depth + 1, :] = (
                    tile[f, depth : depth + 1, :] + row_effect[depth][f : f + 1]
                )
                tile[f, bottom : bottom + 1, :] = (
                    tile[f, bottom : bottom + 1, :] + row_effect[depth][V + f : V + f + 1]
                )
            send(f).start()

    for f in range(V):
        send(f).wait()


def last(courant, diffusion, nest_patch, *arrays):
    return pl.pallas_call(
        last_kernel,
        in_specs=[SMEM] * 3 + [VMEM] * 16,
        out_specs=ANY,
        out_shape=jax.ShapeDtypeStruct((V, H, W), F32),
        scratch_shapes=[pltpu.VMEM((V, H, W), F32), pltpu.SemaphoreType.DMA((V,))],
        compiler_params=SMALL,
        name="last",
    )(courant, diffusion, nest_patch, *near(*arrays))


def routes(sizes, source, move):
    _, n_rows, n_cols = sizes
    out = []
    for r in range(n_rows):
        for c in range(n_cols):
            to_sec, to_r, to_c = move(r, c)
            if 0 <= to_r < n_rows and 0 <= to_c < n_cols:
                out.append(
                    (
                        (source * n_rows + r) * n_cols + c,
                        (to_sec * n_rows + to_r) * n_cols + to_c,
                    )
                )
    return out


def on_device(sizes, *arrays):
    return compute(sizes, *arrays)


def compute(sizes, fields, forcing, courant, diffusion, nest_patch):
    x = fields.reshape(V, H, W)
    drive = forcing.reshape(V, H, W)
    courant = courant.reshape(2)

    def shift(value, source, move):
        return lax.ppermute(value, AXES, routes(sizes, source, move))

    downward, upward = edge(x, drive)
    north = shift(downward, 0, lambda r, c: (0, r + 1, c))
    south = shift(upward, 0, lambda r, c: (0, r - 1, c))
    one, source, y, mean, rows, cols = first(courant, diffusion, x, drive)
    means = [shift(mean, 1, lambda r, c, m=m: (0, r + 1 - m, c)) for m in range(3)]
    to_west, to_east = pack(cols, north, south)
    west = shift(to_east, 0, lambda r, c: (0, r, c + 1))
    east = shift(to_west, 0, lambda r, c: (0, r, c - 1))
    sent = rims(courant, diffusion, nest_patch, rows, cols, north, south, west, east)
    got = [shift(sent[m], 0, lambda r, c, m=m: (1, r + m - 1, c)) for m in range(3)]
    out = last(
        courant, diffusion, nest_patch, one, source, y, north, south, west, east, *sent, *got, *means
    )
    return out.reshape(fields.shape)


def solution(mesh):
    sizes = tuple(mesh.shape[axis] for axis in AXES)
    spec = P("sec", None, None, "gy", "gx")
    return jax.shard_map(
        functools.partial(on_device, sizes),
        mesh=mesh,
        in_specs=(spec, spec, P(), P(), P()),
        out_specs=spec,
        check_vma=False,
    )
```

```python
import functools

import jax
import jax.numpy as jnp
from jax import lax
from jax.experimental import pallas as pl
from jax.experimental.pallas import tpu as pltpu
from jax.sharding import PartitionSpec as P


F32 = jnp.float32
BF16 = jnp.bfloat16
V, H, W = 4, 192, 384
PH, PW = H // 3, W // 3
CHUNK = 16
OFF = 160


def inner(n):
    lines = (n - 1, n, 2 * n - 1, 2 * n)
    return lines, (n - 2, n - 1, n, n + 1, 2 * n - 2, 2 * n - 1, 2 * n, 2 * n + 1)


IN_ROWS, BANK_ROWS = inner(PH)
IN_COLS, BANK_COLS = inner(PW)
WIDE = W + 256
COURANT, PATCH_ROW, PATCH_COL, MEMBER = V, V + 2, V + 5, V + 8
AXES = ("sec", "gy", "gx")
VMEM = pl.BlockSpec(memory_space=pltpu.VMEM)
ANY = pl.BlockSpec(memory_space=pl.ANY)
SMALL = pltpu.CompilerParams(vmem_limit_bytes=16 << 20)


def iota(shape, dim):
    return lax.broadcasted_iota(jnp.int32, shape, dim)


def split2(a):
    high = a.astype(BF16)
    return high, (a - high.astype(F32)).astype(BF16)


def dot_right(a, m):
    return sum(jnp.dot(part, m, preferred_element_type=F32) for part in split2(a))


def dot_nt(m, a):
    dims = (((1,), (1,)), ((), ()))
    return sum(lax.dot_general(m, part, dims, preferred_element_type=F32) for part in split2(a))


def dot_left(m, a):
    return sum(jnp.dot(m, part, preferred_element_type=F32) for part in split2(a))


def select_rows(picks, width):
    row, lane = iota((16, width), 0), iota((16, width), 1)
    wanted = jnp.full((16, width), -1, jnp.int32)
    for i, pick in enumerate(picks):
        wanted = jnp.where(row == i, pick, wanted)
    return jnp.where(lane == wanted, 1.0, 0.0).astype(BF16)


def weights(k, params):
    width = k.shape[1]
    half_x = 0.5 * params[COURANT : COURANT + 1, 0:width]
    half_y = 0.5 * params[COURANT + 1 : COURANT + 2, 0:width]
    return 1.0 - 4.0 * k, k - half_x, k + half_x, k - half_y, k + half_y


def per_field(params, shape, dim):
    index = iota(shape, dim) & (V - 1)
    out = jnp.broadcast_to(params[0:1, 0:1], shape)
    for f in range(1, V):
        out = jnp.where(index == f, params[f : f + 1, 0:1], out)
    return out


def weights_of(k, params):
    half_x = 0.5 * params[COURANT : COURANT + 1, 0:1]
    half_y = 0.5 * params[COURANT + 1 : COURANT + 2, 0:1]
    return 1.0 - 4.0 * k, k - half_x, k + half_x, k - half_y, k + half_y


def closed(k, params):
    a0, east, west, south, north = weights(k, params)
    lane = iota((1, W), 1)
    return a0, jnp.where(lane == W - 1, 0.0, east), jnp.where(lane == 0, 0.0, west), south, north


def step_rows(get, r, coefs, force):
    a0, east, west, south, north = coefs
    centre = get(r)
    return (
        a0 * centre
        + east * pltpu.roll(centre, W - 1, 1)
        + west * pltpu.roll(centre, 1, 1)
        + south * get(r + 1)
        + north * get(r - 1)
        + force
    )


def padded(ref):
    return lambda r: ref[8 + r : 8 + r + CHUNK, :]


def between(before, ref, after):
    def get(r):
        if r < 0:
            return jnp.concatenate([before, ref[0 : CHUNK - 1, :]], axis=0)
        if r + CHUNK > H:
            return jnp.concatenate([ref[r:H, :], after], axis=0)
        return ref[r : r + CHUNK, :]

    return get


def near(*values):
    return [pltpu.with_memory_space_constraint(v, pltpu.VMEM) for v in values]


def far(*values):
    return [pltpu.with_memory_space_constraint(v, pltpu.HBM) for v in values]


def position():
    return [lax.axis_index(axis) for axis in AXES]


def edge_kernel(
    x, drive, courant, diffusion, nest_patch, down, up, params,
    x_top, x_bottom, d_top, d_bottom, c_now, k_now, entries, sems,
):
    copies = [
        pltpu.make_async_copy(source, target, sems.at[i])
        for i, (source, target) in enumerate(
            (
                (x.at[:, 0:8, :], x_top),
                (x.at[:, H - 8 : H, :], x_bottom),
                (drive.at[:, 0:16, :], d_top),
                (drive.at[:, H - 16 : H, :], d_bottom),
                (courant, c_now),
                (diffusion, k_now),
                (nest_patch, entries),
            )
        )
    ]
    for copy in copies:
        copy.start()
    for copy in copies:
        copy.wait()
    for f in range(V):
        down[0, f : f + 1] = x_bottom[f, 7:8, :]
        down[1, f : f + 1] = x_bottom[f, 6:7, :]
        down[2, f : f + 1] = d_bottom[f].astype(F32)[15:16]
        up[0, f : f + 1] = x_top[f, 0:1, :]
        up[1, f : f + 1] = x_top[f, 1:2, :]
        up[2, f : f + 1] = d_top[f].astype(F32)[0:1]

    def put(at, value):
        params[at : at + 1, :] = jnp.full((1, WIDE), value, F32)

    for f in range(V):
        put(f, k_now[f])
    put(COURANT, c_now[0])
    put(COURANT + 1, c_now[1])
    _, row, column = position()
    count = nest_patch.shape[0]
    for member in range(3):
        slot = lax.rem(role_entry(entries, row, column, member, count), 9)
        put(PATCH_ROW + member, lax.div(slot, 3).astype(F32))
        put(PATCH_COL + member, lax.rem(slot, 3).astype(F32))
    put(MEMBER, (row - lax.div(entries[row, column], 9) + 1).astype(F32))


def edge(x, drive, courant, diffusion, nest_patch):
    return pl.pallas_call(
        edge_kernel,
        in_specs=[ANY] * 5,
        out_specs=[VMEM] * 3,
        out_shape=[
            pltpu.VMEM((3, V, W), F32),
            pltpu.VMEM((3, V, W), F32),
            pltpu.VMEM((16, WIDE), F32),
        ],
        scratch_shapes=[
            pltpu.VMEM((V, 8, W), F32),
            pltpu.VMEM((V, 8, W), F32),
            pltpu.VMEM((V, 16, W), BF16),
            pltpu.VMEM((V, 16, W), BF16),
            pltpu.SMEM((2,), F32),
            pltpu.SMEM((V,), F32),
            pltpu.SMEM(nest_patch.shape, jnp.int32),
            pltpu.SemaphoreType.DMA((7,)),
        ],
        compiler_params=SMALL,
        name="edge",
    )(*far(x, drive, courant, diffusion, nest_patch))


def role_entry(entries, row, column, member, count):
    nest = jnp.clip(row + member - 1, 0, count - 1)
    return entries[nest, column]


NT = (((1,), (1,)), ((), ()))


def nests_kernel(
    params, x, drive, y, mean, ends, tent_row, tent_col, two, three, force, thirds
):
    parent = position()[0] == 0

    @pl.when(parent)
    def _():
        ends[...] = jnp.zeros(ends.shape, F32)
        none = -1
        x_west, x_east = select_rows((0, 1), 128), select_rows((none, none, none, 127, 126), 128)
        d_west = select_rows((none, none, 0), 128)
        d_east = select_rows((none, none, none, none, none, 127), 128)
        for f in range(V):
            values = dot_nt(x_west, x[f, :, 0:128]) + dot_nt(x_east, x[f, :, W - 128 : W])
            values = values + lax.dot_general(
                d_west, drive[f, :, 0:128], NT, preferred_element_type=F32
            )
            values = values + lax.dot_general(
                d_east, drive[f, :, W - 128 : W], NT, preferred_element_type=F32
            )
            for i in range(6):
                ends[i, f : f + 1, 0:H] = values[i : i + 1]

    @pl.when(jnp.logical_not(parent))
    def _():
        for buffer in (two, three):
            buffer[0:8, :] = jnp.zeros((8, W), F32)
            buffer[H + 8 : H + 16, :] = jnp.zeros((8, W), F32)
        blocks = mean_matrix()
        zero = jnp.zeros((1, W), F32)
        tent_row[...] = row_tent()
        tent_col[...] = col_tent()

        @pl.loop(0, V)
        def _(f):
            coefs = closed(3.0 * params[pl.ds(f, 1), :][:, 0:W], params)

            def step(get, new, at):
                for r in range(0, H, CHUNK):
                    new[at + r : at + r + CHUNK, :] = step_rows(
                        get, r, coefs, force[r : r + CHUNK, :]
                    )

            force[...] = drive[f].astype(F32) * (1.0 / 3.0)
            step(between(zero, x.at[f], zero), two, 8)
            step(padded(two), three, 8)
            step(padded(three), y.at[f], 0)
            thirds[...] = dot_right(y[f], blocks)
            total = (
                thirds[pl.ds(0, PH, stride=3), :]
                + thirds[pl.ds(1, PH, stride=3), :]
                + thirds[pl.ds(2, PH, stride=3), :]
            )
            mean[f] = total * (1.0 / 9.0)


def mean_matrix():
    gap = iota((W, PW), 0) - 3 * iota((W, PW), 1)
    return jnp.where((gap >= 0) & (gap <= 2), 1.0, 0.0).astype(BF16)


def row_tent():
    tent = jnp.maximum(3 - jnp.abs(iota((256, W), 1) - 3 * iota((256, W), 0) + 2), 0)
    return tent.astype(F32).astype(BF16)


def col_tent():
    tent = jnp.maximum(3 - jnp.abs(iota((H, 256), 0) - 3 * (iota((H, 256), 1) - OFF) + 2), 0)
    return tent.astype(F32).astype(BF16)


def nests(params, x, drive):
    return pl.pallas_call(
        nests_kernel,
        in_specs=[VMEM] * 3,
        out_specs=[VMEM] * 5,
        out_shape=[
            pltpu.VMEM((V, H, W), F32),
            pltpu.VMEM((V, PH, PW), F32),
            pltpu.VMEM((6, V, 256), F32),
            pltpu.VMEM((256, W), BF16),
            pltpu.VMEM((H, 256), BF16),
        ],
        scratch_shapes=[
            pltpu.VMEM((H + 16, W), F32),
            pltpu.VMEM((H + 16, W), F32),
            pltpu.VMEM((H, W), F32),
            pltpu.VMEM((H, PW), F32),
        ],
        compiler_params=SMALL,
        name="nests",
    )(*near(params, x, drive))


def bank_kernel(x, drive, rows, cols):
    @pl.when(position()[0] == 0)
    def _():
        cols[...] = jnp.zeros(cols.shape, F32)
        picks, force_picks = select_rows(BANK_COLS, W), select_rows(IN_COLS, W)
        for f in range(V):
            for i, r in enumerate((0, *BANK_ROWS, H - 1)):
                rows[i, f : f + 1] = x[f, r : r + 1, :]
            for i, r in enumerate(IN_ROWS):
                band = drive[f, r // 16 * 16 : r // 16 * 16 + 16, :].astype(F32)
                rows[10 + i, f : f + 1] = band[r % 16 : r % 16 + 1]
            from_x = dot_nt(picks, x[f])
            from_drive = lax.dot_general(force_picks, drive[f], NT, preferred_element_type=F32)
            for i in range(8):
                cols[i, f : f + 1, 0:H] = from_x[i : i + 1]
            for i in range(4):
                cols[8 + i, f : f + 1, 0:H] = from_drive[i : i + 1]


def banks(x, drive):
    return pl.pallas_call(
        bank_kernel,
        in_specs=[VMEM] * 2,
        out_specs=[VMEM] * 2,
        out_shape=[pltpu.VMEM((14, V, W), F32), pltpu.VMEM((12, V, 256), F32)],
        compiler_params=SMALL,
        name="banks",
    )(*near(x, drive))


def pack_kernel(ends, north, south, to_west, to_east):
    for out, at, lo in ((to_west, 0, 0), (to_east, 3, W - 128)):
        out[0:3] = ends[at : at + 3]
        out[3, :, 0:128] = north[0, :, lo : lo + 128]
        out[3, :, 128:256] = north[1, :, lo : lo + 128]
        out[4, :, 0:128] = north[2, :, lo : lo + 128]
        out[4, :, 128:256] = south[2, :, lo : lo + 128]
        out[5, :, 0:128] = south[0, :, lo : lo + 128]
        out[5, :, 128:256] = south[1, :, lo : lo + 128]


def pack(ends, north, south):
    shape = pltpu.VMEM((6, V, 256), F32)
    return pl.pallas_call(
        pack_kernel,
        in_specs=[VMEM] * 3,
        out_specs=[VMEM] * 2,
        out_shape=[shape, shape],
        compiler_params=SMALL,
        name="pack",
    )(*near(ends, north, south))


def rims_kernel(
    params, shape, rows, cols, ends, north, south, west, east, *out
):
    section, row, column = position()
    count, columns = shape

    @pl.when(section == 0)
    def _():
        k = per_field(params, (V, 1), 0)
        a0, ae, aw, as_, an = weights_of(k, params)
        has_n = jnp.where(row > 0, 1.0, 0.0)
        has_s = jnp.where(row < count - 1, 1.0, 0.0)
        has_w = jnp.where(column > 0, 1.0, 0.0)
        has_e = jnp.where(column < columns - 1, 1.0, 0.0)
        lane128 = iota((V, 128), 1)
        lane256 = iota((V, 256), 1)
        wide = WIDE
        lane_wide = iota((V, wide), 1)
        keep = jnp.where(lane_wide < 128, has_w, jnp.where(lane_wide >= 128 + W, has_e, 1.0))
        near_w, near_e = west[0], east[0]

        def join(before, middle, after):
            return jnp.concatenate([before, middle, after], axis=1)

        def with_sides(middle, left, right):
            return join(
                jnp.where(lane128 == 127, left, 0.0), middle, jnp.where(lane128 == 0, right, 0.0)
            )

        def lanes(value, at):
            return value[:, at : at + 1]

        def halo_row(near, far, force, inner, a_far, a_inner, exists):
            value = (
                a0 * near
                + ae * pltpu.roll(near, wide - 1, 1)
                + aw * pltpu.roll(near, 1, 1)
                + a_far * far
                + a_inner * inner
                + force
            )
            return value * keep * exists

        north_1 = join(west[3, :, 0:128], north[0], east[3, :, 0:128])
        north_2 = join(west[3, :, 128:256], north[1], east[3, :, 128:256])
        north_f = join(west[4, :, 0:128], north[2], east[4, :, 0:128])
        south_1 = join(west[5, :, 0:128], south[0], east[5, :, 0:128])
        south_2 = join(west[5, :, 128:256], south[1], east[5, :, 128:256])
        south_f = join(west[4, :, 128:256], south[2], east[4, :, 128:256])
        top = with_sides(rows[0], lanes(near_w, 0), lanes(near_e, 0))
        bottom = with_sides(rows[9], lanes(near_w, H - 1), lanes(near_e, H - 1))
        new_north = halo_row(north_1, north_2, north_f, top, an, as_, has_n)
        new_south = halo_row(south_1, south_2, south_f, bottom, as_, an, has_s)

        def with_ends(column_values, before, after):
            return jnp.where(
                lane256 == 255, before, jnp.where(lane256 == H, after, column_values)
            )

        def halo_column(near, far, force, inner, a_far, a_inner, exists, at):
            full = with_ends(near, lanes(north_1, at), lanes(south_1, at))
            value = (
                a0 * full
                + as_ * pltpu.roll(full, 255, 1)
                + an * pltpu.roll(full, 1, 1)
                + a_far * far
                + a_inner * inner
                + force
            )
            new = with_ends(value * exists, lanes(new_north, at), lanes(new_south, at))
            return full, new

        at_w, at_e = 127, 128 + W
        old_west, new_west = halo_column(near_w, west[1], west[2], ends[0], aw, ae, has_w, at_w)
        old_east, new_east = halo_column(near_e, east[1], east[2], ends[3], ae, aw, has_e, at_e)

        bank = {(0, 0): north_1, (1, 0): new_north, (0, 5): south_1, (1, 5): new_south}
        side = {(0, 0): old_west, (1, 0): new_west, (0, 5): old_east, (1, 5): new_east}
        blank = jnp.zeros((V, 128), F32)
        for i, r in enumerate(IN_ROWS):
            place, at = (1, 3, 2, 4)[i], 1 + BANK_ROWS.index(r)
            old = with_sides(rows[at], lanes(near_w, r), lanes(near_e, r))
            bank[0, place] = old
            new = (
                a0 * old
                + ae * pltpu.roll(old, wide - 1, 1)
                + aw * pltpu.roll(old, 1, 1)
                + join(blank, an * rows[at - 1] + as_ * rows[at + 1] + rows[10 + i], blank)
            )
            bank[1, place] = jnp.where(
                lane_wide == 127,
                lanes(new_west, r),
                jnp.where(lane_wide == 128 + W, lanes(new_east, r), new),
            )
        for i, c in enumerate(IN_COLS):
            place, at = (1, 3, 2, 4)[i], BANK_COLS.index(c)
            old, new = halo_column(
                cols[at], cols[at - 1], cols[8 + i], cols[at + 1], aw, ae, 1.0, 128 + c
            )
            side[0, place] = old
            side[1, place] = new

        def choose(which, candidates):
            return jnp.where(
                which == 0.0, candidates[0], jnp.where(which == 1.0, candidates[1], candidates[2])
            )

        for member in range(3):
            at = PATCH_ROW + member
            patch_row = params[at : at + 1, :]
            at = PATCH_COL + member
            patch_col = params[at : at + 1, :]
            for time in range(2):
                for half in range(2):
                    line = choose(patch_row, [bank[time, 3 * half + i] for i in range(3)])
                    rim = choose(
                        patch_col[:, 0:W], [line[:, i * PW : i * PW + W] for i in range(3)]
                    )
                    rim = pltpu.roll(rim, W - 127, 1)[:, 0:256]
                    flank = choose(
                        patch_col[:, 0:256], [side[time, 3 * half + i] for i in range(3)]
                    )
                    flank = choose(
                        patch_row[:, 0:256],
                        [pltpu.roll(flank, OFF + 1 - PH * i, 1) for i in range(3)],
                    )
                    flank = jnp.where((lane256 >= OFF) & (lane256 < OFF + PH + 2), flank, 0.0)
                    place = (2 * time + half) * V
                    out[member][place : place + V, :] = jnp.where(lane256 < PW + 2, rim, flank)


def rims(shape, *arrays):
    def kernel(params, *refs):
        rims_kernel(params, shape, *refs)

    return pl.pallas_call(
        kernel,
        in_specs=[VMEM] * 8,
        out_specs=[VMEM] * 3,
        out_shape=[pltpu.VMEM((4 * V, 256), F32)] * 3,
        compiler_params=SMALL,
        name="rims",
    )(*near(*arrays))


def edge_effect(old, new, params, tent_row, tent_col):
    n = old.shape[0]
    k_row = 3.0 * per_field(params, (n, 1), 0)
    a0_row, ae, aw, as_, an = weights_of(k_row, params)
    upper = (iota((n, 1), 0) & V) == 0
    outer, inner = jnp.where(upper, an, as_), jnp.where(upper, as_, an)
    lane = iota((n, W), 1)
    east = jnp.where(lane == W - 1, 0.0, ae)
    west = jnp.where(lane == 0, 0.0, aw)

    def along_row(v):
        return a0_row * v + east * pltpu.roll(v, W - 1, 1) + west * pltpu.roll(v, 1, 1)

    row_effect = depths(
        dot_right(old, tent_row) * (1.0 / 3.0), dot_right(new, tent_row) * (1.0 / 3.0), outer, inner, along_row
    )

    k_col = 3.0 * per_field(params, (1, n), 1)
    a0_col, ae, aw, as_, an = weights_of(k_col, params)
    left = (iota((1, n), 1) & V) == 0
    outer, inner = jnp.where(left, aw, ae), jnp.where(left, ae, aw)
    down = iota((H, n), 0)
    south = jnp.where(down == H - 1, 0.0, as_)
    north = jnp.where(down == 0, 0.0, an)

    def along_column(v):
        return a0_col * v + south * pltpu.roll(v, H - 1, 0) + north * pltpu.roll(v, 1, 0)

    col_effect = depths(
        dot_nt(tent_col, old) * (1.0 / 3.0), dot_nt(tent_col, new) * (1.0 / 3.0), outer, inner, along_column
    )
    return row_effect, col_effect


def depths(old, new, outer, inner, along):
    third = (new - old) * (1.0 / 3.0)
    first_0 = outer * old
    second_0 = along(first_0) + outer * (old + third)
    second_1 = outer * first_0
    third_0 = along(second_0) + inner * second_1 + outer * (old + 2.0 * third)
    third_1 = along(second_1) + outer * second_0
    third_2 = outer * second_1
    return third_0, third_1, third_2


def spread(values, depth, first=0):
    shape = (values.shape[1], 2 * V * 128)
    block, lane = iota(shape, 0) - first, iota(shape, 1)
    target = block * 128 + jnp.where(block < V, depth, 127 - depth)
    return dot_right(values, jnp.where(lane == target, 1.0, 0.0).astype(BF16))


def last_kernel(
    nest_patch, params, x, drive, y, tent_row, tent_col, north, south, west, east,
    sent_0, sent_1, sent_2, got_0, got_1, got_2, mean_0, mean_1, mean_2, out, tile, entries, sems,
):
    section, row, column = position()
    count = nest_patch.shape[0]
    parent = section == 0
    sent, got, means = (sent_0, sent_1, sent_2), (got_0, got_1, got_2), (mean_0, mean_1, mean_2)
    n = 2 * V

    def send(f):
        return pltpu.make_async_copy(tile.at[f], out.at[f], sems.at[f])

    @pl.when(parent)
    def _():
        fetch = pltpu.make_async_copy(nest_patch, entries, sems.at[V])
        fetch.start()
        _, ae, aw, _, _ = weights_of(per_field(params, (1, n), 1), params)
        eye = jnp.where(iota((H, H), 0) == iota((H, H), 1), 1.0, 0.0).astype(BF16)
        beyond = jnp.concatenate([west[0, :, 0:H], east[0, :, 0:H]], axis=0)
        outer = jnp.where(iota((1, n), 1) < V, aw, ae)
        both = spread(dot_nt(eye, beyond) * outer, 0)
        for f in range(V):
            coefs = closed(params[f : f + 1, 0:W], params)
            get = between(north[0, f : f + 1, :], x.at[f], south[0, f : f + 1, :])
            left, right = f * 128, (V + f) * 128
            for r in range(0, H, CHUNK):
                end = r + CHUNK
                value = step_rows(get, r, coefs, drive[f, r:end, :].astype(F32))
                tile[f, r:end, 0:128] = value[:, 0:128] + both[r:end, left : left + 128]
                tile[f, r:end, 128 : W - 128] = value[:, 128 : W - 128]
                tile[f, r:end, W - 128 : W] = (
                    value[:, W - 128 : W] + both[r:end, right : right + 128]
                )
        old = jnp.concatenate([s[0:n, :] for s in sent], axis=0)
        new = jnp.concatenate([s[n : 2 * n, :] for s in sent], axis=0)
        row_effect, col_effect = edge_effect(old, new, params, row_tent(), col_tent())
        by_row = dot_right(sum(row_effect), mean_matrix()) * (1.0 / 9.0)
        thirds = iota((PH, H), 1) - 3 * iota((PH, H), 0)
        thirds = jnp.where((thirds >= 0) & (thirds <= 2), 1.0, 0.0).astype(BF16)
        by_col = dot_left(thirds, sum(col_effect)) * (1.0 / 9.0)
        line = iota((PH, PW), 0)
        fetch.wait()
        for member in range(3):
            nest = row + member - 1
            entry = role_entry(entries, row, column, member, count)
            slot = lax.rem(entry, 9)

            @pl.when((nest >= 0) & (nest < count) & (lax.div(entry, 9) == row))
            def _(member=member, slot=slot):
                at_row = pl.multiple_of(lax.div(slot, 3) * PH, PH)
                at_col = pl.multiple_of(lax.rem(slot, 3) * PW, PW)
                beside = spread(by_col, 0, member * n)
                for f in range(V):
                    left, right, up = f * 128, (V + f) * 128, member * n + f
                    tile[f, pl.ds(at_row, PH), pl.ds(at_col, PW)] = (
                        means[member][f]
                        + jnp.where(line == 0, by_row[up : up + 1], 0.0)
                        + jnp.where(line == PH - 1, by_row[up + V : up + V + 1], 0.0)
                        + beside[:, left : left + 128]
                        + beside[:, right : right + 128]
                    )

        for f in range(V):
            send(f).start()

    @pl.when(jnp.logical_not(parent))
    def _():
        member = params[MEMBER : MEMBER + 1, 0:256]
        u = jnp.where(
            member == 0.0, got[0][...], jnp.where(member == 1.0, got[1][...], got[2][...])
        )
        row_effect, col_effect = edge_effect(
            u[0:n], u[n : 2 * n], params, tent_row[...], tent_col[...]
        )
        both = sum(spread(col_effect[depth], depth) for depth in range(3))
        for f in range(V):
            left, right = f * 128, (V + f) * 128
            tile[f, :, 0:128] = y[f, :, 0:128] + both[:, left : left + 128]
            tile[f, :, 128 : W - 128] = y[f, :, 128 : W - 128]
            tile[f, :, W - 128 : W] = y[f, :, W - 128 : W] + both[:, right : right + 128]
            for depth in range(3):
                bottom = H - 1 - depth
                tile[f, depth : depth + 1, :] = (
                    tile[f, depth : depth + 1, :] + row_effect[depth][f : f + 1]
                )
                tile[f, bottom : bottom + 1, :] = (
                    tile[f, bottom : bottom + 1, :] + row_effect[depth][V + f : V + f + 1]
                )
            send(f).start()

    for f in range(V):
        send(f).wait()


def last(nest_patch, *arrays):
    return pl.pallas_call(
        last_kernel,
        in_specs=[ANY] + [VMEM] * 19,
        out_specs=ANY,
        out_shape=jax.ShapeDtypeStruct((V, H, W), F32),
        scratch_shapes=[
            pltpu.VMEM((V, H, W), F32),
            pltpu.SMEM(nest_patch.shape, jnp.int32),
            pltpu.SemaphoreType.DMA((V + 1,)),
        ],
        compiler_params=SMALL,
        name="last",
    )(*far(nest_patch), *near(*arrays))


def routes(sizes, source, move):
    _, n_rows, n_cols = sizes
    out = []
    for r in range(n_rows):
        for c in range(n_cols):
            to_sec, to_r, to_c = move(r, c)
            if 0 <= to_r < n_rows and 0 <= to_c < n_cols:
                out.append(
                    (
                        (source * n_rows + r) * n_cols + c,
                        (to_sec * n_rows + to_r) * n_cols + to_c,
                    )
                )
    return out


def on_device(sizes, *arrays):
    return compute(sizes, *arrays)


def compute(sizes, fields, forcing, courant, diffusion, nest_patch):
    x = fields.reshape(V, H, W)
    drive = forcing.reshape(V, H, W)
    courant = courant.reshape(2)

    def shift(value, source, move):
        return lax.ppermute(value, AXES, routes(sizes, source, move))

    downward, upward, params = edge(x, drive, courant, diffusion, nest_patch)
    north = shift(downward, 0, lambda r, c: (0, r + 1, c))
    south = shift(upward, 0, lambda r, c: (0, r - 1, c))
    y, mean, ends, *tents = nests(params, x, drive)
    means = [shift(mean, 1, lambda r, c, m=m: (0, r + 1 - m, c)) for m in range(3)]
    to_west, to_east = pack(ends, north, south)
    west = shift(to_east, 0, lambda r, c: (0, r, c + 1))
    east = shift(to_west, 0, lambda r, c: (0, r, c - 1))
    rows, cols = banks(x, drive)
    halos = north, south, west, east
    sent = rims(sizes[1:], params, rows, cols, ends, *halos)
    got = [shift(sent[m], 0, lambda r, c, m=m: (1, r + m - 1, c)) for m in range(3)]
    out = last(nest_patch, params, x, drive, y, *tents, *halos, *sent, *got, *means)
    return out.reshape(fields.shape)


def solution(mesh):
    sizes = tuple(mesh.shape[axis] for axis in AXES)
    spec = P("sec", None, None, "gy", "gx")
    return jax.shard_map(
        functools.partial(on_device, sizes),
        mesh=mesh,
        in_specs=(spec, spec, P(), P(), P()),
        out_specs=spec,
        check_vma=False,
    )
```

```python
import functools

import jax
import jax.numpy as jnp
from jax import lax
from jax.experimental import pallas as pl
from jax.experimental.pallas import tpu as pltpu
from jax.sharding import PartitionSpec as P


F32 = jnp.float32
BF16 = jnp.bfloat16
V, H, W = 4, 192, 384
PH, PW = H // 3, W // 3
CHUNK = 16
OFF = 160


def inner(n):
    lines = (n - 1, n, 2 * n - 1, 2 * n)
    return lines, (n - 2, n - 1, n, n + 1, 2 * n - 2, 2 * n - 1, 2 * n, 2 * n + 1)


IN_ROWS, BANK_ROWS = inner(PH)
IN_COLS, BANK_COLS = inner(PW)
WIDE = W + 256
COURANT, PATCH_ROW, PATCH_COL, MEMBER = V, V + 2, V + 5, V + 8
AXES = ("sec", "gy", "gx")
VMEM = pl.BlockSpec(memory_space=pltpu.VMEM)
ANY = pl.BlockSpec(memory_space=pl.ANY)
SMALL = pltpu.CompilerParams(vmem_limit_bytes=16 << 20)


def iota(shape, dim):
    return lax.broadcasted_iota(jnp.int32, shape, dim)


def split2(a):
    high = a.astype(BF16)
    return high, (a - high.astype(F32)).astype(BF16)


def dot_right(a, m):
    return sum(jnp.dot(part, m, preferred_element_type=F32) for part in split2(a))


def dot_nt(m, a):
    dims = (((1,), (1,)), ((), ()))
    return sum(lax.dot_general(m, part, dims, preferred_element_type=F32) for part in split2(a))


def dot_left(m, a):
    return sum(jnp.dot(m, part, preferred_element_type=F32) for part in split2(a))


def select_rows(picks, width):
    row, lane = iota((16, width), 0), iota((16, width), 1)
    wanted = jnp.full((16, width), -1, jnp.int32)
    for i, pick in enumerate(picks):
        wanted = jnp.where(row == i, pick, wanted)
    return jnp.where(lane == wanted, 1.0, 0.0).astype(BF16)


def weights(k, params):
    width = k.shape[1]
    half_x = 0.5 * params[COURANT : COURANT + 1, 0:width]
    half_y = 0.5 * params[COURANT + 1 : COURANT + 2, 0:width]
    return 1.0 - 4.0 * k, k - half_x, k + half_x, k - half_y, k + half_y


def per_field(params, shape, dim):
    index = iota(shape, dim) & (V - 1)
    out = jnp.broadcast_to(params[0:1, 0:1], shape)
    for f in range(1, V):
        out = jnp.where(index == f, params[f : f + 1, 0:1], out)
    return out


def weights_of(k, params):
    half_x = 0.5 * params[COURANT : COURANT + 1, 0:1]
    half_y = 0.5 * params[COURANT + 1 : COURANT + 2, 0:1]
    return 1.0 - 4.0 * k, k - half_x, k + half_x, k - half_y, k + half_y


def closed(k, params):
    a0, east, west, south, north = weights(k, params)
    lane = iota((1, W), 1)
    return a0, jnp.where(lane == W - 1, 0.0, east), jnp.where(lane == 0, 0.0, west), south, north


def step_rows(get, r, coefs, force):
    a0, east, west, south, north = coefs
    centre = get(r)
    return (
        a0 * centre
        + east * pltpu.roll(centre, W - 1, 1)
        + west * pltpu.roll(centre, 1, 1)
        + south * get(r + 1)
        + north * get(r - 1)
        + force
    )


def padded(ref):
    return lambda r: ref[8 + r : 8 + r + CHUNK, :]


def between(before, ref, after):
    def get(r):
        if r < 0:
            return jnp.concatenate([before, ref[0 : CHUNK - 1, :]], axis=0)
        if r + CHUNK > H:
            return jnp.concatenate([ref[r:H, :], after], axis=0)
        return ref[r : r + CHUNK, :]

    return get


def near(*values):
    return [pltpu.with_memory_space_constraint(v, pltpu.VMEM) for v in values]


def far(*values):
    return [pltpu.with_memory_space_constraint(v, pltpu.HBM) for v in values]


def position():
    return [lax.axis_index(axis) for axis in AXES]


def edge_kernel(
    x, drive, courant, diffusion, nest_patch, down, up, params,
    x_top, x_bottom, d_top, d_bottom, c_now, k_now, entries, sems,
):
    copies = [
        pltpu.make_async_copy(source, target, sems.at[i])
        for i, (source, target) in enumerate(
            (
                (x.at[:, 0:8, :], x_top),
                (x.at[:, H - 8 : H, :], x_bottom),
                (drive.at[:, 0:16, :], d_top),
                (drive.at[:, H - 16 : H, :], d_bottom),
                (courant, c_now),
                (diffusion, k_now),
                (nest_patch, entries),
            )
        )
    ]
    for copy in copies:
        copy.start()
    for copy in copies:
        copy.wait()
    for f in range(V):
        down[0, f : f + 1] = x_bottom[f, 7:8, :]
        down[1, f : f + 1] = x_bottom[f, 6:7, :]
        down[2, f : f + 1] = d_bottom[f].astype(F32)[15:16]
        up[0, f : f + 1] = x_top[f, 0:1, :]
        up[1, f : f + 1] = x_top[f, 1:2, :]
        up[2, f : f + 1] = d_top[f].astype(F32)[0:1]

    def put(at, value):
        params[at : at + 1, :] = jnp.full((1, WIDE), value, F32)

    for f in range(V):
        put(f, k_now[f])
    put(COURANT, c_now[0])
    put(COURANT + 1, c_now[1])
    _, row, column = position()
    count = nest_patch.shape[0]
    for member in range(3):
        slot = lax.rem(role_entry(entries, row, column, member, count), 9)
        put(PATCH_ROW + member, lax.div(slot, 3).astype(F32))
        put(PATCH_COL + member, lax.rem(slot, 3).astype(F32))
    put(MEMBER, (row - lax.div(entries[row, column], 9) + 1).astype(F32))


def edge(x, drive, courant, diffusion, nest_patch):
    return pl.pallas_call(
        edge_kernel,
        in_specs=[ANY] * 5,
        out_specs=[VMEM] * 3,
        out_shape=[
            pltpu.VMEM((3, V, W), F32),
            pltpu.VMEM((3, V, W), F32),
            pltpu.VMEM((16, WIDE), F32),
        ],
        scratch_shapes=[
            pltpu.VMEM((V, 8, W), F32),
            pltpu.VMEM((V, 8, W), F32),
            pltpu.VMEM((V, 16, W), BF16),
            pltpu.VMEM((V, 16, W), BF16),
            pltpu.SMEM((2,), F32),
            pltpu.SMEM((V,), F32),
            pltpu.SMEM(nest_patch.shape, jnp.int32),
            pltpu.SemaphoreType.DMA((7,)),
        ],
        compiler_params=SMALL,
        name="edge",
    )(*far(x, drive, courant, diffusion, nest_patch))


def role_entry(entries, row, column, member, count):
    nest = jnp.clip(row + member - 1, 0, count - 1)
    return entries[nest, column]


NT = (((1,), (1,)), ((), ()))


def nests_kernel(
    params, x, drive, y, mean, ends, tent_row, tent_col, two, three, force, thirds
):
    parent = position()[0] == 0

    @pl.when(parent)
    def _():
        ends[...] = jnp.zeros(ends.shape, F32)
        none = -1
        x_west, x_east = select_rows((0, 1), 128), select_rows((none, none, none, 127, 126), 128)
        d_west = select_rows((none, none, 0), 128)
        d_east = select_rows((none, none, none, none, none, 127), 128)
        for f in range(V):
            values = dot_nt(x_west, x[f, :, 0:128]) + dot_nt(x_east, x[f, :, W - 128 : W])
            values = values + lax.dot_general(
                d_west, drive[f, :, 0:128], NT, preferred_element_type=F32
            )
            values = values + lax.dot_general(
                d_east, drive[f, :, W - 128 : W], NT, preferred_element_type=F32
            )
            for i in range(6):
                ends[i, f : f + 1, 0:H] = values[i : i + 1]

    @pl.when(jnp.logical_not(parent))
    def _():
        for buffer in (two, three):
            buffer[0:8, :] = jnp.zeros((8, W), F32)
            buffer[H + 8 : H + 16, :] = jnp.zeros((8, W), F32)
        blocks = mean_matrix()
        zero = jnp.zeros((1, W), F32)
        tent_row[...] = row_tent()
        tent_col[...] = col_tent()

        @pl.loop(0, V)
        def _(f):
            coefs = closed(3.0 * params[pl.ds(f, 1), :][:, 0:W], params)

            def step(get, new, at):
                for r in range(0, H, CHUNK):
                    new[at + r : at + r + CHUNK, :] = step_rows(
                        get, r, coefs, force[r : r + CHUNK, :]
                    )

            force[...] = drive[f].astype(F32) * (1.0 / 3.0)
            step(between(zero, x.at[f], zero), two, 8)
            step(padded(two), three, 8)
            step(padded(three), y.at[f], 0)
            thirds[...] = dot_right(y[f], blocks)
            total = (
                thirds[pl.ds(0, PH, stride=3), :]
                + thirds[pl.ds(1, PH, stride=3), :]
                + thirds[pl.ds(2, PH, stride=3), :]
            )
            mean[f] = total * (1.0 / 9.0)


def mean_matrix():
    gap = iota((W, PW), 0) - 3 * iota((W, PW), 1)
    return jnp.where((gap >= 0) & (gap <= 2), 1.0, 0.0).astype(BF16)


def row_tent():
    tent = jnp.maximum(3 - jnp.abs(iota((256, W), 1) - 3 * iota((256, W), 0) + 2), 0)
    return tent.astype(F32).astype(BF16)


def col_tent():
    tent = jnp.maximum(3 - jnp.abs(iota((H, 256), 0) - 3 * (iota((H, 256), 1) - OFF) + 2), 0)
    return tent.astype(F32).astype(BF16)


def nests(params, x, drive):
    return pl.pallas_call(
        nests_kernel,
        in_specs=[VMEM] * 3,
        out_specs=[VMEM] * 5,
        out_shape=[
            pltpu.VMEM((V, H, W), F32),
            pltpu.VMEM((V, PH, PW), F32),
            pltpu.VMEM((6, V, 256), F32),
            pltpu.VMEM((256, W), BF16),
            pltpu.VMEM((H, 256), BF16),
        ],
        scratch_shapes=[
            pltpu.VMEM((H + 16, W), F32),
            pltpu.VMEM((H + 16, W), F32),
            pltpu.VMEM((H, W), F32),
            pltpu.VMEM((H, PW), F32),
        ],
        compiler_params=SMALL,
        name="nests",
    )(*near(params, x, drive))


def bank_kernel(x, drive, rows, cols):
    @pl.when(position()[0] == 0)
    def _():
        cols[...] = jnp.zeros(cols.shape, F32)
        picks, force_picks = select_rows(BANK_COLS, W), select_rows(IN_COLS, W)
        for f in range(V):
            for i, r in enumerate((0, *BANK_ROWS, H - 1)):
                rows[i, f : f + 1] = x[f, r : r + 1, :]
            for i, r in enumerate(IN_ROWS):
                band = drive[f, r // 16 * 16 : r // 16 * 16 + 16, :].astype(F32)
                rows[10 + i, f : f + 1] = band[r % 16 : r % 16 + 1]
            from_x = dot_nt(picks, x[f])
            from_drive = lax.dot_general(force_picks, drive[f], NT, preferred_element_type=F32)
            for i in range(8):
                cols[i, f : f + 1, 0:H] = from_x[i : i + 1]
            for i in range(4):
                cols[8 + i, f : f + 1, 0:H] = from_drive[i : i + 1]


def banks(x, drive):
    return pl.pallas_call(
        bank_kernel,
        in_specs=[VMEM] * 2,
        out_specs=[VMEM] * 2,
        out_shape=[pltpu.VMEM((14, V, W), F32), pltpu.VMEM((12, V, 256), F32)],
        compiler_params=SMALL,
        name="banks",
    )(*near(x, drive))


def pack_kernel(ends, north, south, to_west, to_east):
    for out, at, lo in ((to_west, 0, 0), (to_east, 3, W - 128)):
        out[0:3] = ends[at : at + 3]
        out[3, :, 0:128] = north[0, :, lo : lo + 128]
        out[3, :, 128:256] = north[1, :, lo : lo + 128]
        out[4, :, 0:128] = north[2, :, lo : lo + 128]
        out[4, :, 128:256] = south[2, :, lo : lo + 128]
        out[5, :, 0:128] = south[0, :, lo : lo + 128]
        out[5, :, 128:256] = south[1, :, lo : lo + 128]


def pack(ends, north, south):
    shape = pltpu.VMEM((6, V, 256), F32)
    return pl.pallas_call(
        pack_kernel,
        in_specs=[VMEM] * 3,
        out_specs=[VMEM] * 2,
        out_shape=[shape, shape],
        compiler_params=SMALL,
        name="pack",
    )(*near(ends, north, south))


def rims_kernel(
    params, shape, rows, cols, ends, north, south, west, east, *out
):
    section, row, column = position()
    count, columns = shape

    @pl.when(section == 0)
    def _():
        k = per_field(params, (V, 1), 0)
        a0, ae, aw, as_, an = weights_of(k, params)
        has_n = jnp.where(row > 0, 1.0, 0.0)
        has_s = jnp.where(row < count - 1, 1.0, 0.0)
        has_w = jnp.where(column > 0, 1.0, 0.0)
        has_e = jnp.where(column < columns - 1, 1.0, 0.0)
        lane128 = iota((V, 128), 1)
        lane256 = iota((V, 256), 1)
        wide = WIDE
        lane_wide = iota((V, wide), 1)
        keep = jnp.where(lane_wide < 128, has_w, jnp.where(lane_wide >= 128 + W, has_e, 1.0))
        near_w, near_e = west[0], east[0]

        def join(before, middle, after):
            return jnp.concatenate([before, middle, after], axis=1)

        def with_sides(middle, left, right):
            return join(
                jnp.where(lane128 == 127, left, 0.0), middle, jnp.where(lane128 == 0, right, 0.0)
            )

        def lanes(value, at):
            return value[:, at : at + 1]

        def halo_row(near, far, force, inner, a_far, a_inner, exists):
            value = (
                a0 * near
                + ae * pltpu.roll(near, wide - 1, 1)
                + aw * pltpu.roll(near, 1, 1)
                + a_far * far
                + a_inner * inner
                + force
            )
            return value * keep * exists

        north_1 = join(west[3, :, 0:128], north[0], east[3, :, 0:128])
        north_2 = join(west[3, :, 128:256], north[1], east[3, :, 128:256])
        north_f = join(west[4, :, 0:128], north[2], east[4, :, 0:128])
        south_1 = join(west[5, :, 0:128], south[0], east[5, :, 0:128])
        south_2 = join(west[5, :, 128:256], south[1], east[5, :, 128:256])
        south_f = join(west[4, :, 128:256], south[2], east[4, :, 128:256])
        top = with_sides(rows[0], lanes(near_w, 0), lanes(near_e, 0))
        bottom = with_sides(rows[9], lanes(near_w, H - 1), lanes(near_e, H - 1))
        new_north = halo_row(north_1, north_2, north_f, top, an, as_, has_n)
        new_south = halo_row(south_1, south_2, south_f, bottom, as_, an, has_s)

        def with_ends(column_values, before, after):
            return jnp.where(
                lane256 == 255, before, jnp.where(lane256 == H, after, column_values)
            )

        def halo_column(near, far, force, inner, a_far, a_inner, exists, at):
            full = with_ends(near, lanes(north_1, at), lanes(south_1, at))
            value = (
                a0 * full
                + as_ * pltpu.roll(full, 255, 1)
                + an * pltpu.roll(full, 1, 1)
                + a_far * far
                + a_inner * inner
                + force
            )
            new = with_ends(value * exists, lanes(new_north, at), lanes(new_south, at))
            return full, new

        at_w, at_e = 127, 128 + W
        old_west, new_west = halo_column(near_w, west[1], west[2], ends[0], aw, ae, has_w, at_w)
        old_east, new_east = halo_column(near_e, east[1], east[2], ends[3], ae, aw, has_e, at_e)

        bank = {(0, 0): north_1, (1, 0): new_north, (0, 5): south_1, (1, 5): new_south}
        side = {(0, 0): old_west, (1, 0): new_west, (0, 5): old_east, (1, 5): new_east}
        blank = jnp.zeros((V, 128), F32)
        for i, r in enumerate(IN_ROWS):
            place, at = (1, 3, 2, 4)[i], 1 + BANK_ROWS.index(r)
            old = with_sides(rows[at], lanes(near_w, r), lanes(near_e, r))
            bank[0, place] = old
            new = (
                a0 * old
                + ae * pltpu.roll(old, wide - 1, 1)
                + aw * pltpu.roll(old, 1, 1)
                + join(blank, an * rows[at - 1] + as_ * rows[at + 1] + rows[10 + i], blank)
            )
            bank[1, place] = jnp.where(
                lane_wide == 127,
                lanes(new_west, r),
                jnp.where(lane_wide == 128 + W, lanes(new_east, r), new),
            )
        for i, c in enumerate(IN_COLS):
            place, at = (1, 3, 2, 4)[i], BANK_COLS.index(c)
            old, new = halo_column(
                cols[at], cols[at - 1], cols[8 + i], cols[at + 1], aw, ae, 1.0, 128 + c
            )
            side[0, place] = old
            side[1, place] = new

        def choose(which, candidates):
            return jnp.where(
                which == 0.0, candidates[0], jnp.where(which == 1.0, candidates[1], candidates[2])
            )

        for member in range(3):
            at = PATCH_ROW + member
            patch_row = params[at : at + 1, :]
            at = PATCH_COL + member
            patch_col = params[at : at + 1, :]
            for time in range(2):
                for half in range(2):
                    line = choose(patch_row, [bank[time, 3 * half + i] for i in range(3)])
                    rim = choose(
                        patch_col[:, 0:W], [line[:, i * PW : i * PW + W] for i in range(3)]
                    )
                    rim = pltpu.roll(rim, W - 127, 1)[:, 0:256]
                    flank = choose(
                        patch_col[:, 0:256], [side[time, 3 * half + i] for i in range(3)]
                    )
                    flank = choose(
                        patch_row[:, 0:256],
                        [pltpu.roll(flank, OFF + 1 - PH * i, 1) for i in range(3)],
                    )
                    flank = jnp.where((lane256 >= OFF) & (lane256 < OFF + PH + 2), flank, 0.0)
                    place = (2 * time + half) * V
                    out[member][place : place + V, :] = jnp.where(lane256 < PW + 2, rim, flank)


def rims(shape, *arrays):
    def kernel(params, *refs):
        rims_kernel(params, shape, *refs)

    return pl.pallas_call(
        kernel,
        in_specs=[VMEM] * 8,
        out_specs=[VMEM] * 3,
        out_shape=[pltpu.VMEM((4 * V, 256), F32)] * 3,
        compiler_params=SMALL,
        name="rims",
    )(*near(*arrays))


def edge_effect(old, new, params, tent_row, tent_col):
    n = old.shape[0]
    k_row = 3.0 * per_field(params, (n, 1), 0)
    a0_row, ae, aw, as_, an = weights_of(k_row, params)
    upper = (iota((n, 1), 0) & V) == 0
    outer, inner = jnp.where(upper, an, as_), jnp.where(upper, as_, an)
    lane = iota((n, W), 1)
    east = jnp.where(lane == W - 1, 0.0, ae)
    west = jnp.where(lane == 0, 0.0, aw)

    def along_row(v):
        return a0_row * v + east * pltpu.roll(v, W - 1, 1) + west * pltpu.roll(v, 1, 1)

    row_effect = depths(
        dot_right(old, tent_row) * (1.0 / 3.0), dot_right(new, tent_row) * (1.0 / 3.0), outer, inner, along_row
    )

    if n == 2 * V:
        old, new, n = jnp.concatenate([old] * 3, axis=0), jnp.concatenate([new] * 3, axis=0), 3 * n
    k_col = 3.0 * per_field(params, (1, n), 1)
    a0_col, ae, aw, as_, an = weights_of(k_col, params)
    left = (iota((1, n), 1) & V) == 0
    outer, inner = jnp.where(left, aw, ae), jnp.where(left, ae, aw)
    down = iota((H, n), 0)
    south = jnp.where(down == H - 1, 0.0, as_)
    north = jnp.where(down == 0, 0.0, an)

    def along_column(v):
        return a0_col * v + south * pltpu.roll(v, H - 1, 0) + north * pltpu.roll(v, 1, 0)

    col_effect = depths(
        dot_nt(tent_col, old) * (1.0 / 3.0), dot_nt(tent_col, new) * (1.0 / 3.0), outer, inner, along_column
    )
    return row_effect, col_effect


def depths(old, new, outer, inner, along):
    third = (new - old) * (1.0 / 3.0)
    first_0 = outer * old
    second_0 = along(first_0) + outer * (old + third)
    second_1 = outer * first_0
    third_0 = along(second_0) + inner * second_1 + outer * (old + 2.0 * third)
    third_1 = along(second_1) + outer * second_0
    third_2 = outer * second_1
    return third_0, third_1, third_2


def spread(values, first=0):
    shape = (values.shape[1], 2 * V * 128)
    index, lane = iota(shape, 0) - first, iota(shape, 1)
    block, depth = index & (2 * V - 1), index >> 3
    target = block * 128 + jnp.where(block < V, depth, 127 - depth)
    valid = (index >= 0) & (depth < 3)
    return dot_right(values, jnp.where((lane == target) & valid, 1.0, 0.0).astype(BF16))


def last_kernel(
    nest_patch, params, x, drive, y, tent_row, tent_col, north, south, west, east,
    sent_0, sent_1, sent_2, got_0, got_1, got_2, mean_0, mean_1, mean_2, out, tile, entries, sems,
):
    section, row, column = position()
    count = nest_patch.shape[0]
    parent = section == 0
    sent, got, means = (sent_0, sent_1, sent_2), (got_0, got_1, got_2), (mean_0, mean_1, mean_2)
    n = 2 * V

    def send(f):
        return pltpu.make_async_copy(tile.at[f], out.at[f], sems.at[f])

    @pl.when(parent)
    def _():
        fetch = pltpu.make_async_copy(nest_patch, entries, sems.at[V])
        fetch.start()
        _, ae, aw, _, _ = weights_of(per_field(params, (1, n), 1), params)
        eye = jnp.where(iota((H, H), 0) == iota((H, H), 1), 1.0, 0.0).astype(BF16)
        beyond = jnp.concatenate([west[0, :, 0:H], east[0, :, 0:H]], axis=0)
        outer = jnp.where(iota((1, n), 1) < V, aw, ae)
        both = spread(dot_nt(eye, beyond) * outer)
        for f in range(V):
            coefs = closed(params[f : f + 1, 0:W], params)
            get = between(north[0, f : f + 1, :], x.at[f], south[0, f : f + 1, :])
            left, right = f * 128, (V + f) * 128
            for r in range(0, H, CHUNK):
                end = r + CHUNK
                value = step_rows(get, r, coefs, drive[f, r:end, :].astype(F32))
                tile[f, r:end, 0:128] = value[:, 0:128] + both[r:end, left : left + 128]
                tile[f, r:end, 128 : W - 128] = value[:, 128 : W - 128]
                tile[f, r:end, W - 128 : W] = (
                    value[:, W - 128 : W] + both[r:end, right : right + 128]
                )
        old = jnp.concatenate([s[0:n, :] for s in sent], axis=0)
        new = jnp.concatenate([s[n : 2 * n, :] for s in sent], axis=0)
        row_effect, col_effect = edge_effect(old, new, params, row_tent(), col_tent())
        by_row = dot_right(sum(row_effect), mean_matrix()) * (1.0 / 9.0)
        thirds = iota((PH, H), 1) - 3 * iota((PH, H), 0)
        thirds = jnp.where((thirds >= 0) & (thirds <= 2), 1.0, 0.0).astype(BF16)
        by_col = dot_left(thirds, sum(col_effect)) * (1.0 / 9.0)
        line = iota((PH, PW), 0)
        fetch.wait()
        for member in range(3):
            nest = row + member - 1
            entry = role_entry(entries, row, column, member, count)
            slot = lax.rem(entry, 9)

            @pl.when((nest >= 0) & (nest < count) & (lax.div(entry, 9) == row))
            def _(member=member, slot=slot):
                at_row = pl.multiple_of(lax.div(slot, 3) * PH, PH)
                at_col = pl.multiple_of(lax.rem(slot, 3) * PW, PW)
                mine = (iota(by_col.shape, 1) >> 3) == member
                beside = spread(jnp.where(mine, by_col, 0.0), member * n)
                for f in range(V):
                    left, right, up = f * 128, (V + f) * 128, member * n + f
                    tile[f, pl.ds(at_row, PH), pl.ds(at_col, PW)] = (
                        means[member][f]
                        + jnp.where(line == 0, by_row[up : up + 1], 0.0)
                        + jnp.where(line == PH - 1, by_row[up + V : up + V + 1], 0.0)
                        + beside[:, left : left + 128]
                        + beside[:, right : right + 128]
                    )

        for f in range(V):
            send(f).start()

    @pl.when(jnp.logical_not(parent))
    def _():
        member = params[MEMBER : MEMBER + 1, 0:256]
        u = jnp.where(
            member == 0.0, got[0][...], jnp.where(member == 1.0, got[1][...], got[2][...])
        )
        row_effect, col_effect = edge_effect(
            u[0:n], u[n : 2 * n], params, tent_row[...], tent_col[...]
        )
        depth = iota(col_effect[0].shape, 1) >> 3
        both = spread(
            jnp.where(
                depth == 0, col_effect[0], jnp.where(depth == 1, col_effect[1], col_effect[2])
            )
        )
        for f in range(V):
            left, right = f * 128, (V + f) * 128
            tile[f, :, 0:128] = y[f, :, 0:128] + both[:, left : left + 128]
            tile[f, :, 128 : W - 128] = y[f, :, 128 : W - 128]
            tile[f, :, W - 128 : W] = y[f, :, W - 128 : W] + both[:, right : right + 128]
            for depth in range(3):
                bottom = H - 1 - depth
                tile[f, depth : depth + 1, :] = (
                    tile[f, depth : depth + 1, :] + row_effect[depth][f : f + 1]
                )
                tile[f, bottom : bottom + 1, :] = (
                    tile[f, bottom : bottom + 1, :] + row_effect[depth][V + f : V + f + 1]
                )
            send(f).start()

    for f in range(V):
        send(f).wait()


def last(nest_patch, *arrays):
    return pl.pallas_call(
        last_kernel,
        in_specs=[ANY] + [VMEM] * 19,
        out_specs=ANY,
        out_shape=jax.ShapeDtypeStruct((V, H, W), F32),
        scratch_shapes=[
            pltpu.VMEM((V, H, W), F32),
            pltpu.SMEM(nest_patch.shape, jnp.int32),
            pltpu.SemaphoreType.DMA((V + 1,)),
        ],
        compiler_params=SMALL,
        name="last",
    )(*far(nest_patch), *near(*arrays))


def routes(sizes, source, move):
    _, n_rows, n_cols = sizes
    out = []
    for r in range(n_rows):
        for c in range(n_cols):
            to_sec, to_r, to_c = move(r, c)
            if 0 <= to_r < n_rows and 0 <= to_c < n_cols:
                out.append(
                    (
                        (source * n_rows + r) * n_cols + c,
                        (to_sec * n_rows + to_r) * n_cols + to_c,
                    )
                )
    return out


def on_device(sizes, *arrays):
    return compute(sizes, *arrays)


def compute(sizes, fields, forcing, courant, diffusion, nest_patch):
    x = fields.reshape(V, H, W)
    drive = forcing.reshape(V, H, W)
    courant = courant.reshape(2)

    def shift(value, source, move):
        return lax.ppermute(value, AXES, routes(sizes, source, move))

    downward, upward, params = edge(x, drive, courant, diffusion, nest_patch)
    north = shift(downward, 0, lambda r, c: (0, r + 1, c))
    south = shift(upward, 0, lambda r, c: (0, r - 1, c))
    y, mean, ends, *tents = nests(params, x, drive)
    means = [shift(mean, 1, lambda r, c, m=m: (0, r + 1 - m, c)) for m in range(3)]
    to_west, to_east = pack(ends, north, south)
    west = shift(to_east, 0, lambda r, c: (0, r, c + 1))
    east = shift(to_west, 0, lambda r, c: (0, r, c - 1))
    rows, cols = banks(x, drive)
    halos = north, south, west, east
    sent = rims(sizes[1:], params, rows, cols, ends, *halos)
    got = [shift(sent[m], 0, lambda r, c, m=m: (1, r + m - 1, c)) for m in range(3)]
    out = last(nest_patch, params, x, drive, y, *tents, *halos, *sent, *got, *means)
    return out.reshape(fields.shape)


def solution(mesh):
    sizes = tuple(mesh.shape[axis] for axis in AXES)
    spec = P("sec", None, None, "gy", "gx")
    return jax.shard_map(
        functools.partial(on_device, sizes),
        mesh=mesh,
        in_specs=(spec, spec, P(), P(), P()),
        out_specs=spec,
        check_vma=False,
    )
```

```python
import functools

import jax
import jax.numpy as jnp
from jax import lax
from jax.experimental import pallas as pl
from jax.experimental.pallas import tpu as pltpu
from jax.sharding import PartitionSpec as P


F32 = jnp.float32
BF16 = jnp.bfloat16
V, H, W = 4, 192, 384
PH, PW = H // 3, W // 3
CHUNK = 16
OFF = 160


def inner(n):
    lines = (n - 1, n, 2 * n - 1, 2 * n)
    return lines, (n - 2, n - 1, n, n + 1, 2 * n - 2, 2 * n - 1, 2 * n, 2 * n + 1)


IN_ROWS, BANK_ROWS = inner(PH)
IN_COLS, BANK_COLS = inner(PW)
WIDE = W + 256
COURANT, PATCH_ROW, PATCH_COL, MEMBER = V, V + 2, V + 5, V + 8
AXES = ("sec", "gy", "gx")
VMEM = pl.BlockSpec(memory_space=pltpu.VMEM)
ANY = pl.BlockSpec(memory_space=pl.ANY)
SMALL = pltpu.CompilerParams(vmem_limit_bytes=16 << 20)


def iota(shape, dim):
    return lax.broadcasted_iota(jnp.int32, shape, dim)


def split2(a):
    high = a.astype(BF16)
    return high, (a - high.astype(F32)).astype(BF16)


def dot_right(a, m):
    return sum(jnp.dot(part, m, preferred_element_type=F32) for part in split2(a))


def dot_nt(m, a):
    dims = (((1,), (1,)), ((), ()))
    return sum(lax.dot_general(m, part, dims, preferred_element_type=F32) for part in split2(a))


def dot_left(m, a):
    return sum(jnp.dot(m, part, preferred_element_type=F32) for part in split2(a))


def select_rows(picks, width):
    row, lane = iota((16, width), 0), iota((16, width), 1)
    wanted = jnp.full((16, width), -1, jnp.int32)
    for i, pick in enumerate(picks):
        wanted = jnp.where(row == i, pick, wanted)
    return jnp.where(lane == wanted, 1.0, 0.0).astype(BF16)


def weights(k, params):
    width = k.shape[1]
    half_x = 0.5 * params[COURANT : COURANT + 1, 0:width]
    half_y = 0.5 * params[COURANT + 1 : COURANT + 2, 0:width]
    return 1.0 - 4.0 * k, k - half_x, k + half_x, k - half_y, k + half_y


def per_field(params, shape, dim):
    index = iota(shape, dim) & (V - 1)
    out = jnp.broadcast_to(params[0:1, 0:1], shape)
    for f in range(1, V):
        out = jnp.where(index == f, params[f : f + 1, 0:1], out)
    return out


def weights_of(k, params):
    half_x = 0.5 * params[COURANT : COURANT + 1, 0:1]
    half_y = 0.5 * params[COURANT + 1 : COURANT + 2, 0:1]
    return 1.0 - 4.0 * k, k - half_x, k + half_x, k - half_y, k + half_y


def closed(k, params):
    a0, east, west, south, north = weights(k, params)
    lane = iota((1, W), 1)
    return a0, jnp.where(lane == W - 1, 0.0, east), jnp.where(lane == 0, 0.0, west), south, north


def step_rows(get, r, coefs, force):
    a0, east, west, south, north = coefs
    centre = get(r)
    return (
        a0 * centre
        + east * pltpu.roll(centre, W - 1, 1)
        + west * pltpu.roll(centre, 1, 1)
        + south * get(r + 1)
        + north * get(r - 1)
        + force
    )


def padded(ref):
    return lambda r: ref[8 + r : 8 + r + CHUNK, :]


def between(before, ref, after):
    def get(r):
        if r < 0:
            return jnp.concatenate([before, ref[0 : CHUNK - 1, :]], axis=0)
        if r + CHUNK > H:
            return jnp.concatenate([ref[r:H, :], after], axis=0)
        return ref[r : r + CHUNK, :]

    return get


def near(*values):
    return [pltpu.with_memory_space_constraint(v, pltpu.VMEM) for v in values]


def far(*values):
    return [pltpu.with_memory_space_constraint(v, pltpu.HBM) for v in values]


def position():
    return [lax.axis_index(axis) for axis in AXES]


def by_parity(index, even, odd):
    pl.when(lax.rem(index, 2) == 0)(even)
    pl.when(lax.rem(index, 2) == 1)(odd)


def edge_kernel(
    x, drive, courant, diffusion, nest_patch, one, two, params,
    x_top, x_bottom, d_top, d_bottom, c_now, k_now, entries, sems,
):
    copies = [
        pltpu.make_async_copy(source, target, sems.at[i])
        for i, (source, target) in enumerate(
            (
                (x.at[:, 0:8, :], x_top),
                (x.at[:, H - 8 : H, :], x_bottom),
                (drive.at[:, 0:16, :], d_top),
                (drive.at[:, H - 16 : H, :], d_bottom),
                (courant, c_now),
                (diffusion, k_now),
                (nest_patch, entries),
            )
        )
    ]
    for copy in copies:
        copy.start()
    for copy in copies:
        copy.wait()
    _, row, column = position()

    def fill(down, up):
        for f in range(V):
            down[0, f : f + 1] = x_bottom[f, 7:8, :]
            down[1, f : f + 1] = x_bottom[f, 6:7, :]
            down[2, f : f + 1] = d_bottom[f].astype(F32)[15:16]
            up[0, f : f + 1] = x_top[f, 0:1, :]
            up[1, f : f + 1] = x_top[f, 1:2, :]
            up[2, f : f + 1] = d_top[f].astype(F32)[0:1]

    by_parity(row, lambda: fill(one, two), lambda: fill(two, one))

    def put(at, value):
        params[at : at + 1, :] = jnp.full((1, WIDE), value, F32)

    for f in range(V):
        put(f, k_now[f])
    put(COURANT, c_now[0])
    put(COURANT + 1, c_now[1])
    count = nest_patch.shape[0]
    for member in range(3):
        slot = lax.rem(role_entry(entries, row, column, member, count), 9)
        put(PATCH_ROW + member, lax.div(slot, 3).astype(F32))
        put(PATCH_COL + member, lax.rem(slot, 3).astype(F32))
    put(MEMBER, (row - lax.div(entries[row, column], 9) + 1).astype(F32))


def edge(x, drive, courant, diffusion, nest_patch):
    return pl.pallas_call(
        edge_kernel,
        in_specs=[ANY] * 5,
        out_specs=[VMEM] * 3,
        out_shape=[
            pltpu.VMEM((3, V, W), F32),
            pltpu.VMEM((3, V, W), F32),
            pltpu.VMEM((16, WIDE), F32),
        ],
        scratch_shapes=[
            pltpu.VMEM((V, 8, W), F32),
            pltpu.VMEM((V, 8, W), F32),
            pltpu.VMEM((V, 16, W), BF16),
            pltpu.VMEM((V, 16, W), BF16),
            pltpu.SMEM((2,), F32),
            pltpu.SMEM((V,), F32),
            pltpu.SMEM(nest_patch.shape, jnp.int32),
            pltpu.SemaphoreType.DMA((7,)),
        ],
        compiler_params=SMALL,
        name="edge",
    )(*far(x, drive, courant, diffusion, nest_patch))


def role_entry(entries, row, column, member, count):
    nest = jnp.clip(row + member - 1, 0, count - 1)
    return entries[nest, column]


NT = (((1,), (1,)), ((), ()))


def nests_kernel(
    params, x, drive, y, mean, ends, tent_row, tent_col, two, three, force, thirds
):
    parent = position()[0] == 0

    @pl.when(parent)
    def _():
        ends[...] = jnp.zeros(ends.shape, F32)
        none = -1
        x_west, x_east = select_rows((0, 1), 128), select_rows((none, none, none, 127, 126), 128)
        d_west = select_rows((none, none, 0), 128)
        d_east = select_rows((none, none, none, none, none, 127), 128)
        for f in range(V):
            values = dot_nt(x_west, x[f, :, 0:128]) + dot_nt(x_east, x[f, :, W - 128 : W])
            values = values + lax.dot_general(
                d_west, drive[f, :, 0:128], NT, preferred_element_type=F32
            )
            values = values + lax.dot_general(
                d_east, drive[f, :, W - 128 : W], NT, preferred_element_type=F32
            )
            for i in range(6):
                ends[i, f : f + 1, 0:H] = values[i : i + 1]

    @pl.when(jnp.logical_not(parent))
    def _():
        for buffer in (two, three):
            buffer[0:8, :] = jnp.zeros((8, W), F32)
            buffer[H + 8 : H + 16, :] = jnp.zeros((8, W), F32)
        blocks = mean_matrix()
        zero = jnp.zeros((1, W), F32)
        tent_row[...] = row_tent()
        tent_col[...] = col_tent()

        @pl.loop(0, V)
        def _(f):
            coefs = closed(3.0 * params[pl.ds(f, 1), :][:, 0:W], params)

            def step(get, new, at):
                for r in range(0, H, CHUNK):
                    new[at + r : at + r + CHUNK, :] = step_rows(
                        get, r, coefs, force[r : r + CHUNK, :]
                    )

            force[...] = drive[f].astype(F32) * (1.0 / 3.0)
            step(between(zero, x.at[f], zero), two, 8)
            step(padded(two), three, 8)
            step(padded(three), y.at[f], 0)
            thirds[...] = dot_right(y[f], blocks)
            total = (
                thirds[pl.ds(0, PH, stride=3), :]
                + thirds[pl.ds(1, PH, stride=3), :]
                + thirds[pl.ds(2, PH, stride=3), :]
            )
            mean[f] = total * (1.0 / 9.0)


def mean_matrix():
    gap = iota((W, PW), 0) - 3 * iota((W, PW), 1)
    return jnp.where((gap >= 0) & (gap <= 2), 1.0, 0.0).astype(BF16)


def row_tent():
    tent = jnp.maximum(3 - jnp.abs(iota((256, W), 1) - 3 * iota((256, W), 0) + 2), 0)
    return tent.astype(F32).astype(BF16)


def col_tent():
    tent = jnp.maximum(3 - jnp.abs(iota((H, 256), 0) - 3 * (iota((H, 256), 1) - OFF) + 2), 0)
    return tent.astype(F32).astype(BF16)


def nests(params, x, drive):
    return pl.pallas_call(
        nests_kernel,
        in_specs=[VMEM] * 3,
        out_specs=[VMEM] * 5,
        out_shape=[
            pltpu.VMEM((V, H, W), F32),
            pltpu.VMEM((V, PH, PW), F32),
            pltpu.VMEM((6, V, 256), F32),
            pltpu.VMEM((256, W), BF16),
            pltpu.VMEM((H, 256), BF16),
        ],
        scratch_shapes=[
            pltpu.VMEM((H + 16, W), F32),
            pltpu.VMEM((H + 16, W), F32),
            pltpu.VMEM((H, W), F32),
            pltpu.VMEM((H, PW), F32),
        ],
        compiler_params=SMALL,
        name="nests",
    )(*near(params, x, drive))


def bank_kernel(x, drive, rows, cols):
    @pl.when(position()[0] == 0)
    def _():
        cols[...] = jnp.zeros(cols.shape, F32)
        picks, force_picks = select_rows(BANK_COLS, W), select_rows(IN_COLS, W)
        for f in range(V):
            for i, r in enumerate((0, *BANK_ROWS, H - 1)):
                rows[i, f : f + 1] = x[f, r : r + 1, :]
            for i, r in enumerate(IN_ROWS):
                band = drive[f, r // 16 * 16 : r // 16 * 16 + 16, :].astype(F32)
                rows[10 + i, f : f + 1] = band[r % 16 : r % 16 + 1]
            from_x = dot_nt(picks, x[f])
            from_drive = lax.dot_general(force_picks, drive[f], NT, preferred_element_type=F32)
            for i in range(8):
                cols[i, f : f + 1, 0:H] = from_x[i : i + 1]
            for i in range(4):
                cols[8 + i, f : f + 1, 0:H] = from_drive[i : i + 1]


def banks(x, drive):
    return pl.pallas_call(
        bank_kernel,
        in_specs=[VMEM] * 2,
        out_specs=[VMEM] * 2,
        out_shape=[pltpu.VMEM((14, V, W), F32), pltpu.VMEM((12, V, 256), F32)],
        compiler_params=SMALL,
        name="banks",
    )(*near(x, drive))


def pack_kernel(ends, from_one, from_two, one, two, north, south):
    section, row, column = position()

    def sort(up, down):
        north[...] = up[...]
        south[...] = down[...]

    def fill(to_west, to_east):
        for out, at, lo in ((to_west, 0, 0), (to_east, 3, W - 128)):
            out[0:3] = ends[at : at + 3]
            out[3, :, 0:128] = north[0, :, lo : lo + 128]
            out[3, :, 128:256] = north[1, :, lo : lo + 128]
            out[4, :, 0:128] = north[2, :, lo : lo + 128]
            out[4, :, 128:256] = south[2, :, lo : lo + 128]
            out[5, :, 0:128] = south[0, :, lo : lo + 128]
            out[5, :, 128:256] = south[1, :, lo : lo + 128]

    @pl.when(section == 0)
    def _():
        by_parity(row, lambda: sort(from_two, from_one), lambda: sort(from_one, from_two))
        by_parity(column, lambda: fill(two, one), lambda: fill(one, two))


def pack(ends, from_one, from_two):
    flank, row = pltpu.VMEM((6, V, 256), F32), pltpu.VMEM((3, V, W), F32)
    return pl.pallas_call(
        pack_kernel,
        in_specs=[VMEM] * 3,
        out_specs=[VMEM] * 4,
        out_shape=[flank, flank, row, row],
        compiler_params=SMALL,
        name="pack",
    )(*near(ends, from_one, from_two))


def rims_kernel(
    params, shape, rows, cols, ends, north, south, from_one, from_two, *out
):
    *out, beyond, west, east = out
    section, row, column = position()
    count, columns = shape

    def sort(left, right):
        west[...] = left[...]
        east[...] = right[...]

    @pl.when(section == 0)
    def _():
        by_parity(column, lambda: sort(from_two, from_one), lambda: sort(from_one, from_two))
        beyond[0:V] = west[0]
        beyond[V : 2 * V] = east[0]
        k = per_field(params, (V, 1), 0)
        a0, ae, aw, as_, an = weights_of(k, params)
        has_n = jnp.where(row > 0, 1.0, 0.0)
        has_s = jnp.where(row < count - 1, 1.0, 0.0)
        has_w = jnp.where(column > 0, 1.0, 0.0)
        has_e = jnp.where(column < columns - 1, 1.0, 0.0)
        lane128 = iota((V, 128), 1)
        lane256 = iota((V, 256), 1)
        wide = WIDE
        lane_wide = iota((V, wide), 1)
        keep = jnp.where(lane_wide < 128, has_w, jnp.where(lane_wide >= 128 + W, has_e, 1.0))
        near_w, near_e = west[0], east[0]

        def join(before, middle, after):
            return jnp.concatenate([before, middle, after], axis=1)

        def with_sides(middle, left, right):
            return join(
                jnp.where(lane128 == 127, left, 0.0), middle, jnp.where(lane128 == 0, right, 0.0)
            )

        def lanes(value, at):
            return value[:, at : at + 1]

        def halo_row(near, far, force, inner, a_far, a_inner, exists):
            value = (
                a0 * near
                + ae * pltpu.roll(near, wide - 1, 1)
                + aw * pltpu.roll(near, 1, 1)
                + a_far * far
                + a_inner * inner
                + force
            )
            return value * keep * exists

        north_1 = join(west[3, :, 0:128], north[0], east[3, :, 0:128])
        north_2 = join(west[3, :, 128:256], north[1], east[3, :, 128:256])
        north_f = join(west[4, :, 0:128], north[2], east[4, :, 0:128])
        south_1 = join(west[5, :, 0:128], south[0], east[5, :, 0:128])
        south_2 = join(west[5, :, 128:256], south[1], east[5, :, 128:256])
        south_f = join(west[4, :, 128:256], south[2], east[4, :, 128:256])
        top = with_sides(rows[0], lanes(near_w, 0), lanes(near_e, 0))
        bottom = with_sides(rows[9], lanes(near_w, H - 1), lanes(near_e, H - 1))
        new_north = halo_row(north_1, north_2, north_f, top, an, as_, has_n)
        new_south = halo_row(south_1, south_2, south_f, bottom, as_, an, has_s)

        def with_ends(column_values, before, after):
            return jnp.where(
                lane256 == 255, before, jnp.where(lane256 == H, after, column_values)
            )

        def halo_column(near, far, force, inner, a_far, a_inner, exists, at):
            full = with_ends(near, lanes(north_1, at), lanes(south_1, at))
            value = (
                a0 * full
                + as_ * pltpu.roll(full, 255, 1)
                + an * pltpu.roll(full, 1, 1)
                + a_far * far
                + a_inner * inner
                + force
            )
            new = with_ends(value * exists, lanes(new_north, at), lanes(new_south, at))
            return full, new

        at_w, at_e = 127, 128 + W
        old_west, new_west = halo_column(near_w, west[1], west[2], ends[0], aw, ae, has_w, at_w)
        old_east, new_east = halo_column(near_e, east[1], east[2], ends[3], ae, aw, has_e, at_e)

        bank = {(0, 0): north_1, (1, 0): new_north, (0, 5): south_1, (1, 5): new_south}
        side = {(0, 0): old_west, (1, 0): new_west, (0, 5): old_east, (1, 5): new_east}
        blank = jnp.zeros((V, 128), F32)
        for i, r in enumerate(IN_ROWS):
            place, at = (1, 3, 2, 4)[i], 1 + BANK_ROWS.index(r)
            old = with_sides(rows[at], lanes(near_w, r), lanes(near_e, r))
            bank[0, place] = old
            new = (
                a0 * old
                + ae * pltpu.roll(old, wide - 1, 1)
                + aw * pltpu.roll(old, 1, 1)
                + join(blank, an * rows[at - 1] + as_ * rows[at + 1] + rows[10 + i], blank)
            )
            bank[1, place] = jnp.where(
                lane_wide == 127,
                lanes(new_west, r),
                jnp.where(lane_wide == 128 + W, lanes(new_east, r), new),
            )
        for i, c in enumerate(IN_COLS):
            place, at = (1, 3, 2, 4)[i], BANK_COLS.index(c)
            old, new = halo_column(
                cols[at], cols[at - 1], cols[8 + i], cols[at + 1], aw, ae, 1.0, 128 + c
            )
            side[0, place] = old
            side[1, place] = new

        def choose(which, candidates):
            return jnp.where(
                which == 0.0, candidates[0], jnp.where(which == 1.0, candidates[1], candidates[2])
            )

        for member in range(3):
            at = PATCH_ROW + member
            patch_row = params[at : at + 1, :]
            at = PATCH_COL + member
            patch_col = params[at : at + 1, :]
            for time in range(2):
                for half in range(2):
                    line = choose(patch_row, [bank[time, 3 * half + i] for i in range(3)])
                    rim = choose(
                        patch_col[:, 0:W], [line[:, i * PW : i * PW + W] for i in range(3)]
                    )
                    rim = pltpu.roll(rim, W - 127, 1)[:, 0:256]
                    flank = choose(
                        patch_col[:, 0:256], [side[time, 3 * half + i] for i in range(3)]
                    )
                    flank = choose(
                        patch_row[:, 0:256],
                        [pltpu.roll(flank, OFF + 1 - PH * i, 1) for i in range(3)],
                    )
                    flank = jnp.where((lane256 >= OFF) & (lane256 < OFF + PH + 2), flank, 0.0)
                    place = (2 * time + half) * V
                    out[member][place : place + V, :] = jnp.where(lane256 < PW + 2, rim, flank)


def rims(shape, *arrays):
    def kernel(params, *refs):
        rims_kernel(params, shape, *refs)

    return pl.pallas_call(
        kernel,
        in_specs=[VMEM] * 8,
        out_specs=[VMEM] * 4,
        out_shape=[pltpu.VMEM((4 * V, 256), F32)] * 3 + [pltpu.VMEM((2 * V, 256), F32)],
        scratch_shapes=[pltpu.VMEM((6, V, 256), F32)] * 2,
        compiler_params=SMALL,
        name="rims",
    )(*near(*arrays))


def edge_effect(old, new, params, tent_row, tent_col):
    n = old.shape[0]
    k_row = 3.0 * per_field(params, (n, 1), 0)
    a0_row, ae, aw, as_, an = weights_of(k_row, params)
    upper = (iota((n, 1), 0) & V) == 0
    outer, inner = jnp.where(upper, an, as_), jnp.where(upper, as_, an)
    lane = iota((n, W), 1)
    east = jnp.where(lane == W - 1, 0.0, ae)
    west = jnp.where(lane == 0, 0.0, aw)

    def along_row(v):
        return a0_row * v + east * pltpu.roll(v, W - 1, 1) + west * pltpu.roll(v, 1, 1)

    row_effect = depths(
        dot_right(old, tent_row) * (1.0 / 3.0), dot_right(new, tent_row) * (1.0 / 3.0), outer, inner, along_row
    )

    if n == 2 * V:
        old, new, n = jnp.concatenate([old] * 3, axis=0), jnp.concatenate([new] * 3, axis=0), 3 * n
    k_col = 3.0 * per_field(params, (1, n), 1)
    a0_col, ae, aw, as_, an = weights_of(k_col, params)
    left = (iota((1, n), 1) & V) == 0
    outer, inner = jnp.where(left, aw, ae), jnp.where(left, ae, aw)
    down = iota((H, n), 0)
    south = jnp.where(down == H - 1, 0.0, as_)
    north = jnp.where(down == 0, 0.0, an)

    def along_column(v):
        return a0_col * v + south * pltpu.roll(v, H - 1, 0) + north * pltpu.roll(v, 1, 0)

    col_effect = depths(
        dot_nt(tent_col, old) * (1.0 / 3.0), dot_nt(tent_col, new) * (1.0 / 3.0), outer, inner, along_column
    )
    return row_effect, col_effect


def depths(old, new, outer, inner, along):
    third = (new - old) * (1.0 / 3.0)
    first_0 = outer * old
    second_0 = along(first_0) + outer * (old + third)
    second_1 = outer * first_0
    third_0 = along(second_0) + inner * second_1 + outer * (old + 2.0 * third)
    third_1 = along(second_1) + outer * second_0
    third_2 = outer * second_1
    return third_0, third_1, third_2


def spread(values, first=0):
    shape = (values.shape[1], 2 * V * 128)
    index, lane = iota(shape, 0) - first, iota(shape, 1)
    block, depth = index & (2 * V - 1), index >> 3
    target = block * 128 + jnp.where(block < V, depth, 127 - depth)
    valid = (index >= 0) & (depth < 3)
    return dot_right(values, jnp.where((lane == target) & valid, 1.0, 0.0).astype(BF16))


def last_kernel(
    nest_patch, params, x, drive, y, tent_row, tent_col, north, south, beyond,
    sent_0, sent_1, sent_2, got_0, got_1, got_2, mean_0, mean_1, mean_2, out, tile, entries, sems,
):
    section, row, column = position()
    count = nest_patch.shape[0]
    parent = section == 0
    sent, got, means = (sent_0, sent_1, sent_2), (got_0, got_1, got_2), (mean_0, mean_1, mean_2)
    n = 2 * V

    def send(f):
        return pltpu.make_async_copy(tile.at[f], out.at[f], sems.at[f])

    @pl.when(parent)
    def _():
        fetch = pltpu.make_async_copy(nest_patch, entries, sems.at[V])
        fetch.start()
        _, ae, aw, _, _ = weights_of(per_field(params, (1, n), 1), params)
        eye = jnp.where(iota((H, H), 0) == iota((H, H), 1), 1.0, 0.0).astype(BF16)
        outer = jnp.where(iota((1, n), 1) < V, aw, ae)
        both = spread(dot_nt(eye, beyond[:, 0:H]) * outer)
        for f in range(V):
            coefs = closed(params[f : f + 1, 0:W], params)
            get = between(north[0, f : f + 1, :], x.at[f], south[0, f : f + 1, :])
            left, right = f * 128, (V + f) * 128
            for r in range(0, H, CHUNK):
                end = r + CHUNK
                value = step_rows(get, r, coefs, drive[f, r:end, :].astype(F32))
                tile[f, r:end, 0:128] = value[:, 0:128] + both[r:end, left : left + 128]
                tile[f, r:end, 128 : W - 128] = value[:, 128 : W - 128]
                tile[f, r:end, W - 128 : W] = (
                    value[:, W - 128 : W] + both[r:end, right : right + 128]
                )
        old = jnp.concatenate([s[0:n, :] for s in sent], axis=0)
        new = jnp.concatenate([s[n : 2 * n, :] for s in sent], axis=0)
        row_effect, col_effect = edge_effect(old, new, params, row_tent(), col_tent())
        by_row = dot_right(sum(row_effect), mean_matrix()) * (1.0 / 9.0)
        thirds = iota((PH, H), 1) - 3 * iota((PH, H), 0)
        thirds = jnp.where((thirds >= 0) & (thirds <= 2), 1.0, 0.0).astype(BF16)
        by_col = dot_left(thirds, sum(col_effect)) * (1.0 / 9.0)
        line = iota((PH, PW), 0)
        fetch.wait()
        for member in range(3):
            nest = row + member - 1
            entry = role_entry(entries, row, column, member, count)
            slot = lax.rem(entry, 9)

            @pl.when((nest >= 0) & (nest < count) & (lax.div(entry, 9) == row))
            def _(member=member, slot=slot):
                at_row = pl.multiple_of(lax.div(slot, 3) * PH, PH)
                at_col = pl.multiple_of(lax.rem(slot, 3) * PW, PW)
                mine = (iota(by_col.shape, 1) >> 3) == member
                beside = spread(jnp.where(mine, by_col, 0.0), member * n)
                for f in range(V):
                    left, right, up = f * 128, (V + f) * 128, member * n + f
                    tile[f, pl.ds(at_row, PH), pl.ds(at_col, PW)] = (
                        means[member][f]
                        + jnp.where(line == 0, by_row[up : up + 1], 0.0)
                        + jnp.where(line == PH - 1, by_row[up + V : up + V + 1], 0.0)
                        + beside[:, left : left + 128]
                        + beside[:, right : right + 128]
                    )

        for f in range(V):
            send(f).start()

    @pl.when(jnp.logical_not(parent))
    def _():
        member = params[MEMBER : MEMBER + 1, 0:256]
        u = jnp.where(
            member == 0.0, got[0][...], jnp.where(member == 1.0, got[1][...], got[2][...])
        )
        row_effect, col_effect = edge_effect(
            u[0:n], u[n : 2 * n], params, tent_row[...], tent_col[...]
        )
        depth = iota(col_effect[0].shape, 1) >> 3
        both = spread(
            jnp.where(
                depth == 0, col_effect[0], jnp.where(depth == 1, col_effect[1], col_effect[2])
            )
        )
        for f in range(V):
            left, right = f * 128, (V + f) * 128
            tile[f, :, 0:128] = y[f, :, 0:128] + both[:, left : left + 128]
            tile[f, :, 128 : W - 128] = y[f, :, 128 : W - 128]
            tile[f, :, W - 128 : W] = y[f, :, W - 128 : W] + both[:, right : right + 128]
            for depth in range(3):
                bottom = H - 1 - depth
                tile[f, depth : depth + 1, :] = (
                    tile[f, depth : depth + 1, :] + row_effect[depth][f : f + 1]
                )
                tile[f, bottom : bottom + 1, :] = (
                    tile[f, bottom : bottom + 1, :] + row_effect[depth][V + f : V + f + 1]
                )
            send(f).start()

    for f in range(V):
        send(f).wait()


def last(nest_patch, *arrays):
    return pl.pallas_call(
        last_kernel,
        in_specs=[ANY] + [VMEM] * 18,
        out_specs=ANY,
        out_shape=jax.ShapeDtypeStruct((V, H, W), F32),
        scratch_shapes=[
            pltpu.VMEM((V, H, W), F32),
            pltpu.SMEM(nest_patch.shape, jnp.int32),
            pltpu.SemaphoreType.DMA((V + 1,)),
        ],
        compiler_params=SMALL,
        name="last",
    )(*far(nest_patch), *near(*arrays))


def routes(sizes, source, move):
    _, n_rows, n_cols = sizes
    out = []
    for r in range(n_rows):
        for c in range(n_cols):
            to_sec, to_r, to_c = move(r, c)
            if 0 <= to_r < n_rows and 0 <= to_c < n_cols:
                out.append(
                    (
                        (source * n_rows + r) * n_cols + c,
                        (to_sec * n_rows + to_r) * n_cols + to_c,
                    )
                )
    return out


def on_device(sizes, *arrays):
    return compute(sizes, *arrays)


def compute(sizes, fields, forcing, courant, diffusion, nest_patch):
    x = fields.reshape(V, H, W)
    drive = forcing.reshape(V, H, W)
    courant = courant.reshape(2)

    def shift(value, source, move):
        return lax.ppermute(value, AXES, routes(sizes, source, move))

    def partner(index, first):
        return index + 1 if index % 2 == first else index - 1

    rows_one, rows_two, params = edge(x, drive, courant, diffusion, nest_patch)
    rows_one = shift(rows_one, 0, lambda r, c: (0, partner(r, 0), c))
    rows_two = shift(rows_two, 0, lambda r, c: (0, partner(r, 1), c))
    y, mean, ends, *tents = nests(params, x, drive)
    means = [shift(mean, 1, lambda r, c, m=m: (0, r + 1 - m, c)) for m in range(3)]
    cols_one, cols_two, north, south = pack(ends, rows_one, rows_two)
    cols_one = shift(cols_one, 0, lambda r, c: (0, r, partner(c, 0)))
    cols_two = shift(cols_two, 0, lambda r, c: (0, r, partner(c, 1)))
    rows, cols = banks(x, drive)
    *sent, beyond = rims(
        sizes[1:], params, rows, cols, ends, north, south, cols_one, cols_two
    )
    got = [shift(sent[m], 0, lambda r, c, m=m: (1, r + m - 1, c)) for m in range(3)]
    out = last(
        nest_patch, params, x, drive, y, *tents, north, south, beyond, *sent, *got, *means
    )
    return out.reshape(fields.shape)


def solution(mesh):
    sizes = tuple(mesh.shape[axis] for axis in AXES)
    spec = P("sec", None, None, "gy", "gx")
    return jax.shard_map(
        functools.partial(on_device, sizes),
        mesh=mesh,
        in_specs=(spec, spec, P(), P(), P()),
        out_specs=spec,
        check_vma=False,
    )
```

```python
import functools

import jax
import jax.numpy as jnp
from jax import lax
from jax.experimental import pallas as pl
from jax.experimental.pallas import tpu as pltpu
from jax.sharding import PartitionSpec as P


F32 = jnp.float32
BF16 = jnp.bfloat16
V, H, W = 4, 192, 384
PH, PW = H // 3, W // 3
CHUNK = 16
OFF = 160


def inner(n):
    lines = (n - 1, n, 2 * n - 1, 2 * n)
    return lines, (n - 2, n - 1, n, n + 1, 2 * n - 2, 2 * n - 1, 2 * n, 2 * n + 1)


IN_ROWS, BANK_ROWS = inner(PH)
IN_COLS, BANK_COLS = inner(PW)
WIDE = W + 256
COURANT, PATCH_ROW, PATCH_COL, MEMBER = V, V + 2, V + 5, V + 8
AXES = ("sec", "gy", "gx")
VMEM = pl.BlockSpec(memory_space=pltpu.VMEM)
ANY = pl.BlockSpec(memory_space=pl.ANY)
SMALL = pltpu.CompilerParams(vmem_limit_bytes=16 << 20)


def iota(shape, dim):
    return lax.broadcasted_iota(jnp.int32, shape, dim)


def split2(a):
    high = a.astype(BF16)
    return high, (a - high.astype(F32)).astype(BF16)


def dot_right(a, m):
    return sum(jnp.dot(part, m, preferred_element_type=F32) for part in split2(a))


def dot_nt(m, a):
    dims = (((1,), (1,)), ((), ()))
    return sum(lax.dot_general(m, part, dims, preferred_element_type=F32) for part in split2(a))


def dot_left(m, a):
    return sum(jnp.dot(m, part, preferred_element_type=F32) for part in split2(a))


def select_rows(picks, width):
    row, lane = iota((16, width), 0), iota((16, width), 1)
    wanted = jnp.full((16, width), -1, jnp.int32)
    for i, pick in enumerate(picks):
        wanted = jnp.where(row == i, pick, wanted)
    return jnp.where(lane == wanted, 1.0, 0.0).astype(BF16)


def weights(k, params):
    width = k.shape[1]
    half_x = 0.5 * params[COURANT : COURANT + 1, 0:width]
    half_y = 0.5 * params[COURANT + 1 : COURANT + 2, 0:width]
    return 1.0 - 4.0 * k, k - half_x, k + half_x, k - half_y, k + half_y


def per_field(params, shape, dim):
    index = iota(shape, dim) & (V - 1)
    out = jnp.broadcast_to(params[0:1, 0:1], shape)
    for f in range(1, V):
        out = jnp.where(index == f, params[f : f + 1, 0:1], out)
    return out


def weights_of(k, params):
    half_x = 0.5 * params[COURANT : COURANT + 1, 0:1]
    half_y = 0.5 * params[COURANT + 1 : COURANT + 2, 0:1]
    return 1.0 - 4.0 * k, k - half_x, k + half_x, k - half_y, k + half_y


def closed(k, params):
    a0, east, west, south, north = weights(k, params)
    lane = iota((1, W), 1)
    return a0, jnp.where(lane == W - 1, 0.0, east), jnp.where(lane == 0, 0.0, west), south, north


def step_rows(get, r, coefs, force):
    a0, east, west, south, north = coefs
    centre = get(r)
    return (
        a0 * centre
        + east * pltpu.roll(centre, W - 1, 1)
        + west * pltpu.roll(centre, 1, 1)
        + south * get(r + 1)
        + north * get(r - 1)
        + force
    )


def padded(ref):
    return lambda r: ref[8 + r : 8 + r + CHUNK, :]


def between(before, ref, after):
    def get(r):
        if r < 0:
            return jnp.concatenate([before, ref[0 : CHUNK - 1, :]], axis=0)
        if r + CHUNK > H:
            return jnp.concatenate([ref[r:H, :], after], axis=0)
        return ref[r : r + CHUNK, :]

    return get


def near(*values):
    return [pltpu.with_memory_space_constraint(v, pltpu.VMEM) for v in values]


def far(*values):
    return [pltpu.with_memory_space_constraint(v, pltpu.HBM) for v in values]


def position():
    return [lax.axis_index(axis) for axis in AXES]


def by_parity(index, even, odd):
    pl.when(lax.rem(index, 2) == 0)(even)
    pl.when(lax.rem(index, 2) == 1)(odd)


def edge_kernel(
    x, drive, courant, diffusion, nest_patch, one, two, params,
    x_top, x_bottom, d_top, d_bottom, c_now, k_now, entries, sems,
):
    copies = [
        pltpu.make_async_copy(source, target, sems.at[i])
        for i, (source, target) in enumerate(
            (
                (x.at[:, 0:8, :], x_top),
                (x.at[:, H - 8 : H, :], x_bottom),
                (drive.at[:, 0:16, :], d_top),
                (drive.at[:, H - 16 : H, :], d_bottom),
                (courant, c_now),
                (diffusion, k_now),
                (nest_patch, entries),
            )
        )
    ]
    for copy in copies:
        copy.start()
    for copy in copies:
        copy.wait()
    _, row, column = position()

    def fill(down, up):
        for f in range(V):
            down[0, f : f + 1] = x_bottom[f, 7:8, :]
            down[1, f : f + 1] = x_bottom[f, 6:7, :]
            down[2, f : f + 1] = d_bottom[f].astype(F32)[15:16]
            up[0, f : f + 1] = x_top[f, 0:1, :]
            up[1, f : f + 1] = x_top[f, 1:2, :]
            up[2, f : f + 1] = d_top[f].astype(F32)[0:1]

    by_parity(row, lambda: fill(one, two), lambda: fill(two, one))

    def put(at, value):
        params[at : at + 1, :] = jnp.full((1, WIDE), value, F32)

    for f in range(V):
        put(f, k_now[f])
    put(COURANT, c_now[0])
    put(COURANT + 1, c_now[1])
    count = nest_patch.shape[0]
    for member in range(3):
        slot = lax.rem(role_entry(entries, row, column, member, count), 9)
        put(PATCH_ROW + member, lax.div(slot, 3).astype(F32))
        put(PATCH_COL + member, lax.rem(slot, 3).astype(F32))
    put(MEMBER, (row - lax.div(entries[row, column], 9) + 1).astype(F32))


def edge(x, drive, courant, diffusion, nest_patch):
    return pl.pallas_call(
        edge_kernel,
        in_specs=[ANY] * 5,
        out_specs=[VMEM] * 3,
        out_shape=[
            pltpu.VMEM((3, V, W), F32),
            pltpu.VMEM((3, V, W), F32),
            pltpu.VMEM((16, WIDE), F32),
        ],
        scratch_shapes=[
            pltpu.VMEM((V, 8, W), F32),
            pltpu.VMEM((V, 8, W), F32),
            pltpu.VMEM((V, 16, W), BF16),
            pltpu.VMEM((V, 16, W), BF16),
            pltpu.SMEM((2,), F32),
            pltpu.SMEM((V,), F32),
            pltpu.SMEM(nest_patch.shape, jnp.int32),
            pltpu.SemaphoreType.DMA((7,)),
        ],
        compiler_params=SMALL,
        name="edge",
    )(*far(x, drive, courant, diffusion, nest_patch))


def role_entry(entries, row, column, member, count):
    nest = jnp.clip(row + member - 1, 0, count - 1)
    return entries[nest, column]


NT = (((1,), (1,)), ((), ()))


def nests_kernel(
    params, x, drive, y, mean, ends, tent_row, tent_col, two, three, force, thirds
):
    parent = position()[0] == 0

    @pl.when(parent)
    def _():
        ends[...] = jnp.zeros(ends.shape, F32)
        none = -1
        x_west, x_east = select_rows((0, 1), 128), select_rows((none, none, none, 127, 126), 128)
        d_west = select_rows((none, none, 0), 128)
        d_east = select_rows((none, none, none, none, none, 127), 128)
        for f in range(V):
            values = dot_nt(x_west, x[f, :, 0:128]) + dot_nt(x_east, x[f, :, W - 128 : W])
            values = values + lax.dot_general(
                d_west, drive[f, :, 0:128], NT, preferred_element_type=F32
            )
            values = values + lax.dot_general(
                d_east, drive[f, :, W - 128 : W], NT, preferred_element_type=F32
            )
            for i in range(6):
                ends[i, f : f + 1, 0:H] = values[i : i + 1]

    @pl.when(jnp.logical_not(parent))
    def _():
        for buffer in (two, three):
            buffer[0:8, :] = jnp.zeros((8, W), F32)
            buffer[H + 8 : H + 16, :] = jnp.zeros((8, W), F32)
        blocks = mean_matrix()
        zero = jnp.zeros((1, W), F32)
        tent_row[...] = row_tent()
        tent_col[...] = col_tent()

        @pl.loop(0, V)
        def _(f):
            coefs = closed(3.0 * params[pl.ds(f, 1), :][:, 0:W], params)

            def step(get, new, at):
                for r in range(0, H, CHUNK):
                    new[at + r : at + r + CHUNK, :] = step_rows(
                        get, r, coefs, force[r : r + CHUNK, :]
                    )

            force[...] = drive[f].astype(F32) * (1.0 / 3.0)
            step(between(zero, x.at[f], zero), two, 8)
            step(padded(two), three, 8)
            step(padded(three), y.at[f], 0)
            thirds[...] = dot_right(y[f], blocks)
            total = (
                thirds[pl.ds(0, PH, stride=3), :]
                + thirds[pl.ds(1, PH, stride=3), :]
                + thirds[pl.ds(2, PH, stride=3), :]
            )
            mean[f] = total * (1.0 / 9.0)


def mean_matrix():
    gap = iota((W, PW), 0) - 3 * iota((W, PW), 1)
    return jnp.where((gap >= 0) & (gap <= 2), 1.0, 0.0).astype(BF16)


def row_tent():
    tent = jnp.maximum(3 - jnp.abs(iota((256, W), 1) - 3 * iota((256, W), 0) + 2), 0)
    return tent.astype(F32).astype(BF16)


def col_tent():
    tent = jnp.maximum(3 - jnp.abs(iota((H, 256), 0) - 3 * (iota((H, 256), 1) - OFF) + 2), 0)
    return tent.astype(F32).astype(BF16)


def nests(params, x, drive):
    return pl.pallas_call(
        nests_kernel,
        in_specs=[VMEM] * 3,
        out_specs=[VMEM] * 5,
        out_shape=[
            pltpu.VMEM((V, H, W), F32),
            pltpu.VMEM((V, PH, PW), F32),
            pltpu.VMEM((6, V, 256), F32),
            pltpu.VMEM((256, W), BF16),
            pltpu.VMEM((H, 256), BF16),
        ],
        scratch_shapes=[
            pltpu.VMEM((H + 16, W), F32),
            pltpu.VMEM((H + 16, W), F32),
            pltpu.VMEM((H, W), F32),
            pltpu.VMEM((H, PW), F32),
        ],
        compiler_params=SMALL,
        name="nests",
    )(*near(params, x, drive))


def bank_kernel(params, x, drive, north, south, rows, cols, y):
    @pl.when(position()[0] == 0)
    def _():
        cols[...] = jnp.zeros(cols.shape, F32)
        picks, force_picks = select_rows(BANK_COLS, W), select_rows(IN_COLS, W)
        for f in range(V):
            for i, r in enumerate((0, *BANK_ROWS, H - 1)):
                rows[i, f : f + 1] = x[f, r : r + 1, :]
            for i, r in enumerate(IN_ROWS):
                band = drive[f, r // 16 * 16 : r // 16 * 16 + 16, :].astype(F32)
                rows[10 + i, f : f + 1] = band[r % 16 : r % 16 + 1]
            from_x = dot_nt(picks, x[f])
            from_drive = lax.dot_general(force_picks, drive[f], NT, preferred_element_type=F32)
            for i in range(8):
                cols[i, f : f + 1, 0:H] = from_x[i : i + 1]
            for i in range(4):
                cols[8 + i, f : f + 1, 0:H] = from_drive[i : i + 1]
            coefs = closed(params[f : f + 1, 0:W], params)
            get = between(north[0, f : f + 1, :], x.at[f], south[0, f : f + 1, :])
            for r in range(0, H, CHUNK):
                end = r + CHUNK
                y[f, r:end, :] = step_rows(get, r, coefs, drive[f, r:end, :].astype(F32))


def banks(params, x, drive, north, south):
    return pl.pallas_call(
        bank_kernel,
        in_specs=[VMEM] * 5,
        out_specs=[VMEM] * 3,
        out_shape=[
            pltpu.VMEM((14, V, W), F32),
            pltpu.VMEM((12, V, 256), F32),
            pltpu.VMEM((V, H, W), F32),
        ],
        compiler_params=SMALL,
        name="banks",
    )(*near(params, x, drive, north, south))


def pack_kernel(ends, from_one, from_two, one, two, north, south):
    section, row, column = position()

    def sort(up, down):
        north[...] = up[...]
        south[...] = down[...]

    def fill(to_west, to_east):
        for out, at, lo in ((to_west, 0, 0), (to_east, 3, W - 128)):
            out[0:3] = ends[at : at + 3]
            out[3, :, 0:128] = north[0, :, lo : lo + 128]
            out[3, :, 128:256] = north[1, :, lo : lo + 128]
            out[4, :, 0:128] = north[2, :, lo : lo + 128]
            out[4, :, 128:256] = south[2, :, lo : lo + 128]
            out[5, :, 0:128] = south[0, :, lo : lo + 128]
            out[5, :, 128:256] = south[1, :, lo : lo + 128]

    @pl.when(section == 0)
    def _():
        by_parity(row, lambda: sort(from_two, from_one), lambda: sort(from_one, from_two))
        by_parity(column, lambda: fill(two, one), lambda: fill(one, two))


def pack(ends, from_one, from_two):
    flank, row = pltpu.VMEM((6, V, 256), F32), pltpu.VMEM((3, V, W), F32)
    return pl.pallas_call(
        pack_kernel,
        in_specs=[VMEM] * 3,
        out_specs=[VMEM] * 4,
        out_shape=[flank, flank, row, row],
        compiler_params=SMALL,
        name="pack",
    )(*near(ends, from_one, from_two))


def rims_kernel(
    params, shape, rows, cols, ends, north, south, from_one, from_two, *out
):
    *out, beyond, west, east = out
    section, row, column = position()
    count, columns = shape

    def sort(left, right):
        west[...] = left[...]
        east[...] = right[...]

    @pl.when(section == 0)
    def _():
        by_parity(column, lambda: sort(from_two, from_one), lambda: sort(from_one, from_two))
        beyond[0:V] = west[0]
        beyond[V : 2 * V] = east[0]
        k = per_field(params, (V, 1), 0)
        a0, ae, aw, as_, an = weights_of(k, params)
        has_n = jnp.where(row > 0, 1.0, 0.0)
        has_s = jnp.where(row < count - 1, 1.0, 0.0)
        has_w = jnp.where(column > 0, 1.0, 0.0)
        has_e = jnp.where(column < columns - 1, 1.0, 0.0)
        lane128 = iota((V, 128), 1)
        lane256 = iota((V, 256), 1)
        wide = WIDE
        lane_wide = iota((V, wide), 1)
        keep = jnp.where(lane_wide < 128, has_w, jnp.where(lane_wide >= 128 + W, has_e, 1.0))
        near_w, near_e = west[0], east[0]

        def join(before, middle, after):
            return jnp.concatenate([before, middle, after], axis=1)

        def with_sides(middle, left, right):
            return join(
                jnp.where(lane128 == 127, left, 0.0), middle, jnp.where(lane128 == 0, right, 0.0)
            )

        def lanes(value, at):
            return value[:, at : at + 1]

        def halo_row(near, far, force, inner, a_far, a_inner, exists):
            value = (
                a0 * near
                + ae * pltpu.roll(near, wide - 1, 1)
                + aw * pltpu.roll(near, 1, 1)
                + a_far * far
                + a_inner * inner
                + force
            )
            return value * keep * exists

        north_1 = join(west[3, :, 0:128], north[0], east[3, :, 0:128])
        north_2 = join(west[3, :, 128:256], north[1], east[3, :, 128:256])
        north_f = join(west[4, :, 0:128], north[2], east[4, :, 0:128])
        south_1 = join(west[5, :, 0:128], south[0], east[5, :, 0:128])
        south_2 = join(west[5, :, 128:256], south[1], east[5, :, 128:256])
        south_f = join(west[4, :, 128:256], south[2], east[4, :, 128:256])
        top = with_sides(rows[0], lanes(near_w, 0), lanes(near_e, 0))
        bottom = with_sides(rows[9], lanes(near_w, H - 1), lanes(near_e, H - 1))
        new_north = halo_row(north_1, north_2, north_f, top, an, as_, has_n)
        new_south = halo_row(south_1, south_2, south_f, bottom, as_, an, has_s)

        def with_ends(column_values, before, after):
            return jnp.where(
                lane256 == 255, before, jnp.where(lane256 == H, after, column_values)
            )

        def halo_column(near, far, force, inner, a_far, a_inner, exists, at):
            full = with_ends(near, lanes(north_1, at), lanes(south_1, at))
            value = (
                a0 * full
                + as_ * pltpu.roll(full, 255, 1)
                + an * pltpu.roll(full, 1, 1)
                + a_far * far
                + a_inner * inner
                + force
            )
            new = with_ends(value * exists, lanes(new_north, at), lanes(new_south, at))
            return full, new

        at_w, at_e = 127, 128 + W
        old_west, new_west = halo_column(near_w, west[1], west[2], ends[0], aw, ae, has_w, at_w)
        old_east, new_east = halo_column(near_e, east[1], east[2], ends[3], ae, aw, has_e, at_e)

        bank = {(0, 0): north_1, (1, 0): new_north, (0, 5): south_1, (1, 5): new_south}
        side = {(0, 0): old_west, (1, 0): new_west, (0, 5): old_east, (1, 5): new_east}
        blank = jnp.zeros((V, 128), F32)
        for i, r in enumerate(IN_ROWS):
            place, at = (1, 3, 2, 4)[i], 1 + BANK_ROWS.index(r)
            old = with_sides(rows[at], lanes(near_w, r), lanes(near_e, r))
            bank[0, place] = old
            new = (
                a0 * old
                + ae * pltpu.roll(old, wide - 1, 1)
                + aw * pltpu.roll(old, 1, 1)
                + join(blank, an * rows[at - 1] + as_ * rows[at + 1] + rows[10 + i], blank)
            )
            bank[1, place] = jnp.where(
                lane_wide == 127,
                lanes(new_west, r),
                jnp.where(lane_wide == 128 + W, lanes(new_east, r), new),
            )
        for i, c in enumerate(IN_COLS):
            place, at = (1, 3, 2, 4)[i], BANK_COLS.index(c)
            old, new = halo_column(
                cols[at], cols[at - 1], cols[8 + i], cols[at + 1], aw, ae, 1.0, 128 + c
            )
            side[0, place] = old
            side[1, place] = new

        def choose(which, candidates):
            return jnp.where(
                which == 0.0, candidates[0], jnp.where(which == 1.0, candidates[1], candidates[2])
            )

        for member in range(3):
            at = PATCH_ROW + member
            patch_row = params[at : at + 1, :]
            at = PATCH_COL + member
            patch_col = params[at : at + 1, :]
            for time in range(2):
                for half in range(2):
                    line = choose(patch_row, [bank[time, 3 * half + i] for i in range(3)])
                    rim = choose(
                        patch_col[:, 0:W], [line[:, i * PW : i * PW + W] for i in range(3)]
                    )
                    rim = pltpu.roll(rim, W - 127, 1)[:, 0:256]
                    flank = choose(
                        patch_col[:, 0:256], [side[time, 3 * half + i] for i in range(3)]
                    )
                    flank = choose(
                        patch_row[:, 0:256],
                        [pltpu.roll(flank, OFF + 1 - PH * i, 1) for i in range(3)],
                    )
                    flank = jnp.where((lane256 >= OFF) & (lane256 < OFF + PH + 2), flank, 0.0)
                    place = (2 * time + half) * V
                    out[member][place : place + V, :] = jnp.where(lane256 < PW + 2, rim, flank)


def rims(shape, *arrays):
    def kernel(params, *refs):
        rims_kernel(params, shape, *refs)

    return pl.pallas_call(
        kernel,
        in_specs=[VMEM] * 8,
        out_specs=[VMEM] * 4,
        out_shape=[pltpu.VMEM((4 * V, 256), F32)] * 3 + [pltpu.VMEM((2 * V, 256), F32)],
        scratch_shapes=[pltpu.VMEM((6, V, 256), F32)] * 2,
        compiler_params=SMALL,
        name="rims",
    )(*near(*arrays))


def edge_effect(old, new, params, tent_row, tent_col):
    n = old.shape[0]
    k_row = 3.0 * per_field(params, (n, 1), 0)
    a0_row, ae, aw, as_, an = weights_of(k_row, params)
    upper = (iota((n, 1), 0) & V) == 0
    outer, inner = jnp.where(upper, an, as_), jnp.where(upper, as_, an)
    lane = iota((n, W), 1)
    east = jnp.where(lane == W - 1, 0.0, ae)
    west = jnp.where(lane == 0, 0.0, aw)

    def along_row(v):
        return a0_row * v + east * pltpu.roll(v, W - 1, 1) + west * pltpu.roll(v, 1, 1)

    row_effect = depths(
        dot_right(old, tent_row) * (1.0 / 3.0), dot_right(new, tent_row) * (1.0 / 3.0), outer, inner, along_row
    )

    if n == 2 * V:
        old, new, n = jnp.concatenate([old] * 3, axis=0), jnp.concatenate([new] * 3, axis=0), 3 * n
    k_col = 3.0 * per_field(params, (1, n), 1)
    a0_col, ae, aw, as_, an = weights_of(k_col, params)
    left = (iota((1, n), 1) & V) == 0
    outer, inner = jnp.where(left, aw, ae), jnp.where(left, ae, aw)
    down = iota((H, n), 0)
    south = jnp.where(down == H - 1, 0.0, as_)
    north = jnp.where(down == 0, 0.0, an)

    def along_column(v):
        return a0_col * v + south * pltpu.roll(v, H - 1, 0) + north * pltpu.roll(v, 1, 0)

    col_effect = depths(
        dot_nt(tent_col, old) * (1.0 / 3.0), dot_nt(tent_col, new) * (1.0 / 3.0), outer, inner, along_column
    )
    return row_effect, col_effect


def depths(old, new, outer, inner, along):
    third = (new - old) * (1.0 / 3.0)
    first_0 = outer * old
    second_0 = along(first_0) + outer * (old + third)
    second_1 = outer * first_0
    third_0 = along(second_0) + inner * second_1 + outer * (old + 2.0 * third)
    third_1 = along(second_1) + outer * second_0
    third_2 = outer * second_1
    return third_0, third_1, third_2


def spread(values, first=0):
    shape = (values.shape[1], 2 * V * 128)
    index, lane = iota(shape, 0) - first, iota(shape, 1)
    block, depth = index & (2 * V - 1), index >> 3
    target = block * 128 + jnp.where(block < V, depth, 127 - depth)
    valid = (index >= 0) & (depth < 3)
    return dot_right(values, jnp.where((lane == target) & valid, 1.0, 0.0).astype(BF16))


def last_kernel(
    nest_patch, params, stepped, y, tent_row, tent_col, beyond,
    sent_0, sent_1, sent_2, got_0, got_1, got_2, mean_0, mean_1, mean_2, out, tile, entries, sems,
):
    section, row, column = position()
    count = nest_patch.shape[0]
    parent = section == 0
    sent, got, means = (sent_0, sent_1, sent_2), (got_0, got_1, got_2), (mean_0, mean_1, mean_2)
    n = 2 * V

    def send(f):
        return pltpu.make_async_copy(tile.at[f], out.at[f], sems.at[f])

    def with_sides(base, f, both):
        left, right = f * 128, (V + f) * 128
        tile[f, :, 0:128] = base[f, :, 0:128] + both[:, left : left + 128]
        tile[f, :, 128 : W - 128] = base[f, :, 128 : W - 128]
        tile[f, :, W - 128 : W] = base[f, :, W - 128 : W] + both[:, right : right + 128]

    @pl.when(parent)
    def _():
        fetch = pltpu.make_async_copy(nest_patch, entries, sems.at[V])
        fetch.start()
        _, ae, aw, _, _ = weights_of(per_field(params, (1, n), 1), params)
        eye = jnp.where(iota((H, H), 0) == iota((H, H), 1), 1.0, 0.0).astype(BF16)
        outer = jnp.where(iota((1, n), 1) < V, aw, ae)
        both = spread(dot_nt(eye, beyond[:, 0:H]) * outer)
        for f in range(V):
            with_sides(stepped, f, both)
        old = jnp.concatenate([s[0:n, :] for s in sent], axis=0)
        new = jnp.concatenate([s[n : 2 * n, :] for s in sent], axis=0)
        row_effect, col_effect = edge_effect(old, new, params, row_tent(), col_tent())
        by_row = dot_right(sum(row_effect), mean_matrix()) * (1.0 / 9.0)
        thirds = iota((PH, H), 1) - 3 * iota((PH, H), 0)
        thirds = jnp.where((thirds >= 0) & (thirds <= 2), 1.0, 0.0).astype(BF16)
        by_col = dot_left(thirds, sum(col_effect)) * (1.0 / 9.0)
        line = iota((PH, PW), 0)
        fetch.wait()
        for member in range(3):
            nest = row + member - 1
            entry = role_entry(entries, row, column, member, count)
            slot = lax.rem(entry, 9)

            @pl.when((nest >= 0) & (nest < count) & (lax.div(entry, 9) == row))
            def _(member=member, slot=slot):
                at_row = pl.multiple_of(lax.div(slot, 3) * PH, PH)
                at_col = pl.multiple_of(lax.rem(slot, 3) * PW, PW)
                mine = (iota(by_col.shape, 1) >> 3) == member
                beside = spread(jnp.where(mine, by_col, 0.0), member * n)
                for f in range(V):
                    left, right, up = f * 128, (V + f) * 128, member * n + f
                    tile[f, pl.ds(at_row, PH), pl.ds(at_col, PW)] = (
                        means[member][f]
                        + jnp.where(line == 0, by_row[up : up + 1], 0.0)
                        + jnp.where(line == PH - 1, by_row[up + V : up + V + 1], 0.0)
                        + beside[:, left : left + 128]
                        + beside[:, right : right + 128]
                    )

        for f in range(V):
            send(f).start()

    @pl.when(jnp.logical_not(parent))
    def _():
        member = params[MEMBER : MEMBER + 1, 0:256]
        u = jnp.where(
            member == 0.0, got[0][...], jnp.where(member == 1.0, got[1][...], got[2][...])
        )
        row_effect, col_effect = edge_effect(
            u[0:n], u[n : 2 * n], params, tent_row[...], tent_col[...]
        )
        depth = iota(col_effect[0].shape, 1) >> 3
        both = spread(
            jnp.where(
                depth == 0, col_effect[0], jnp.where(depth == 1, col_effect[1], col_effect[2])
            )
        )
        for f in range(V):
            with_sides(y, f, both)
            for depth in range(3):
                bottom = H - 1 - depth
                tile[f, depth : depth + 1, :] = (
                    tile[f, depth : depth + 1, :] + row_effect[depth][f : f + 1]
                )
                tile[f, bottom : bottom + 1, :] = (
                    tile[f, bottom : bottom + 1, :] + row_effect[depth][V + f : V + f + 1]
                )
            send(f).start()

    for f in range(V):
        send(f).wait()


def last(nest_patch, *arrays):
    return pl.pallas_call(
        last_kernel,
        in_specs=[ANY] + [VMEM] * 15,
        out_specs=ANY,
        out_shape=jax.ShapeDtypeStruct((V, H, W), F32),
        scratch_shapes=[
            pltpu.VMEM((V, H, W), F32),
            pltpu.SMEM(nest_patch.shape, jnp.int32),
            pltpu.SemaphoreType.DMA((V + 1,)),
        ],
        compiler_params=SMALL,
        name="last",
    )(*far(nest_patch), *near(*arrays))


def routes(sizes, source, move):
    _, n_rows, n_cols = sizes
    out = []
    for r in range(n_rows):
        for c in range(n_cols):
            to_sec, to_r, to_c = move(r, c)
            if 0 <= to_r < n_rows and 0 <= to_c < n_cols:
                out.append(
                    (
                        (source * n_rows + r) * n_cols + c,
                        (to_sec * n_rows + to_r) * n_cols + to_c,
                    )
                )
    return out


def on_device(sizes, *arrays):
    return compute(sizes, *arrays)


def compute(sizes, fields, forcing, courant, diffusion, nest_patch):
    x = fields.reshape(V, H, W)
    drive = forcing.reshape(V, H, W)
    courant = courant.reshape(2)

    def shift(value, source, move):
        return lax.ppermute(value, AXES, routes(sizes, source, move))

    def partner(index, first):
        return index + 1 if index % 2 == first else index - 1

    rows_one, rows_two, params = edge(x, drive, courant, diffusion, nest_patch)
    rows_one = shift(rows_one, 0, lambda r, c: (0, partner(r, 0), c))
    rows_two = shift(rows_two, 0, lambda r, c: (0, partner(r, 1), c))
    y, mean, ends, *tents = nests(params, x, drive)
    means = [shift(mean, 1, lambda r, c, m=m: (0, r + 1 - m, c)) for m in range(3)]
    cols_one, cols_two, north, south = pack(ends, rows_one, rows_two)
    cols_one = shift(cols_one, 0, lambda r, c: (0, r, partner(c, 0)))
    cols_two = shift(cols_two, 0, lambda r, c: (0, r, partner(c, 1)))
    rows, cols, stepped = banks(params, x, drive, north, south)
    *sent, beyond = rims(
        sizes[1:], params, rows, cols, ends, north, south, cols_one, cols_two
    )
    got = [shift(sent[m], 0, lambda r, c, m=m: (1, r + m - 1, c)) for m in range(3)]
    out = last(
        nest_patch, params, stepped, y, *tents, beyond, *sent, *got, *means
    )
    return out.reshape(fields.shape)


def solution(mesh):
    sizes = tuple(mesh.shape[axis] for axis in AXES)
    spec = P("sec", None, None, "gy", "gx")
    return jax.shard_map(
        functools.partial(on_device, sizes),
        mesh=mesh,
        in_specs=(spec, spec, P(), P(), P()),
        out_specs=spec,
        check_vma=False,
    )
```

```python
import functools

import jax
import jax.numpy as jnp
from jax import lax
from jax.experimental import pallas as pl
from jax.experimental.pallas import tpu as pltpu
from jax.sharding import PartitionSpec as P


F32 = jnp.float32
BF16 = jnp.bfloat16
V, H, W = 4, 192, 384
PH, PW = H // 3, W // 3
CHUNK = 16
OFF = 160


def inner(n):
    lines = (n - 1, n, 2 * n - 1, 2 * n)
    return lines, (n - 2, n - 1, n, n + 1, 2 * n - 2, 2 * n - 1, 2 * n, 2 * n + 1)


IN_ROWS, BANK_ROWS = inner(PH)
IN_COLS, BANK_COLS = inner(PW)
WIDE = W + 256
COURANT, PATCH_ROW, PATCH_COL, MEMBER = V, V + 2, V + 5, V + 8
AXES = ("sec", "gy", "gx")
VMEM = pl.BlockSpec(memory_space=pltpu.VMEM)
ANY = pl.BlockSpec(memory_space=pl.ANY)
SMALL = pltpu.CompilerParams(vmem_limit_bytes=16 << 20)


def iota(shape, dim):
    return lax.broadcasted_iota(jnp.int32, shape, dim)


def split2(a):
    high = a.astype(BF16)
    return high, (a - high.astype(F32)).astype(BF16)


def dot_right(a, m):
    return sum(jnp.dot(part, m, preferred_element_type=F32) for part in split2(a))


def dot_nt(m, a):
    dims = (((1,), (1,)), ((), ()))
    return sum(lax.dot_general(m, part, dims, preferred_element_type=F32) for part in split2(a))


def dot_left(m, a):
    return sum(jnp.dot(m, part, preferred_element_type=F32) for part in split2(a))


def select_rows(picks, width):
    row, lane = iota((16, width), 0), iota((16, width), 1)
    wanted = jnp.full((16, width), -1, jnp.int32)
    for i, pick in enumerate(picks):
        wanted = jnp.where(row == i, pick, wanted)
    return jnp.where(lane == wanted, 1.0, 0.0).astype(BF16)


def weights(k, params):
    width = k.shape[1]
    half_x = 0.5 * params[COURANT : COURANT + 1, 0:width]
    half_y = 0.5 * params[COURANT + 1 : COURANT + 2, 0:width]
    return 1.0 - 4.0 * k, k - half_x, k + half_x, k - half_y, k + half_y


def per_field(params, shape, dim):
    index = iota(shape, dim) & (V - 1)
    out = jnp.broadcast_to(params[0:1, 0:1], shape)
    for f in range(1, V):
        out = jnp.where(index == f, params[f : f + 1, 0:1], out)
    return out


def weights_of(k, params):
    half_x = 0.5 * params[COURANT : COURANT + 1, 0:1]
    half_y = 0.5 * params[COURANT + 1 : COURANT + 2, 0:1]
    return 1.0 - 4.0 * k, k - half_x, k + half_x, k - half_y, k + half_y


def closed(k, params):
    a0, east, west, south, north = weights(k, params)
    lane = iota((1, W), 1)
    return a0, jnp.where(lane == W - 1, 0.0, east), jnp.where(lane == 0, 0.0, west), south, north


def step_rows(get, r, coefs, force):
    a0, east, west, south, north = coefs
    centre = get(r)
    return (
        a0 * centre
        + east * pltpu.roll(centre, W - 1, 1)
        + west * pltpu.roll(centre, 1, 1)
        + south * get(r + 1)
        + north * get(r - 1)
        + force
    )


def padded(ref):
    return lambda r: ref[8 + r : 8 + r + CHUNK, :]


def between(before, ref, after):
    def get(r):
        if r < 0:
            return jnp.concatenate([before, ref[0 : CHUNK - 1, :]], axis=0)
        if r + CHUNK > H:
            return jnp.concatenate([ref[r:H, :], after], axis=0)
        return ref[r : r + CHUNK, :]

    return get


def near(*values):
    return [pltpu.with_memory_space_constraint(v, pltpu.VMEM) for v in values]


def far(*values):
    return [pltpu.with_memory_space_constraint(v, pltpu.HBM) for v in values]


def position():
    return [lax.axis_index(axis) for axis in AXES]


def by_parity(index, even, odd):
    pl.when(lax.rem(index, 2) == 0)(even)
    pl.when(lax.rem(index, 2) == 1)(odd)


def edge_kernel(
    x, drive, courant, diffusion, nest_patch, one, two, params,
    x_top, x_bottom, d_top, d_bottom, c_now, k_now, entries, sems,
):
    copies = [
        pltpu.make_async_copy(source, target, sems.at[i])
        for i, (source, target) in enumerate(
            (
                (x.at[:, 0:8, :], x_top),
                (x.at[:, H - 8 : H, :], x_bottom),
                (drive.at[:, 0:16, :], d_top),
                (drive.at[:, H - 16 : H, :], d_bottom),
                (courant, c_now),
                (diffusion, k_now),
                (nest_patch, entries),
            )
        )
    ]
    for copy in copies:
        copy.start()
    for copy in copies:
        copy.wait()
    _, row, column = position()

    def fill(down, up):
        for f in range(V):
            down[0, f : f + 1] = x_bottom[f, 7:8, :]
            down[1, f : f + 1] = x_bottom[f, 6:7, :]
            down[2, f : f + 1] = d_bottom[f].astype(F32)[15:16]
            up[0, f : f + 1] = x_top[f, 0:1, :]
            up[1, f : f + 1] = x_top[f, 1:2, :]
            up[2, f : f + 1] = d_top[f].astype(F32)[0:1]

    by_parity(row, lambda: fill(one, two), lambda: fill(two, one))

    def put(at, value):
        params[at : at + 1, :] = jnp.full((1, WIDE), value, F32)

    for f in range(V):
        put(f, k_now[f])
    put(COURANT, c_now[0])
    put(COURANT + 1, c_now[1])
    count = nest_patch.shape[0]
    for member in range(3):
        slot = lax.rem(role_entry(entries, row, column, member, count), 9)
        put(PATCH_ROW + member, lax.div(slot, 3).astype(F32))
        put(PATCH_COL + member, lax.rem(slot, 3).astype(F32))
    put(MEMBER, (row - lax.div(entries[row, column], 9) + 1).astype(F32))


def edge(x, drive, courant, diffusion, nest_patch):
    return pl.pallas_call(
        edge_kernel,
        in_specs=[ANY] * 5,
        out_specs=[VMEM] * 3,
        out_shape=[
            pltpu.VMEM((3, V, W), F32),
            pltpu.VMEM((3, V, W), F32),
            pltpu.VMEM((16, WIDE), F32),
        ],
        scratch_shapes=[
            pltpu.VMEM((V, 8, W), F32),
            pltpu.VMEM((V, 8, W), F32),
            pltpu.VMEM((V, 16, W), BF16),
            pltpu.VMEM((V, 16, W), BF16),
            pltpu.SMEM((2,), F32),
            pltpu.SMEM((V,), F32),
            pltpu.SMEM(nest_patch.shape, jnp.int32),
            pltpu.SemaphoreType.DMA((7,)),
        ],
        compiler_params=SMALL,
        name="edge",
    )(*far(x, drive, courant, diffusion, nest_patch))


def role_entry(entries, row, column, member, count):
    nest = jnp.clip(row + member - 1, 0, count - 1)
    return entries[nest, column]


NT = (((1,), (1,)), ((), ()))


def nests_kernel(
    params, x, drive, y, mean, ends, tent_row, tent_col, two, three, force, thirds
):
    parent = position()[0] == 0

    @pl.when(parent)
    def _():
        ends[...] = jnp.zeros(ends.shape, F32)
        none = -1
        x_west, x_east = select_rows((0, 1), 128), select_rows((none, none, none, 127, 126), 128)
        d_west = select_rows((none, none, 0), 128)
        d_east = select_rows((none, none, none, none, none, 127), 128)
        picks = jnp.concatenate([x_west, x_west, x_east, x_east, d_west, d_east], axis=1)
        for f in range(V):
            parts = (
                *split2(x[f, :, 0:128]),
                *split2(x[f, :, W - 128 : W]),
                drive[f, :, 0:128],
                drive[f, :, W - 128 : W],
            )
            values = lax.dot_general(
                picks, jnp.concatenate(parts, axis=1), NT, preferred_element_type=F32
            )
            for i in range(6):
                ends[i, f : f + 1, 0:H] = values[i : i + 1]

    @pl.when(jnp.logical_not(parent))
    def _():
        for buffer in (two, three):
            buffer[0:8, :] = jnp.zeros((8, W), F32)
            buffer[H + 8 : H + 16, :] = jnp.zeros((8, W), F32)
        blocks = mean_matrix()
        zero = jnp.zeros((1, W), F32)
        tent_row[...] = row_tent()
        tent_col[...] = col_tent()

        @pl.loop(0, V)
        def _(f):
            coefs = closed(3.0 * params[pl.ds(f, 1), :][:, 0:W], params)

            def step(get, new, at):
                for r in range(0, H, CHUNK):
                    new[at + r : at + r + CHUNK, :] = step_rows(
                        get, r, coefs, force[r : r + CHUNK, :]
                    )

            force[...] = drive[f].astype(F32) * (1.0 / 3.0)
            step(between(zero, x.at[f], zero), two, 8)
            step(padded(two), three, 8)
            step(padded(three), y.at[f], 0)
            thirds[...] = dot_right(y[f], blocks)
            total = (
                thirds[pl.ds(0, PH, stride=3), :]
                + thirds[pl.ds(1, PH, stride=3), :]
                + thirds[pl.ds(2, PH, stride=3), :]
            )
            mean[f] = total * (1.0 / 9.0)


def mean_matrix():
    gap = iota((W, PW), 0) - 3 * iota((W, PW), 1)
    return jnp.where((gap >= 0) & (gap <= 2), 1.0, 0.0).astype(BF16)


def row_tent():
    tent = jnp.maximum(3 - jnp.abs(iota((256, W), 1) - 3 * iota((256, W), 0) + 2), 0)
    return tent.astype(F32).astype(BF16)


def col_tent():
    tent = jnp.maximum(3 - jnp.abs(iota((H, 256), 0) - 3 * (iota((H, 256), 1) - OFF) + 2), 0)
    return tent.astype(F32).astype(BF16)


def nests(params, x, drive):
    return pl.pallas_call(
        nests_kernel,
        in_specs=[VMEM] * 3,
        out_specs=[VMEM] * 5,
        out_shape=[
            pltpu.VMEM((V, H, W), F32),
            pltpu.VMEM((V, PH, PW), F32),
            pltpu.VMEM((6, V, 256), F32),
            pltpu.VMEM((256, W), BF16),
            pltpu.VMEM((H, 256), BF16),
        ],
        scratch_shapes=[
            pltpu.VMEM((H + 16, W), F32),
            pltpu.VMEM((H + 16, W), F32),
            pltpu.VMEM((H, W), F32),
            pltpu.VMEM((H, PW), F32),
        ],
        compiler_params=SMALL,
        name="nests",
    )(*near(params, x, drive))


def bank_kernel(params, x, drive, north, south, rows, cols, y):
    @pl.when(position()[0] == 0)
    def _():
        cols[...] = jnp.zeros(cols.shape, F32)
        picks, force_picks = select_rows(BANK_COLS, W), select_rows(IN_COLS, W)
        for f in range(V):
            for i, r in enumerate((0, *BANK_ROWS, H - 1)):
                rows[i, f : f + 1] = x[f, r : r + 1, :]
            for i, r in enumerate(IN_ROWS):
                band = drive[f, r // 16 * 16 : r // 16 * 16 + 16, :].astype(F32)
                rows[10 + i, f : f + 1] = band[r % 16 : r % 16 + 1]
            from_x = dot_nt(picks, x[f])
            from_drive = lax.dot_general(force_picks, drive[f], NT, preferred_element_type=F32)
            for i in range(8):
                cols[i, f : f + 1, 0:H] = from_x[i : i + 1]
            for i in range(4):
                cols[8 + i, f : f + 1, 0:H] = from_drive[i : i + 1]
            coefs = closed(params[f : f + 1, 0:W], params)
            get = between(north[0, f : f + 1, :], x.at[f], south[0, f : f + 1, :])
            for r in range(0, H, CHUNK):
                end = r + CHUNK
                y[f, r:end, :] = step_rows(get, r, coefs, drive[f, r:end, :].astype(F32))


def banks(params, x, drive, north, south):
    return pl.pallas_call(
        bank_kernel,
        in_specs=[VMEM] * 5,
        out_specs=[VMEM] * 3,
        out_shape=[
            pltpu.VMEM((14, V, W), F32),
            pltpu.VMEM((12, V, 256), F32),
            pltpu.VMEM((V, H, W), F32),
        ],
        compiler_params=SMALL,
        name="banks",
    )(*near(params, x, drive, north, south))


def pack_kernel(ends, from_one, from_two, one, two, north, south):
    section, row, column = position()

    def sort(up, down):
        north[...] = up[...]
        south[...] = down[...]

    lane = iota((V, 128), 1)

    def fill(to_west, to_east):
        for i in range(3):
            to_west[i, :, 0:128] = ends[i, :, 0:128]
            above = pltpu.roll(north[i, :, 0:128], H - 128, 1)
            below = pltpu.roll(south[i, :, 0:128], H - 126, 1)
            to_west[i, :, 128:256] = jnp.where(
                lane < H - 128, ends[i, :, 128:256], jnp.where(lane < H - 126, above, below)
            )
            to_east[i, :, 0:128] = ends[3 + i, :, 0:128]
            above = north[i, :, W - 128 : W]
            below = pltpu.roll(south[i, :, W - 128 : W], 126, 1)
            to_east[i, :, 128:256] = jnp.where(
                lane < H - 128, ends[3 + i, :, 128:256], jnp.where(lane >= 126, above, below)
            )

    @pl.when(section == 0)
    def _():
        by_parity(row, lambda: sort(from_two, from_one), lambda: sort(from_one, from_two))
        by_parity(column, lambda: fill(two, one), lambda: fill(one, two))


def pack(ends, from_one, from_two):
    flank, row = pltpu.VMEM((3, V, 256), F32), pltpu.VMEM((3, V, W), F32)
    return pl.pallas_call(
        pack_kernel,
        in_specs=[VMEM] * 3,
        out_specs=[VMEM] * 4,
        out_shape=[flank, flank, row, row],
        compiler_params=SMALL,
        name="pack",
    )(*near(ends, from_one, from_two))


def rims_kernel(
    params, shape, rows, cols, ends, north, south, from_one, from_two, *out
):
    *out, beyond, west, east = out
    section, row, column = position()
    count, columns = shape

    def sort(left, right):
        west[...] = left[...]
        east[...] = right[...]

    @pl.when(section == 0)
    def _():
        by_parity(column, lambda: sort(from_two, from_one), lambda: sort(from_one, from_two))
        beyond[0:V] = west[0]
        beyond[V : 2 * V] = east[0]
        k = per_field(params, (V, 1), 0)
        a0, ae, aw, as_, an = weights_of(k, params)
        has_n = jnp.where(row > 0, 1.0, 0.0)
        has_s = jnp.where(row < count - 1, 1.0, 0.0)
        has_w = jnp.where(column > 0, 1.0, 0.0)
        has_e = jnp.where(column < columns - 1, 1.0, 0.0)
        lane128 = iota((V, 128), 1)
        lane256 = iota((V, 256), 1)
        wide = WIDE
        lane_wide = iota((V, wide), 1)
        keep = jnp.where(lane_wide < 128, has_w, jnp.where(lane_wide >= 128 + W, has_e, 1.0))
        near_w, near_e = west[0], east[0]

        def join(before, middle, after):
            return jnp.concatenate([before, middle, after], axis=1)

        def with_sides(middle, left, right):
            return join(
                jnp.where(lane128 == 127, left, 0.0), middle, jnp.where(lane128 == 0, right, 0.0)
            )

        def lanes(value, at):
            return value[:, at : at + 1]

        def halo_row(near, far, force, inner, a_far, a_inner, exists):
            value = (
                a0 * near
                + ae * pltpu.roll(near, wide - 1, 1)
                + aw * pltpu.roll(near, 1, 1)
                + a_far * far
                + a_inner * inner
                + force
            )
            return value * keep * exists

        def beyond_rows(values, to_west, to_east):
            out = []
            for i in range(3):
                before = pltpu.roll(west[i, :, 128:256], to_west, 1)
                after = pltpu.roll(east[i, :, 128:256], to_east, 1)
                out.append(join(before, values[i], after))
            return out

        north_1, north_2, north_f = beyond_rows(north, 0, 256 - H)
        south_1, south_2, south_f = beyond_rows(south, 2, 254 - H)
        top = with_sides(rows[0], lanes(near_w, 0), lanes(near_e, 0))
        bottom = with_sides(rows[9], lanes(near_w, H - 1), lanes(near_e, H - 1))
        new_north = halo_row(north_1, north_2, north_f, top, an, as_, has_n)
        new_south = halo_row(south_1, south_2, south_f, bottom, as_, an, has_s)

        def with_ends(column_values, before, after):
            return jnp.where(
                lane256 == 255, before, jnp.where(lane256 == H, after, column_values)
            )

        def halo_column(near, far, force, inner, a_far, a_inner, exists, at):
            full = with_ends(near, lanes(north_1, at), lanes(south_1, at))
            value = (
                a0 * full
                + as_ * pltpu.roll(full, 255, 1)
                + an * pltpu.roll(full, 1, 1)
                + a_far * far
                + a_inner * inner
                + force
            )
            new = with_ends(value * exists, lanes(new_north, at), lanes(new_south, at))
            return full, new

        at_w, at_e = 127, 128 + W
        old_west, new_west = halo_column(near_w, west[1], west[2], ends[0], aw, ae, has_w, at_w)
        old_east, new_east = halo_column(near_e, east[1], east[2], ends[3], ae, aw, has_e, at_e)

        bank = {(0, 0): north_1, (1, 0): new_north, (0, 5): south_1, (1, 5): new_south}
        side = {(0, 0): old_west, (1, 0): new_west, (0, 5): old_east, (1, 5): new_east}
        blank = jnp.zeros((V, 128), F32)
        for i, r in enumerate(IN_ROWS):
            place, at = (1, 3, 2, 4)[i], 1 + BANK_ROWS.index(r)
            old = with_sides(rows[at], lanes(near_w, r), lanes(near_e, r))
            bank[0, place] = old
            new = (
                a0 * old
                + ae * pltpu.roll(old, wide - 1, 1)
                + aw * pltpu.roll(old, 1, 1)
                + join(blank, an * rows[at - 1] + as_ * rows[at + 1] + rows[10 + i], blank)
            )
            bank[1, place] = jnp.where(
                lane_wide == 127,
                lanes(new_west, r),
                jnp.where(lane_wide == 128 + W, lanes(new_east, r), new),
            )
        for i, c in enumerate(IN_COLS):
            place, at = (1, 3, 2, 4)[i], BANK_COLS.index(c)
            old, new = halo_column(
                cols[at], cols[at - 1], cols[8 + i], cols[at + 1], aw, ae, 1.0, 128 + c
            )
            side[0, place] = old
            side[1, place] = new

        def choose(which, candidates):
            return jnp.where(
                which == 0.0, candidates[0], jnp.where(which == 1.0, candidates[1], candidates[2])
            )

        for member in range(3):
            at = PATCH_ROW + member
            patch_row = params[at : at + 1, :]
            at = PATCH_COL + member
            patch_col = params[at : at + 1, :]
            for time in range(2):
                for half in range(2):
                    line = choose(patch_row, [bank[time, 3 * half + i] for i in range(3)])
                    rim = choose(
                        patch_col[:, 0:W], [line[:, i * PW : i * PW + W] for i in range(3)]
                    )
                    rim = pltpu.roll(rim, W - 127, 1)[:, 0:256]
                    flank = choose(
                        patch_col[:, 0:256], [side[time, 3 * half + i] for i in range(3)]
                    )
                    flank = choose(
                        patch_row[:, 0:256],
                        [pltpu.roll(flank, OFF + 1 - PH * i, 1) for i in range(3)],
                    )
                    flank = jnp.where((lane256 >= OFF) & (lane256 < OFF + PH + 2), flank, 0.0)
                    place = (2 * time + half) * V
                    out[member][place : place + V, :] = jnp.where(lane256 < PW + 2, rim, flank)


def rims(shape, *arrays):
    def kernel(params, *refs):
        rims_kernel(params, shape, *refs)

    return pl.pallas_call(
        kernel,
        in_specs=[VMEM] * 8,
        out_specs=[VMEM] * 4,
        out_shape=[pltpu.VMEM((4 * V, 256), F32)] * 3 + [pltpu.VMEM((2 * V, 256), F32)],
        scratch_shapes=[pltpu.VMEM((3, V, 256), F32)] * 2,
        compiler_params=SMALL,
        name="rims",
    )(*near(*arrays))


def edge_effect(old, new, params, tent_row, tent_col):
    n = old.shape[0]
    k_row = 3.0 * per_field(params, (n, 1), 0)
    a0_row, ae, aw, as_, an = weights_of(k_row, params)
    upper = (iota((n, 1), 0) & V) == 0
    outer, inner = jnp.where(upper, an, as_), jnp.where(upper, as_, an)
    lane = iota((n, W), 1)
    east = jnp.where(lane == W - 1, 0.0, ae)
    west = jnp.where(lane == 0, 0.0, aw)

    def along_row(v):
        return a0_row * v + east * pltpu.roll(v, W - 1, 1) + west * pltpu.roll(v, 1, 1)

    row_effect = depths(
        dot_right(old, tent_row) * (1.0 / 3.0), dot_right(new, tent_row) * (1.0 / 3.0), outer, inner, along_row
    )

    if n == 2 * V:
        old, new, n = jnp.concatenate([old] * 3, axis=0), jnp.concatenate([new] * 3, axis=0), 3 * n
    k_col = 3.0 * per_field(params, (1, n), 1)
    a0_col, ae, aw, as_, an = weights_of(k_col, params)
    left = (iota((1, n), 1) & V) == 0
    outer, inner = jnp.where(left, aw, ae), jnp.where(left, ae, aw)
    down = iota((H, n), 0)
    south = jnp.where(down == H - 1, 0.0, as_)
    north = jnp.where(down == 0, 0.0, an)

    def along_column(v):
        return a0_col * v + south * pltpu.roll(v, H - 1, 0) + north * pltpu.roll(v, 1, 0)

    col_effect = depths(
        dot_nt(tent_col, old) * (1.0 / 3.0), dot_nt(tent_col, new) * (1.0 / 3.0), outer, inner, along_column
    )
    return row_effect, col_effect


def depths(old, new, outer, inner, along):
    third = (new - old) * (1.0 / 3.0)
    first_0 = outer * old
    second_0 = along(first_0) + outer * (old + third)
    second_1 = outer * first_0
    third_0 = along(second_0) + inner * second_1 + outer * (old + 2.0 * third)
    third_1 = along(second_1) + outer * second_0
    third_2 = outer * second_1
    return third_0, third_1, third_2


def spread(values, first=0):
    shape = (values.shape[1], 2 * V * 128)
    index, lane = iota(shape, 0) - first, iota(shape, 1)
    block, depth = index & (2 * V - 1), index >> 3
    target = block * 128 + jnp.where(block < V, depth, 127 - depth)
    valid = (index >= 0) & (depth < 3)
    return dot_right(values, jnp.where((lane == target) & valid, 1.0, 0.0).astype(BF16))


def last_kernel(
    nest_patch, params, stepped, y, tent_row, tent_col, beyond,
    sent_0, sent_1, sent_2, got_0, got_1, got_2, mean_0, mean_1, mean_2, out, tile, entries, sems,
):
    section, row, column = position()
    count = nest_patch.shape[0]
    parent = section == 0
    sent, got, means = (sent_0, sent_1, sent_2), (got_0, got_1, got_2), (mean_0, mean_1, mean_2)
    n = 2 * V

    def send(f):
        return pltpu.make_async_copy(tile.at[f], out.at[f], sems.at[f])

    def with_sides(base, f, both):
        left, right = f * 128, (V + f) * 128
        tile[f, :, 0:128] = base[f, :, 0:128] + both[:, left : left + 128]
        tile[f, :, 128 : W - 128] = base[f, :, 128 : W - 128]
        tile[f, :, W - 128 : W] = base[f, :, W - 128 : W] + both[:, right : right + 128]

    @pl.when(parent)
    def _():
        fetch = pltpu.make_async_copy(nest_patch, entries, sems.at[V])
        fetch.start()
        _, ae, aw, _, _ = weights_of(per_field(params, (1, n), 1), params)
        eye = jnp.where(iota((H, H), 0) == iota((H, H), 1), 1.0, 0.0).astype(BF16)
        outer = jnp.where(iota((1, n), 1) < V, aw, ae)
        both = spread(dot_nt(eye, beyond[:, 0:H]) * outer)
        old = jnp.concatenate([s[0:n, :] for s in sent], axis=0)
        new = jnp.concatenate([s[n : 2 * n, :] for s in sent], axis=0)
        row_effect, col_effect = edge_effect(old, new, params, row_tent(), col_tent())
        by_row = dot_right(sum(row_effect), mean_matrix()) * (1.0 / 9.0)
        thirds = iota((PH, H), 1) - 3 * iota((PH, H), 0)
        thirds = jnp.where((thirds >= 0) & (thirds <= 2), 1.0, 0.0).astype(BF16)
        by_col = dot_left(thirds, sum(col_effect)) * (1.0 / 9.0)
        line = iota((PH, PW), 0)
        fetch.wait()
        patches = []
        for member in range(3):
            nest = row + member - 1
            entry = role_entry(entries, row, column, member, count)
            slot = lax.rem(entry, 9)
            mine = (iota(by_col.shape, 1) >> 3) == member
            patches.append(
                (
                    (nest >= 0) & (nest < count) & (lax.div(entry, 9) == row),
                    pl.multiple_of(lax.div(slot, 3) * PH, PH),
                    pl.multiple_of(lax.rem(slot, 3) * PW, PW),
                    spread(jnp.where(mine, by_col, 0.0), member * n),
                )
            )
        for f in range(V):
            with_sides(stepped, f, both)
            for member, (valid, at_row, at_col, beside) in enumerate(patches):
                left, right, up = f * 128, (V + f) * 128, member * n + f
                patch = (
                    means[member][f]
                    + jnp.where(line == 0, by_row[up : up + 1], 0.0)
                    + jnp.where(line == PH - 1, by_row[up + V : up + V + 1], 0.0)
                    + beside[:, left : left + 128]
                    + beside[:, right : right + 128]
                )

                @pl.when(valid)
                def _(at_row=at_row, at_col=at_col, patch=patch):
                    tile[f, pl.ds(at_row, PH), pl.ds(at_col, PW)] = patch

            send(f).start()

    @pl.when(jnp.logical_not(parent))
    def _():
        member = params[MEMBER : MEMBER + 1, 0:256]
        u = jnp.where(
            member == 0.0, got[0][...], jnp.where(member == 1.0, got[1][...], got[2][...])
        )
        row_effect, col_effect = edge_effect(
            u[0:n], u[n : 2 * n], params, tent_row[...], tent_col[...]
        )
        depth = iota(col_effect[0].shape, 1) >> 3
        both = spread(
            jnp.where(
                depth == 0, col_effect[0], jnp.where(depth == 1, col_effect[1], col_effect[2])
            )
        )
        for f in range(V):
            with_sides(y, f, both)
            for depth in range(3):
                bottom = H - 1 - depth
                tile[f, depth : depth + 1, :] = (
                    tile[f, depth : depth + 1, :] + row_effect[depth][f : f + 1]
                )
                tile[f, bottom : bottom + 1, :] = (
                    tile[f, bottom : bottom + 1, :] + row_effect[depth][V + f : V + f + 1]
                )
            send(f).start()

    for f in range(V):
        send(f).wait()


def last(nest_patch, *arrays):
    return pl.pallas_call(
        last_kernel,
        in_specs=[ANY] + [VMEM] * 15,
        out_specs=ANY,
        out_shape=jax.ShapeDtypeStruct((V, H, W), F32),
        scratch_shapes=[
            pltpu.VMEM((V, H, W), F32),
            pltpu.SMEM(nest_patch.shape, jnp.int32),
            pltpu.SemaphoreType.DMA((V + 1,)),
        ],
        compiler_params=SMALL,
        name="last",
    )(*far(nest_patch), *near(*arrays))


def routes(sizes, source, move):
    _, n_rows, n_cols = sizes
    out = []
    for r in range(n_rows):
        for c in range(n_cols):
            to_sec, to_r, to_c = move(r, c)
            if 0 <= to_r < n_rows and 0 <= to_c < n_cols:
                out.append(
                    (
                        (source * n_rows + r) * n_cols + c,
                        (to_sec * n_rows + to_r) * n_cols + to_c,
                    )
                )
    return out


def on_device(sizes, *arrays):
    return compute(sizes, *arrays)


def compute(sizes, fields, forcing, courant, diffusion, nest_patch):
    x = fields.reshape(V, H, W)
    drive = forcing.reshape(V, H, W)
    courant = courant.reshape(2)

    def shift(value, source, move):
        return lax.ppermute(value, AXES, routes(sizes, source, move))

    def partner(index, first):
        return index + 1 if index % 2 == first else index - 1

    rows_one, rows_two, params = edge(x, drive, courant, diffusion, nest_patch)
    rows_one = shift(rows_one, 0, lambda r, c: (0, partner(r, 0), c))
    rows_two = shift(rows_two, 0, lambda r, c: (0, partner(r, 1), c))
    y, mean, ends, *tents = nests(params, x, drive)
    means = [shift(mean, 1, lambda r, c, m=m: (0, r + 1 - m, c)) for m in range(3)]
    cols_one, cols_two, north, south = pack(ends, rows_one, rows_two)
    cols_one = shift(cols_one, 0, lambda r, c: (0, r, partner(c, 0)))
    cols_two = shift(cols_two, 0, lambda r, c: (0, r, partner(c, 1)))
    rows, cols, stepped = banks(params, x, drive, north, south)
    *sent, beyond = rims(
        sizes[1:], params, rows, cols, ends, north, south, cols_one, cols_two
    )
    got = [shift(sent[m], 0, lambda r, c, m=m: (1, r + m - 1, c)) for m in range(3)]
    out = last(
        nest_patch, params, stepped, y, *tents, beyond, *sent, *got, *means
    )
    return out.reshape(fields.shape)


def solution(mesh):
    sizes = tuple(mesh.shape[axis] for axis in AXES)
    spec = P("sec", None, None, "gy", "gx")
    return jax.shard_map(
        functools.partial(on_device, sizes),
        mesh=mesh,
        in_specs=(spec, spec, P(), P(), P()),
        out_specs=spec,
        check_vma=False,
    )
```

```python
import functools

import jax
import jax.numpy as jnp
from jax import lax
from jax.experimental import pallas as pl
from jax.experimental.pallas import tpu as pltpu
from jax.sharding import PartitionSpec as P


F32 = jnp.float32
BF16 = jnp.bfloat16
V, H, W = 4, 192, 384
PH, PW = H // 3, W // 3
CHUNK = 16
OFF = 160


def inner(n):
    lines = (n - 1, n, 2 * n - 1, 2 * n)
    return lines, (n - 2, n - 1, n, n + 1, 2 * n - 2, 2 * n - 1, 2 * n, 2 * n + 1)


IN_ROWS, BANK_ROWS = inner(PH)
IN_COLS, BANK_COLS = inner(PW)
WIDE = W + 256
COURANT, PATCH_ROW, PATCH_COL, MEMBER = V, V + 2, V + 5, V + 8
AXES = ("sec", "gy", "gx")
VMEM = pl.BlockSpec(memory_space=pltpu.VMEM)
ANY = pl.BlockSpec(memory_space=pl.ANY)
SMALL = pltpu.CompilerParams(vmem_limit_bytes=16 << 20)


def iota(shape, dim):
    return lax.broadcasted_iota(jnp.int32, shape, dim)


def split2(a):
    high = a.astype(BF16)
    return high, (a - high.astype(F32)).astype(BF16)


def dot_right(a, m):
    return sum(jnp.dot(part, m, preferred_element_type=F32) for part in split2(a))


def dot_nt(m, a):
    dims = (((1,), (1,)), ((), ()))
    return sum(lax.dot_general(m, part, dims, preferred_element_type=F32) for part in split2(a))


def dot_left(m, a):
    return sum(jnp.dot(m, part, preferred_element_type=F32) for part in split2(a))


def select_rows(picks, width):
    row, lane = iota((16, width), 0), iota((16, width), 1)
    wanted = jnp.full((16, width), -1, jnp.int32)
    for i, pick in enumerate(picks):
        wanted = jnp.where(row == i, pick, wanted)
    return jnp.where(lane == wanted, 1.0, 0.0).astype(BF16)


def weights(k, params):
    width = k.shape[1]
    half_x = 0.5 * params[COURANT : COURANT + 1, 0:width]
    half_y = 0.5 * params[COURANT + 1 : COURANT + 2, 0:width]
    return 1.0 - 4.0 * k, k - half_x, k + half_x, k - half_y, k + half_y


def per_field(params, shape, dim):
    index = iota(shape, dim) & (V - 1)
    out = jnp.broadcast_to(params[0:1, 0:1], shape)
    for f in range(1, V):
        out = jnp.where(index == f, params[f : f + 1, 0:1], out)
    return out


def weights_of(k, params):
    half_x = 0.5 * params[COURANT : COURANT + 1, 0:1]
    half_y = 0.5 * params[COURANT + 1 : COURANT + 2, 0:1]
    return 1.0 - 4.0 * k, k - half_x, k + half_x, k - half_y, k + half_y


def closed(k, params):
    a0, east, west, south, north = weights(k, params)
    lane = iota((1, W), 1)
    return a0, jnp.where(lane == W - 1, 0.0, east), jnp.where(lane == 0, 0.0, west), south, north


def step_rows(get, r, coefs, force):
    a0, east, west, south, north = coefs
    centre = get(r)
    return (
        a0 * centre
        + east * pltpu.roll(centre, W - 1, 1)
        + west * pltpu.roll(centre, 1, 1)
        + south * get(r + 1)
        + north * get(r - 1)
        + force
    )


def padded(ref):
    return lambda r: ref[8 + r : 8 + r + CHUNK, :]


def between(before, ref, after):
    def get(r):
        if r < 0:
            return jnp.concatenate([before, ref[0 : CHUNK - 1, :]], axis=0)
        if r + CHUNK > H:
            return jnp.concatenate([ref[r:H, :], after], axis=0)
        return ref[r : r + CHUNK, :]

    return get


def near(*values):
    return [pltpu.with_memory_space_constraint(v, pltpu.VMEM) for v in values]


def far(*values):
    return [pltpu.with_memory_space_constraint(v, pltpu.HBM) for v in values]


def position():
    return [lax.axis_index(axis) for axis in AXES]


def by_parity(index, even, odd):
    pl.when(lax.rem(index, 2) == 0)(even)
    pl.when(lax.rem(index, 2) == 1)(odd)


def edge_kernel(
    x, drive, courant, diffusion, nest_patch, one, two, params,
    x_top, x_bottom, d_top, d_bottom, c_now, k_now, entries, sems,
):
    copies = [
        pltpu.make_async_copy(source, target, sems.at[i])
        for i, (source, target) in enumerate(
            (
                (x.at[:, 0:8, :], x_top),
                (x.at[:, H - 8 : H, :], x_bottom),
                (drive.at[:, 0:16, :], d_top),
                (drive.at[:, H - 16 : H, :], d_bottom),
                (courant, c_now),
                (diffusion, k_now),
                (nest_patch, entries),
            )
        )
    ]
    for copy in copies:
        copy.start()
    for copy in copies:
        copy.wait()
    _, row, column = position()

    def fill(down, up):
        for f in range(V):
            down[0, f : f + 1] = x_bottom[f, 7:8, :]
            down[1, f : f + 1] = x_bottom[f, 6:7, :]
            down[2, f : f + 1] = d_bottom[f].astype(F32)[15:16]
            up[0, f : f + 1] = x_top[f, 0:1, :]
            up[1, f : f + 1] = x_top[f, 1:2, :]
            up[2, f : f + 1] = d_top[f].astype(F32)[0:1]

    by_parity(row, lambda: fill(one, two), lambda: fill(two, one))

    def put(at, value):
        params[at : at + 1, :] = jnp.full((1, WIDE), value, F32)

    for f in range(V):
        put(f, k_now[f])
    put(COURANT, c_now[0])
    put(COURANT + 1, c_now[1])
    count = nest_patch.shape[0]
    for member in range(3):
        slot = lax.rem(role_entry(entries, row, column, member, count), 9)
        put(PATCH_ROW + member, lax.div(slot, 3).astype(F32))
        put(PATCH_COL + member, lax.rem(slot, 3).astype(F32))
    put(MEMBER, (row - lax.div(entries[row, column], 9) + 1).astype(F32))


def edge(x, drive, courant, diffusion, nest_patch):
    return pl.pallas_call(
        edge_kernel,
        in_specs=[ANY] * 5,
        out_specs=[VMEM] * 3,
        out_shape=[
            pltpu.VMEM((3, V, W), F32),
            pltpu.VMEM((3, V, W), F32),
            pltpu.VMEM((16, WIDE), F32),
        ],
        scratch_shapes=[
            pltpu.VMEM((V, 8, W), F32),
            pltpu.VMEM((V, 8, W), F32),
            pltpu.VMEM((V, 16, W), BF16),
            pltpu.VMEM((V, 16, W), BF16),
            pltpu.SMEM((2,), F32),
            pltpu.SMEM((V,), F32),
            pltpu.SMEM(nest_patch.shape, jnp.int32),
            pltpu.SemaphoreType.DMA((7,)),
        ],
        compiler_params=SMALL,
        name="edge",
    )(*far(x, drive, courant, diffusion, nest_patch))


def role_entry(entries, row, column, member, count):
    nest = jnp.clip(row + member - 1, 0, count - 1)
    return entries[nest, column]


NT = (((1,), (1,)), ((), ()))


def nests_kernel(
    params, x, drive, y, mean, ends, tent_row, tent_col, two, three, force, thirds
):
    parent = position()[0] == 0

    @pl.when(parent)
    def _():
        ends[...] = jnp.zeros(ends.shape, F32)
        none = -1
        x_west, x_east = select_rows((0, 1), 128), select_rows((none, none, none, 127, 126), 128)
        d_west = select_rows((none, none, 0), 128)
        d_east = select_rows((none, none, none, none, none, 127), 128)
        picks = jnp.concatenate([x_west, x_west, x_east, x_east, d_west, d_east], axis=1)
        for f in range(V):
            parts = (
                *split2(x[f, :, 0:128]),
                *split2(x[f, :, W - 128 : W]),
                drive[f, :, 0:128],
                drive[f, :, W - 128 : W],
            )
            values = lax.dot_general(
                picks, jnp.concatenate(parts, axis=1), NT, preferred_element_type=F32
            )
            for i in range(6):
                ends[i, f : f + 1, 0:H] = values[i : i + 1]

    @pl.when(jnp.logical_not(parent))
    def _():
        for buffer in (two, three):
            buffer[0:8, :] = jnp.zeros((8, W), F32)
            buffer[H + 8 : H + 16, :] = jnp.zeros((8, W), F32)
        blocks = mean_matrix()
        zero = jnp.zeros((1, W), F32)
        tent_row[...] = row_tent()
        tent_col[...] = col_tent()

        @pl.loop(0, V)
        def _(f):
            coefs = closed(3.0 * params[pl.ds(f, 1), :][:, 0:W], params)

            def step(get, new, at):
                for r in range(0, H, CHUNK):
                    new[at + r : at + r + CHUNK, :] = step_rows(
                        get, r, coefs, force[r : r + CHUNK, :]
                    )

            force[...] = drive[f].astype(F32) * (1.0 / 3.0)
            step(between(zero, x.at[f], zero), two, 8)
            step(padded(two), three, 8)
            step(padded(three), y.at[f], 0)
            thirds[...] = dot_right(y[f], blocks)
            total = (
                thirds[pl.ds(0, PH, stride=3), :]
                + thirds[pl.ds(1, PH, stride=3), :]
                + thirds[pl.ds(2, PH, stride=3), :]
            )
            mean[f] = total * (1.0 / 9.0)


def mean_matrix():
    gap = iota((W, PW), 0) - 3 * iota((W, PW), 1)
    return jnp.where((gap >= 0) & (gap <= 2), 1.0, 0.0).astype(BF16)


def row_tent():
    tent = jnp.maximum(3 - jnp.abs(iota((256, W), 1) - 3 * iota((256, W), 0) + 2), 0)
    return tent.astype(F32).astype(BF16)


def col_tent():
    tent = jnp.maximum(3 - jnp.abs(iota((H, 256), 0) - 3 * (iota((H, 256), 1) - OFF) + 2), 0)
    return tent.astype(F32).astype(BF16)


def nests(params, x, drive):
    return pl.pallas_call(
        nests_kernel,
        in_specs=[VMEM] * 3,
        out_specs=[VMEM] * 5,
        out_shape=[
            pltpu.VMEM((V, H, W), F32),
            pltpu.VMEM((V, PH, PW), F32),
            pltpu.VMEM((6, V, 256), F32),
            pltpu.VMEM((256, W), BF16),
            pltpu.VMEM((H, 256), BF16),
        ],
        scratch_shapes=[
            pltpu.VMEM((H + 16, W), F32),
            pltpu.VMEM((H + 16, W), F32),
            pltpu.VMEM((H, W), F32),
            pltpu.VMEM((H, PW), F32),
        ],
        compiler_params=SMALL,
        name="nests",
    )(*near(params, x, drive))


def bank_kernel(params, x, drive, north, south, rows, cols, y):
    @pl.when(position()[0] == 0)
    def _():
        cols[...] = jnp.zeros(cols.shape, F32)
        picks, force_picks = select_rows(BANK_COLS, W), select_rows(IN_COLS, W)
        for f in range(V):
            for i, r in enumerate((0, *BANK_ROWS, H - 1)):
                rows[i, f : f + 1] = x[f, r : r + 1, :]
            for i, r in enumerate(IN_ROWS):
                band = drive[f, r // 16 * 16 : r // 16 * 16 + 16, :].astype(F32)
                rows[10 + i, f : f + 1] = band[r % 16 : r % 16 + 1]
            from_x = dot_nt(picks, x[f])
            from_drive = lax.dot_general(force_picks, drive[f], NT, preferred_element_type=F32)
            for i in range(8):
                cols[i, f : f + 1, 0:H] = from_x[i : i + 1]
            for i in range(4):
                cols[8 + i, f : f + 1, 0:H] = from_drive[i : i + 1]
            coefs = closed(params[f : f + 1, 0:W], params)
            get = between(north[0, f : f + 1, :], x.at[f], south[0, f : f + 1, :])
            for r in range(0, H, CHUNK):
                end = r + CHUNK
                y[f, r:end, :] = step_rows(get, r, coefs, drive[f, r:end, :].astype(F32))


def banks(params, x, drive, north, south):
    return pl.pallas_call(
        bank_kernel,
        in_specs=[VMEM] * 5,
        out_specs=[VMEM] * 3,
        out_shape=[
            pltpu.VMEM((14, V, W), F32),
            pltpu.VMEM((12, V, 256), F32),
            pltpu.VMEM((V, H, W), F32),
        ],
        compiler_params=SMALL,
        name="banks",
    )(*near(params, x, drive, north, south))


def pack_kernel(ends, from_one, from_two, one, two, north, south):
    section, row, column = position()

    def sort(up, down):
        north[...] = up[...]
        south[...] = down[...]

    lane = iota((V, 128), 1)

    def fill(to_west, to_east):
        for i in range(3):
            to_west[i, :, 0:128] = ends[i, :, 0:128]
            above = pltpu.roll(north[i, :, 0:128], H - 128, 1)
            below = pltpu.roll(south[i, :, 0:128], H - 126, 1)
            to_west[i, :, 128:256] = jnp.where(
                lane < H - 128, ends[i, :, 128:256], jnp.where(lane < H - 126, above, below)
            )
            to_east[i, :, 0:128] = ends[3 + i, :, 0:128]
            above = north[i, :, W - 128 : W]
            below = pltpu.roll(south[i, :, W - 128 : W], 126, 1)
            to_east[i, :, 128:256] = jnp.where(
                lane < H - 128, ends[3 + i, :, 128:256], jnp.where(lane >= 126, above, below)
            )

    @pl.when(section == 0)
    def _():
        by_parity(row, lambda: sort(from_two, from_one), lambda: sort(from_one, from_two))
        by_parity(column, lambda: fill(two, one), lambda: fill(one, two))


def pack(ends, from_one, from_two):
    flank, row = pltpu.VMEM((3, V, 256), F32), pltpu.VMEM((3, V, W), F32)
    return pl.pallas_call(
        pack_kernel,
        in_specs=[VMEM] * 3,
        out_specs=[VMEM] * 4,
        out_shape=[flank, flank, row, row],
        compiler_params=SMALL,
        name="pack",
    )(*near(ends, from_one, from_two))


def rims_kernel(
    params, shape, rows, cols, ends, north, south, from_one, from_two, *out
):
    *out, beyond, west, east = out
    section, row, column = position()
    count, columns = shape

    def sort(left, right):
        west[...] = left[...]
        east[...] = right[...]

    @pl.when(section == 0)
    def _():
        by_parity(column, lambda: sort(from_two, from_one), lambda: sort(from_one, from_two))
        beyond[0:V] = west[0]
        beyond[V : 2 * V] = east[0]
        k = per_field(params, (V, 1), 0)
        a0, ae, aw, as_, an = weights_of(k, params)
        has_n = jnp.where(row > 0, 1.0, 0.0)
        has_s = jnp.where(row < count - 1, 1.0, 0.0)
        has_w = jnp.where(column > 0, 1.0, 0.0)
        has_e = jnp.where(column < columns - 1, 1.0, 0.0)
        lane128 = iota((V, 128), 1)
        lane256 = iota((V, 256), 1)
        wide = WIDE
        lane_wide = iota((V, wide), 1)
        keep = jnp.where(lane_wide < 128, has_w, jnp.where(lane_wide >= 128 + W, has_e, 1.0))
        near_w, near_e = west[0], east[0]

        def join(before, middle, after):
            return jnp.concatenate([before, middle, after], axis=1)

        def with_sides(middle, left, right):
            return join(
                jnp.where(lane128 == 127, left, 0.0), middle, jnp.where(lane128 == 0, right, 0.0)
            )

        def lanes(value, at):
            return value[:, at : at + 1]

        def halo_row(near, far, force, inner, a_far, a_inner, exists):
            value = (
                a0 * near
                + ae * pltpu.roll(near, wide - 1, 1)
                + aw * pltpu.roll(near, 1, 1)
                + a_far * far
                + a_inner * inner
                + force
            )
            return value * keep * exists

        def beyond_rows(values, to_west, to_east):
            out = []
            for i in range(3):
                before = pltpu.roll(west[i, :, 128:256], to_west, 1)
                after = pltpu.roll(east[i, :, 128:256], to_east, 1)
                out.append(join(before, values[i], after))
            return out

        north_1, north_2, north_f = beyond_rows(north, 0, 256 - H)
        south_1, south_2, south_f = beyond_rows(south, 2, 254 - H)
        top = with_sides(rows[0], lanes(near_w, 0), lanes(near_e, 0))
        bottom = with_sides(rows[9], lanes(near_w, H - 1), lanes(near_e, H - 1))
        new_north = halo_row(north_1, north_2, north_f, top, an, as_, has_n)
        new_south = halo_row(south_1, south_2, south_f, bottom, as_, an, has_s)

        def with_ends(column_values, before, after):
            return jnp.where(
                lane256 == 255, before, jnp.where(lane256 == H, after, column_values)
            )

        def halo_column(near, far, force, inner, a_far, a_inner, exists, at):
            full = with_ends(near, lanes(north_1, at), lanes(south_1, at))
            value = (
                a0 * full
                + as_ * pltpu.roll(full, 255, 1)
                + an * pltpu.roll(full, 1, 1)
                + a_far * far
                + a_inner * inner
                + force
            )
            new = with_ends(value * exists, lanes(new_north, at), lanes(new_south, at))
            return full, new

        at_w, at_e = 127, 128 + W
        old_west, new_west = halo_column(near_w, west[1], west[2], ends[0], aw, ae, has_w, at_w)
        old_east, new_east = halo_column(near_e, east[1], east[2], ends[3], ae, aw, has_e, at_e)

        bank = {(0, 0): north_1, (1, 0): new_north, (0, 5): south_1, (1, 5): new_south}
        side = {(0, 0): old_west, (1, 0): new_west, (0, 5): old_east, (1, 5): new_east}
        blank = jnp.zeros((V, 128), F32)
        for i, r in enumerate(IN_ROWS):
            place, at = (1, 3, 2, 4)[i], 1 + BANK_ROWS.index(r)
            old = with_sides(rows[at], lanes(near_w, r), lanes(near_e, r))
            bank[0, place] = old
            new = (
                a0 * old
                + ae * pltpu.roll(old, wide - 1, 1)
                + aw * pltpu.roll(old, 1, 1)
                + join(blank, an * rows[at - 1] + as_ * rows[at + 1] + rows[10 + i], blank)
            )
            bank[1, place] = jnp.where(
                lane_wide == 127,
                lanes(new_west, r),
                jnp.where(lane_wide == 128 + W, lanes(new_east, r), new),
            )
        for i, c in enumerate(IN_COLS):
            place, at = (1, 3, 2, 4)[i], BANK_COLS.index(c)
            old, new = halo_column(
                cols[at], cols[at - 1], cols[8 + i], cols[at + 1], aw, ae, 1.0, 128 + c
            )
            side[0, place] = old
            side[1, place] = new

        def choose(which, candidates):
            return jnp.where(
                which == 0.0, candidates[0], jnp.where(which == 1.0, candidates[1], candidates[2])
            )

        for member in range(3):
            at = PATCH_ROW + member
            patch_row = params[at : at + 1, :]
            at = PATCH_COL + member
            patch_col = params[at : at + 1, :]
            for time in range(2):
                for half in range(2):
                    line = choose(patch_row, [bank[time, 3 * half + i] for i in range(3)])
                    rim = choose(
                        patch_col[:, 0:W], [line[:, i * PW : i * PW + W] for i in range(3)]
                    )
                    rim = pltpu.roll(rim, W - 127, 1)[:, 0:256]
                    flank = choose(
                        patch_col[:, 0:256], [side[time, 3 * half + i] for i in range(3)]
                    )
                    flank = choose(
                        patch_row[:, 0:256],
                        [pltpu.roll(flank, OFF + 1 - PH * i, 1) for i in range(3)],
                    )
                    flank = jnp.where((lane256 >= OFF) & (lane256 < OFF + PH + 2), flank, 0.0)
                    place = (2 * time + half) * V
                    out[member][place : place + V, :] = jnp.where(lane256 < PW + 2, rim, flank)


def rims(shape, *arrays):
    def kernel(params, *refs):
        rims_kernel(params, shape, *refs)

    return pl.pallas_call(
        kernel,
        in_specs=[VMEM] * 8,
        out_specs=[VMEM] * 4,
        out_shape=[pltpu.VMEM((4 * V, 256), F32)] * 3 + [pltpu.VMEM((2 * V, 256), F32)],
        scratch_shapes=[pltpu.VMEM((3, V, 256), F32)] * 2,
        compiler_params=SMALL,
        name="rims",
    )(*near(*arrays))


def edge_effect(old, new, params, tent_row, tent_col):
    n = old.shape[0]
    k_row = 3.0 * per_field(params, (n, 1), 0)
    a0_row, ae, aw, as_, an = weights_of(k_row, params)
    upper = (iota((n, 1), 0) & V) == 0
    outer, inner = jnp.where(upper, an, as_), jnp.where(upper, as_, an)
    lane = iota((n, W), 1)
    east = jnp.where(lane == W - 1, 0.0, ae)
    west = jnp.where(lane == 0, 0.0, aw)

    def along_row(v):
        return a0_row * v + east * pltpu.roll(v, W - 1, 1) + west * pltpu.roll(v, 1, 1)

    row_effect = depths(
        dot_right(old, tent_row) * (1.0 / 3.0), dot_right(new, tent_row) * (1.0 / 3.0), outer, inner, along_row
    )

    if n == 2 * V:
        old, new, n = jnp.concatenate([old] * 3, axis=0), jnp.concatenate([new] * 3, axis=0), 3 * n
    k_col = 3.0 * per_field(params, (1, n), 1)
    a0_col, ae, aw, as_, an = weights_of(k_col, params)
    left = (iota((1, n), 1) & V) == 0
    outer, inner = jnp.where(left, aw, ae), jnp.where(left, ae, aw)
    down = iota((H, n), 0)
    south = jnp.where(down == H - 1, 0.0, as_)
    north = jnp.where(down == 0, 0.0, an)

    def along_column(v):
        return a0_col * v + south * pltpu.roll(v, H - 1, 0) + north * pltpu.roll(v, 1, 0)

    col_effect = depths(
        dot_nt(tent_col, old) * (1.0 / 3.0), dot_nt(tent_col, new) * (1.0 / 3.0), outer, inner, along_column
    )
    return row_effect, col_effect


def depths(old, new, outer, inner, along):
    third = (new - old) * (1.0 / 3.0)
    first_0 = outer * old
    second_0 = along(first_0) + outer * (old + third)
    second_1 = outer * first_0
    third_0 = along(second_0) + inner * second_1 + outer * (old + 2.0 * third)
    third_1 = along(second_1) + outer * second_0
    third_2 = outer * second_1
    return third_0, third_1, third_2


def spread(values, first=0):
    shape = (values.shape[1], 2 * V * 128)
    index, lane = iota(shape, 0) - first, iota(shape, 1)
    block, depth = index & (2 * V - 1), index >> 3
    target = block * 128 + jnp.where(block < V, depth, 127 - depth)
    valid = (index >= 0) & (depth < 3)
    return dot_right(values, jnp.where((lane == target) & valid, 1.0, 0.0).astype(BF16))


def put_sides(tile, base, f, both):
    left, right = f * 128, (V + f) * 128
    tile[f, :, 0:128] = base[f, :, 0:128] + both[:, left : left + 128]
    tile[f, :, 128 : W - 128] = base[f, :, 128 : W - 128]
    tile[f, :, W - 128 : W] = base[f, :, W - 128 : W] + both[:, right : right + 128]


def parents_kernel(
    nest_patch, params, stepped, beyond, sent_0, sent_1, sent_2, mean_0, mean_1, mean_2,
    out, tile, entries, sems,
):
    section, row, column = position()
    count = nest_patch.shape[0]
    sent, means = (sent_0, sent_1, sent_2), (mean_0, mean_1, mean_2)
    n = 2 * V

    def send(f):
        return pltpu.make_async_copy(tile.at[f], out.at[f], sems.at[f])

    @pl.when(section == 0)
    def _():
        fetch = pltpu.make_async_copy(nest_patch, entries, sems.at[V])
        fetch.start()
        _, ae, aw, _, _ = weights_of(per_field(params, (1, n), 1), params)
        eye = jnp.where(iota((H, H), 0) == iota((H, H), 1), 1.0, 0.0).astype(BF16)
        outer = jnp.where(iota((1, n), 1) < V, aw, ae)
        both = spread(dot_nt(eye, beyond[:, 0:H]) * outer)
        old = jnp.concatenate([s[0:n, :] for s in sent], axis=0)
        new = jnp.concatenate([s[n : 2 * n, :] for s in sent], axis=0)
        row_effect, col_effect = edge_effect(old, new, params, row_tent(), col_tent())
        by_row = dot_right(sum(row_effect), mean_matrix()) * (1.0 / 9.0)
        thirds = iota((PH, H), 1) - 3 * iota((PH, H), 0)
        thirds = jnp.where((thirds >= 0) & (thirds <= 2), 1.0, 0.0).astype(BF16)
        by_col = dot_left(thirds, sum(col_effect)) * (1.0 / 9.0)
        line = iota((PH, PW), 0)
        fetch.wait()
        patches = []
        for member in range(3):
            nest = row + member - 1
            entry = role_entry(entries, row, column, member, count)
            slot = lax.rem(entry, 9)
            mine = (iota(by_col.shape, 1) >> 3) == member
            patches.append(
                (
                    (nest >= 0) & (nest < count) & (lax.div(entry, 9) == row),
                    pl.multiple_of(lax.div(slot, 3) * PH, PH),
                    pl.multiple_of(lax.rem(slot, 3) * PW, PW),
                    spread(jnp.where(mine, by_col, 0.0), member * n),
                )
            )
        for f in range(V):
            put_sides(tile, stepped, f, both)
            for member, (valid, at_row, at_col, beside) in enumerate(patches):
                left, right, up = f * 128, (V + f) * 128, member * n + f
                patch = (
                    means[member][f]
                    + jnp.where(line == 0, by_row[up : up + 1], 0.0)
                    + jnp.where(line == PH - 1, by_row[up + V : up + V + 1], 0.0)
                    + beside[:, left : left + 128]
                    + beside[:, right : right + 128]
                )

                @pl.when(valid)
                def _(at_row=at_row, at_col=at_col, patch=patch):
                    tile[f, pl.ds(at_row, PH), pl.ds(at_col, PW)] = patch

            send(f).start()

        for f in range(V):
            send(f).wait()


def parents(nest_patch, *arrays):
    return pl.pallas_call(
        parents_kernel,
        in_specs=[ANY] + [VMEM] * 9,
        out_specs=ANY,
        out_shape=jax.ShapeDtypeStruct((V, H, W), F32),
        scratch_shapes=[
            pltpu.VMEM((V, H, W), F32),
            pltpu.SMEM(nest_patch.shape, jnp.int32),
            pltpu.SemaphoreType.DMA((V + 1,)),
        ],
        compiler_params=SMALL,
        name="parents",
    )(*far(nest_patch), *near(*arrays))


def last_kernel(done, params, y, tent_row, tent_col, got_0, got_1, got_2, out, tile, sems):
    del done
    got = (got_0, got_1, got_2)
    n = 2 * V

    def send(f):
        return pltpu.make_async_copy(tile.at[f], out.at[f], sems.at[f])

    @pl.when(position()[0] != 0)
    def _():
        member = params[MEMBER : MEMBER + 1, 0:256]
        u = jnp.where(
            member == 0.0, got[0][...], jnp.where(member == 1.0, got[1][...], got[2][...])
        )
        row_effect, col_effect = edge_effect(
            u[0:n], u[n : 2 * n], params, tent_row[...], tent_col[...]
        )
        depth = iota(col_effect[0].shape, 1) >> 3
        both = spread(
            jnp.where(
                depth == 0, col_effect[0], jnp.where(depth == 1, col_effect[1], col_effect[2])
            )
        )
        for f in range(V):
            put_sides(tile, y, f, both)
            for depth in range(3):
                bottom = H - 1 - depth
                tile[f, depth : depth + 1, :] = (
                    tile[f, depth : depth + 1, :] + row_effect[depth][f : f + 1]
                )
                tile[f, bottom : bottom + 1, :] = (
                    tile[f, bottom : bottom + 1, :] + row_effect[depth][V + f : V + f + 1]
                )
            send(f).start()

        for f in range(V):
            send(f).wait()


def last(done, *arrays):
    return pl.pallas_call(
        last_kernel,
        in_specs=[ANY] + [VMEM] * 7,
        out_specs=ANY,
        out_shape=jax.ShapeDtypeStruct((V, H, W), F32),
        input_output_aliases={0: 0},
        scratch_shapes=[pltpu.VMEM((V, H, W), F32), pltpu.SemaphoreType.DMA((V,))],
        compiler_params=SMALL,
        name="last",
    )(done, *near(*arrays))


def routes(sizes, source, move):
    _, n_rows, n_cols = sizes
    out = []
    for r in range(n_rows):
        for c in range(n_cols):
            to_sec, to_r, to_c = move(r, c)
            if 0 <= to_r < n_rows and 0 <= to_c < n_cols:
                out.append(
                    (
                        (source * n_rows + r) * n_cols + c,
                        (to_sec * n_rows + to_r) * n_cols + to_c,
                    )
                )
    return out


def on_device(sizes, *arrays):
    return compute(sizes, *arrays)


def compute(sizes, fields, forcing, courant, diffusion, nest_patch):
    x = fields.reshape(V, H, W)
    drive = forcing.reshape(V, H, W)
    courant = courant.reshape(2)

    def shift(value, source, move):
        return lax.ppermute(value, AXES, routes(sizes, source, move))

    def partner(index, first):
        return index + 1 if index % 2 == first else index - 1

    rows_one, rows_two, params = edge(x, drive, courant, diffusion, nest_patch)
    rows_one = shift(rows_one, 0, lambda r, c: (0, partner(r, 0), c))
    rows_two = shift(rows_two, 0, lambda r, c: (0, partner(r, 1), c))
    y, mean, ends, *tents = nests(params, x, drive)
    means = [shift(mean, 1, lambda r, c, m=m: (0, r + 1 - m, c)) for m in range(3)]
    cols_one, cols_two, north, south = pack(ends, rows_one, rows_two)
    cols_one = shift(cols_one, 0, lambda r, c: (0, r, partner(c, 0)))
    cols_two = shift(cols_two, 0, lambda r, c: (0, r, partner(c, 1)))
    rows, cols, stepped = banks(params, x, drive, north, south)
    *sent, beyond = rims(
        sizes[1:], params, rows, cols, ends, north, south, cols_one, cols_two
    )
    got = [shift(sent[m], 0, lambda r, c, m=m: (1, r + m - 1, c)) for m in range(3)]
    done = parents(nest_patch, params, stepped, beyond, *sent, *means)
    out = last(done, params, y, *tents, *got)
    return out.reshape(fields.shape)


def solution(mesh):
    sizes = tuple(mesh.shape[axis] for axis in AXES)
    spec = P("sec", None, None, "gy", "gx")
    return jax.shard_map(
        functools.partial(on_device, sizes),
        mesh=mesh,
        in_specs=(spec, spec, P(), P(), P()),
        out_specs=spec,
        check_vma=False,
    )
```

```python
import functools

import jax
import jax.numpy as jnp
from jax import lax
from jax.experimental import pallas as pl
from jax.experimental.pallas import tpu as pltpu
from jax.sharding import PartitionSpec as P


F32 = jnp.float32
BF16 = jnp.bfloat16
V, H, W = 4, 192, 384
PH, PW = H // 3, W // 3
CHUNK = 16
OFF = 160


def inner(n):
    lines = (n - 1, n, 2 * n - 1, 2 * n)
    return lines, (n - 2, n - 1, n, n + 1, 2 * n - 2, 2 * n - 1, 2 * n, 2 * n + 1)


IN_ROWS, BANK_ROWS = inner(PH)
IN_COLS, BANK_COLS = inner(PW)
WIDE = W + 256
COURANT, PATCH_ROW, PATCH_COL, MEMBER = V, V + 2, V + 5, V + 8
AXES = ("sec", "gy", "gx")
VMEM = pl.BlockSpec(memory_space=pltpu.VMEM)
ANY = pl.BlockSpec(memory_space=pl.ANY)
SMALL = pltpu.CompilerParams(vmem_limit_bytes=16 << 20)


def iota(shape, dim):
    return lax.broadcasted_iota(jnp.int32, shape, dim)


def split2(a):
    high = a.astype(BF16)
    return high, (a - high.astype(F32)).astype(BF16)


def dot_right(a, m):
    return sum(jnp.dot(part, m, preferred_element_type=F32) for part in split2(a))


def dot_nt(m, a):
    dims = (((1,), (1,)), ((), ()))
    return sum(lax.dot_general(m, part, dims, preferred_element_type=F32) for part in split2(a))


def dot_left(m, a):
    return sum(jnp.dot(m, part, preferred_element_type=F32) for part in split2(a))


def select_rows(picks, width):
    row, lane = iota((16, width), 0), iota((16, width), 1)
    wanted = jnp.full((16, width), -1, jnp.int32)
    for i, pick in enumerate(picks):
        wanted = jnp.where(row == i, pick, wanted)
    return jnp.where(lane == wanted, 1.0, 0.0).astype(BF16)


def weights(k, params):
    width = k.shape[1]
    half_x = 0.5 * params[COURANT : COURANT + 1, 0:width]
    half_y = 0.5 * params[COURANT + 1 : COURANT + 2, 0:width]
    return 1.0 - 4.0 * k, k - half_x, k + half_x, k - half_y, k + half_y


def per_field(params, shape, dim):
    index = iota(shape, dim) & (V - 1)
    out = jnp.broadcast_to(params[0:1, 0:1], shape)
    for f in range(1, V):
        out = jnp.where(index == f, params[f : f + 1, 0:1], out)
    return out


def weights_of(k, params):
    half_x = 0.5 * params[COURANT : COURANT + 1, 0:1]
    half_y = 0.5 * params[COURANT + 1 : COURANT + 2, 0:1]
    return 1.0 - 4.0 * k, k - half_x, k + half_x, k - half_y, k + half_y


def closed(k, params):
    a0, east, west, south, north = weights(k, params)
    lane = iota((1, W), 1)
    return a0, jnp.where(lane == W - 1, 0.0, east), jnp.where(lane == 0, 0.0, west), south, north


def step_rows(get, r, coefs, force):
    a0, east, west, south, north = coefs
    centre = get(r)
    return (
        a0 * centre
        + east * pltpu.roll(centre, W - 1, 1)
        + west * pltpu.roll(centre, 1, 1)
        + south * get(r + 1)
        + north * get(r - 1)
        + force
    )


def padded(ref):
    return lambda r: ref[8 + r : 8 + r + CHUNK, :]


def between(before, ref, after):
    def get(r):
        if r < 0:
            return jnp.concatenate([before, ref[0 : CHUNK - 1, :]], axis=0)
        if r + CHUNK > H:
            return jnp.concatenate([ref[r:H, :], after], axis=0)
        return ref[r : r + CHUNK, :]

    return get


def near(*values):
    return [pltpu.with_memory_space_constraint(v, pltpu.VMEM) for v in values]


def far(*values):
    return [pltpu.with_memory_space_constraint(v, pltpu.HBM) for v in values]


def position():
    return [lax.axis_index(axis) for axis in AXES]


def by_parity(index, even, odd):
    pl.when(lax.rem(index, 2) == 0)(even)
    pl.when(lax.rem(index, 2) == 1)(odd)


def edge_kernel(
    x, drive, courant, diffusion, nest_patch, one, two, params,
    x_top, x_bottom, d_top, d_bottom, c_now, k_now, entries, sems,
):
    copies = [
        pltpu.make_async_copy(source, target, sems.at[i])
        for i, (source, target) in enumerate(
            (
                (x.at[:, 0:8, :], x_top),
                (x.at[:, H - 8 : H, :], x_bottom),
                (drive.at[:, 0:16, :], d_top),
                (drive.at[:, H - 16 : H, :], d_bottom),
                (courant, c_now),
                (diffusion, k_now),
                (nest_patch, entries),
            )
        )
    ]
    for copy in copies:
        copy.start()
    for copy in copies:
        copy.wait()
    _, row, column = position()

    def fill(down, up):
        for f in range(V):
            down[0, f : f + 1] = x_bottom[f, 7:8, :]
            down[1, f : f + 1] = x_bottom[f, 6:7, :]
            down[2, f : f + 1] = d_bottom[f].astype(F32)[15:16]
            up[0, f : f + 1] = x_top[f, 0:1, :]
            up[1, f : f + 1] = x_top[f, 1:2, :]
            up[2, f : f + 1] = d_top[f].astype(F32)[0:1]

    by_parity(row, lambda: fill(one, two), lambda: fill(two, one))

    def put(at, value):
        params[at : at + 1, :] = jnp.full((1, WIDE), value, F32)

    for f in range(V):
        put(f, k_now[f])
    put(COURANT, c_now[0])
    put(COURANT + 1, c_now[1])
    count = nest_patch.shape[0]
    for member in range(3):
        slot = lax.rem(role_entry(entries, row, column, member, count), 9)
        put(PATCH_ROW + member, lax.div(slot, 3).astype(F32))
        put(PATCH_COL + member, lax.rem(slot, 3).astype(F32))
    put(MEMBER, (row - lax.div(entries[row, column], 9) + 1).astype(F32))


def edge(x, drive, courant, diffusion, nest_patch):
    return pl.pallas_call(
        edge_kernel,
        in_specs=[ANY] * 5,
        out_specs=[VMEM] * 3,
        out_shape=[
            pltpu.VMEM((3, V, W), F32),
            pltpu.VMEM((3, V, W), F32),
            pltpu.VMEM((16, WIDE), F32),
        ],
        scratch_shapes=[
            pltpu.VMEM((V, 8, W), F32),
            pltpu.VMEM((V, 8, W), F32),
            pltpu.VMEM((V, 16, W), BF16),
            pltpu.VMEM((V, 16, W), BF16),
            pltpu.SMEM((2,), F32),
            pltpu.SMEM((V,), F32),
            pltpu.SMEM(nest_patch.shape, jnp.int32),
            pltpu.SemaphoreType.DMA((7,)),
        ],
        compiler_params=SMALL,
        name="edge",
    )(*far(x, drive, courant, diffusion, nest_patch))


def role_entry(entries, row, column, member, count):
    nest = jnp.clip(row + member - 1, 0, count - 1)
    return entries[nest, column]


NT = (((1,), (1,)), ((), ()))


def nests_kernel(
    params, x, drive, y, mean, ends, tent_row, tent_col, two, three, force, thirds
):
    parent = position()[0] == 0

    @pl.when(parent)
    def _():
        ends[...] = jnp.zeros(ends.shape, F32)
        none = -1
        x_west, x_east = select_rows((0, 1), 128), select_rows((none, none, none, 127, 126), 128)
        d_west = select_rows((none, none, 0), 128)
        d_east = select_rows((none, none, none, none, none, 127), 128)
        picks = jnp.concatenate([x_west, x_west, x_east, x_east, d_west, d_east], axis=1)
        for f in range(V):
            parts = (
                *split2(x[f, :, 0:128]),
                *split2(x[f, :, W - 128 : W]),
                drive[f, :, 0:128],
                drive[f, :, W - 128 : W],
            )
            values = lax.dot_general(
                picks, jnp.concatenate(parts, axis=1), NT, preferred_element_type=F32
            )
            for i in range(6):
                ends[i, f : f + 1, 0:H] = values[i : i + 1]

    @pl.when(jnp.logical_not(parent))
    def _():
        for buffer in (two, three):
            buffer[0:8, :] = jnp.zeros((8, W), F32)
            buffer[H + 8 : H + 16, :] = jnp.zeros((8, W), F32)
        blocks = mean_matrix()
        zero = jnp.zeros((1, W), F32)
        tent_row[...] = row_tent()
        tent_col[...] = col_tent()

        @pl.loop(0, V)
        def _(f):
            coefs = closed(3.0 * params[pl.ds(f, 1), :][:, 0:W], params)

            def step(get, new, at):
                for r in range(0, H, CHUNK):
                    new[at + r : at + r + CHUNK, :] = step_rows(
                        get, r, coefs, force[r : r + CHUNK, :]
                    )

            force[...] = drive[f].astype(F32) * (1.0 / 3.0)
            step(between(zero, x.at[f], zero), two, 8)
            step(padded(two), three, 8)
            step(padded(three), y.at[f], 0)
            thirds[...] = dot_right(y[f], blocks)
            total = (
                thirds[pl.ds(0, PH, stride=3), :]
                + thirds[pl.ds(1, PH, stride=3), :]
                + thirds[pl.ds(2, PH, stride=3), :]
            )
            mean[f] = total * (1.0 / 9.0)


def mean_matrix():
    gap = iota((W, PW), 0) - 3 * iota((W, PW), 1)
    return jnp.where((gap >= 0) & (gap <= 2), 1.0, 0.0).astype(BF16)


def row_tent():
    tent = jnp.maximum(3 - jnp.abs(iota((256, W), 1) - 3 * iota((256, W), 0) + 2), 0)
    return tent.astype(F32).astype(BF16)


def col_tent():
    tent = jnp.maximum(3 - jnp.abs(iota((H, 256), 0) - 3 * (iota((H, 256), 1) - OFF) + 2), 0)
    return tent.astype(F32).astype(BF16)


def nests(params, x, drive):
    return pl.pallas_call(
        nests_kernel,
        in_specs=[VMEM] * 3,
        out_specs=[VMEM] * 5,
        out_shape=[
            pltpu.VMEM((V, H, W), F32),
            pltpu.VMEM((V, PH, PW), F32),
            pltpu.VMEM((6, V, 256), F32),
            pltpu.VMEM((256, W), BF16),
            pltpu.VMEM((H, 256), BF16),
        ],
        scratch_shapes=[
            pltpu.VMEM((H + 16, W), F32),
            pltpu.VMEM((H + 16, W), F32),
            pltpu.VMEM((H, W), F32),
            pltpu.VMEM((H, PW), F32),
        ],
        compiler_params=SMALL,
        name="nests",
    )(*near(params, x, drive))


def bank_kernel(params, x, drive, north, south, rows, cols, y):
    @pl.when(position()[0] == 0)
    def _():
        cols[...] = jnp.zeros(cols.shape, F32)
        picks, force_picks = select_rows(BANK_COLS, W), select_rows(IN_COLS, W)
        for f in range(V):
            for i, r in enumerate((0, *BANK_ROWS, H - 1)):
                rows[i, f : f + 1] = x[f, r : r + 1, :]
            for i, r in enumerate(IN_ROWS):
                band = drive[f, r // 16 * 16 : r // 16 * 16 + 16, :].astype(F32)
                rows[10 + i, f : f + 1] = band[r % 16 : r % 16 + 1]
            from_x = dot_nt(picks, x[f])
            from_drive = lax.dot_general(force_picks, drive[f], NT, preferred_element_type=F32)
            for i in range(8):
                cols[i, f : f + 1, 0:H] = from_x[i : i + 1]
            for i in range(4):
                cols[8 + i, f : f + 1, 0:H] = from_drive[i : i + 1]
            coefs = closed(params[f : f + 1, 0:W], params)
            get = between(north[0, f : f + 1, :], x.at[f], south[0, f : f + 1, :])
            for r in range(0, H, CHUNK):
                end = r + CHUNK
                y[f, r:end, :] = step_rows(get, r, coefs, drive[f, r:end, :].astype(F32))


def banks(params, x, drive, north, south):
    return pl.pallas_call(
        bank_kernel,
        in_specs=[VMEM] * 5,
        out_specs=[VMEM] * 3,
        out_shape=[
            pltpu.VMEM((14, V, W), F32),
            pltpu.VMEM((12, V, 256), F32),
            pltpu.VMEM((V, H, W), F32),
        ],
        compiler_params=SMALL,
        name="banks",
    )(*near(params, x, drive, north, south))


def pack_kernel(ends, from_one, from_two, one, two, north, south):
    section, row, column = position()

    def sort(up, down):
        north[...] = up[...]
        south[...] = down[...]

    lane = iota((V, 128), 1)

    def fill(to_west, to_east):
        for i in range(3):
            to_west[i, :, 0:128] = ends[i, :, 0:128]
            above = pltpu.roll(north[i, :, 0:128], H - 128, 1)
            below = pltpu.roll(south[i, :, 0:128], H - 126, 1)
            to_west[i, :, 128:256] = jnp.where(
                lane < H - 128, ends[i, :, 128:256], jnp.where(lane < H - 126, above, below)
            )
            to_east[i, :, 0:128] = ends[3 + i, :, 0:128]
            above = north[i, :, W - 128 : W]
            below = pltpu.roll(south[i, :, W - 128 : W], 126, 1)
            to_east[i, :, 128:256] = jnp.where(
                lane < H - 128, ends[3 + i, :, 128:256], jnp.where(lane >= 126, above, below)
            )

    @pl.when(section == 0)
    def _():
        by_parity(row, lambda: sort(from_two, from_one), lambda: sort(from_one, from_two))
        by_parity(column, lambda: fill(two, one), lambda: fill(one, two))


def pack(ends, from_one, from_two):
    flank, row = pltpu.VMEM((3, V, 256), F32), pltpu.VMEM((3, V, W), F32)
    return pl.pallas_call(
        pack_kernel,
        in_specs=[VMEM] * 3,
        out_specs=[VMEM] * 4,
        out_shape=[flank, flank, row, row],
        compiler_params=SMALL,
        name="pack",
    )(*near(ends, from_one, from_two))


def rims_kernel(
    params, shape, rows, cols, ends, north, south, from_one, from_two, *out
):
    *out, beyond, west, east = out
    section, row, column = position()
    count, columns = shape

    def sort(left, right):
        west[...] = left[...]
        east[...] = right[...]

    @pl.when(section == 0)
    def _():
        by_parity(column, lambda: sort(from_two, from_one), lambda: sort(from_one, from_two))
        beyond[0:V] = west[0]
        beyond[V : 2 * V] = east[0]
        k = per_field(params, (V, 1), 0)
        a0, ae, aw, as_, an = weights_of(k, params)
        has_n = jnp.where(row > 0, 1.0, 0.0)
        has_s = jnp.where(row < count - 1, 1.0, 0.0)
        has_w = jnp.where(column > 0, 1.0, 0.0)
        has_e = jnp.where(column < columns - 1, 1.0, 0.0)
        lane128 = iota((V, 128), 1)
        lane256 = iota((V, 256), 1)
        wide = WIDE
        lane_wide = iota((V, wide), 1)
        keep = jnp.where(lane_wide < 128, has_w, jnp.where(lane_wide >= 128 + W, has_e, 1.0))
        near_w, near_e = west[0], east[0]

        def join(before, middle, after):
            return jnp.concatenate([before, middle, after], axis=1)

        def with_sides(middle, left, right):
            return join(
                jnp.where(lane128 == 127, left, 0.0), middle, jnp.where(lane128 == 0, right, 0.0)
            )

        def lanes(value, at):
            return value[:, at : at + 1]

        def halo_row(near, far, force, inner, a_far, a_inner, exists):
            value = (
                a0 * near
                + ae * pltpu.roll(near, wide - 1, 1)
                + aw * pltpu.roll(near, 1, 1)
                + a_far * far
                + a_inner * inner
                + force
            )
            return value * keep * exists

        def beyond_rows(values, to_west, to_east):
            out = []
            for i in range(3):
                before = pltpu.roll(west[i, :, 128:256], to_west, 1)
                after = pltpu.roll(east[i, :, 128:256], to_east, 1)
                out.append(join(before, values[i], after))
            return out

        north_1, north_2, north_f = beyond_rows(north, 0, 256 - H)
        south_1, south_2, south_f = beyond_rows(south, 2, 254 - H)
        top = with_sides(rows[0], lanes(near_w, 0), lanes(near_e, 0))
        bottom = with_sides(rows[9], lanes(near_w, H - 1), lanes(near_e, H - 1))
        new_north = halo_row(north_1, north_2, north_f, top, an, as_, has_n)
        new_south = halo_row(south_1, south_2, south_f, bottom, as_, an, has_s)

        def with_ends(column_values, before, after):
            return jnp.where(
                lane256 == 255, before, jnp.where(lane256 == H, after, column_values)
            )

        def halo_column(near, far, force, inner, a_far, a_inner, exists, at):
            full = with_ends(near, lanes(north_1, at), lanes(south_1, at))
            value = (
                a0 * full
                + as_ * pltpu.roll(full, 255, 1)
                + an * pltpu.roll(full, 1, 1)
                + a_far * far
                + a_inner * inner
                + force
            )
            new = with_ends(value * exists, lanes(new_north, at), lanes(new_south, at))
            return full, new

        at_w, at_e = 127, 128 + W
        old_west, new_west = halo_column(near_w, west[1], west[2], ends[0], aw, ae, has_w, at_w)
        old_east, new_east = halo_column(near_e, east[1], east[2], ends[3], ae, aw, has_e, at_e)

        bank = {(0, 0): north_1, (1, 0): new_north, (0, 5): south_1, (1, 5): new_south}
        side = {(0, 0): old_west, (1, 0): new_west, (0, 5): old_east, (1, 5): new_east}
        blank = jnp.zeros((V, 128), F32)
        for i, r in enumerate(IN_ROWS):
            place, at = (1, 3, 2, 4)[i], 1 + BANK_ROWS.index(r)
            old = with_sides(rows[at], lanes(near_w, r), lanes(near_e, r))
            bank[0, place] = old
            new = (
                a0 * old
                + ae * pltpu.roll(old, wide - 1, 1)
                + aw * pltpu.roll(old, 1, 1)
                + join(blank, an * rows[at - 1] + as_ * rows[at + 1] + rows[10 + i], blank)
            )
            bank[1, place] = jnp.where(
                lane_wide == 127,
                lanes(new_west, r),
                jnp.where(lane_wide == 128 + W, lanes(new_east, r), new),
            )
        for i, c in enumerate(IN_COLS):
            place, at = (1, 3, 2, 4)[i], BANK_COLS.index(c)
            old, new = halo_column(
                cols[at], cols[at - 1], cols[8 + i], cols[at + 1], aw, ae, 1.0, 128 + c
            )
            side[0, place] = old
            side[1, place] = new

        def choose(which, candidates):
            return jnp.where(
                which == 0.0, candidates[0], jnp.where(which == 1.0, candidates[1], candidates[2])
            )

        for member in range(3):
            at = PATCH_ROW + member
            patch_row = params[at : at + 1, :]
            at = PATCH_COL + member
            patch_col = params[at : at + 1, :]
            for time in range(2):
                for half in range(2):
                    line = choose(patch_row, [bank[time, 3 * half + i] for i in range(3)])
                    rim = choose(
                        patch_col[:, 0:W], [line[:, i * PW : i * PW + W] for i in range(3)]
                    )
                    rim = pltpu.roll(rim, W - 127, 1)[:, 0:256]
                    flank = choose(
                        patch_col[:, 0:256], [side[time, 3 * half + i] for i in range(3)]
                    )
                    flank = choose(
                        patch_row[:, 0:256],
                        [pltpu.roll(flank, OFF + 1 - PH * i, 1) for i in range(3)],
                    )
                    flank = jnp.where((lane256 >= OFF) & (lane256 < OFF + PH + 2), flank, 0.0)
                    place = (2 * time + half) * V
                    out[member][place : place + V, :] = jnp.where(lane256 < PW + 2, rim, flank)


def rims(shape, *arrays):
    def kernel(params, *refs):
        rims_kernel(params, shape, *refs)

    return pl.pallas_call(
        kernel,
        in_specs=[VMEM] * 8,
        out_specs=[VMEM] * 4,
        out_shape=[pltpu.VMEM((4 * V, 256), F32)] * 3 + [pltpu.VMEM((2 * V, 256), F32)],
        scratch_shapes=[pltpu.VMEM((3, V, 256), F32)] * 2,
        compiler_params=SMALL,
        name="rims",
    )(*near(*arrays))


def edge_effect(old, new, params, tent_row, tent_col):
    n = old.shape[0]
    k_row = 3.0 * per_field(params, (n, 1), 0)
    a0_row, ae, aw, as_, an = weights_of(k_row, params)
    upper = (iota((n, 1), 0) & V) == 0
    outer, inner = jnp.where(upper, an, as_), jnp.where(upper, as_, an)
    lane = iota((n, W), 1)
    east = jnp.where(lane == W - 1, 0.0, ae)
    west = jnp.where(lane == 0, 0.0, aw)

    def along_row(v):
        return a0_row * v + east * pltpu.roll(v, W - 1, 1) + west * pltpu.roll(v, 1, 1)

    row_effect = depths(
        dot_right(old, tent_row) * (1.0 / 3.0), dot_right(new, tent_row) * (1.0 / 3.0), outer, inner, along_row
    )

    if n == 2 * V:
        old, new, n = jnp.concatenate([old] * 3, axis=0), jnp.concatenate([new] * 3, axis=0), 3 * n
    k_col = 3.0 * per_field(params, (1, n), 1)
    a0_col, ae, aw, as_, an = weights_of(k_col, params)
    left = (iota((1, n), 1) & V) == 0
    outer, inner = jnp.where(left, aw, ae), jnp.where(left, ae, aw)
    down = iota((H, n), 0)
    south = jnp.where(down == H - 1, 0.0, as_)
    north = jnp.where(down == 0, 0.0, an)

    def along_column(v):
        return a0_col * v + south * pltpu.roll(v, H - 1, 0) + north * pltpu.roll(v, 1, 0)

    col_effect = depths(
        dot_nt(tent_col, old) * (1.0 / 3.0), dot_nt(tent_col, new) * (1.0 / 3.0), outer, inner, along_column
    )
    return row_effect, col_effect


def depths(old, new, outer, inner, along):
    third = (new - old) * (1.0 / 3.0)
    first_0 = outer * old
    second_0 = along(first_0) + outer * (old + third)
    second_1 = outer * first_0
    third_0 = along(second_0) + inner * second_1 + outer * (old + 2.0 * third)
    third_1 = along(second_1) + outer * second_0
    third_2 = outer * second_1
    return third_0, third_1, third_2


def spread(values):
    shape = (values.shape[1], 2 * V * 128)
    index, lane = iota(shape, 0), iota(shape, 1)
    block, depth = index & (2 * V - 1), index >> 3
    target = block * 128 + jnp.where(block < V, depth, 127 - depth)
    return dot_right(values, jnp.where(lane == target, 1.0, 0.0).astype(BF16))


def put_sides(tile, base, f, both):
    left, right = f * 128, (V + f) * 128
    tile[f, :, 0:128] = base[f, :, 0:128] + both[:, left : left + 128]
    tile[f, :, 128 : W - 128] = base[f, :, 128 : W - 128]
    tile[f, :, W - 128 : W] = base[f, :, W - 128 : W] + both[:, right : right + 128]


def parents_kernel(
    nest_patch, params, stepped, beyond, sent_0, sent_1, sent_2, mean_0, mean_1, mean_2,
    out, tile, entries, sems,
):
    section, row, column = position()
    count = nest_patch.shape[0]
    sent, means = (sent_0, sent_1, sent_2), (mean_0, mean_1, mean_2)
    n = 2 * V

    def send(f):
        return pltpu.make_async_copy(tile.at[f], out.at[f], sems.at[f])

    @pl.when(section == 0)
    def _():
        fetch = pltpu.make_async_copy(nest_patch, entries, sems.at[V])
        fetch.start()
        _, ae, aw, _, _ = weights_of(per_field(params, (1, n), 1), params)
        eye = jnp.where(iota((H, H), 0) == iota((H, H), 1), 1.0, 0.0).astype(BF16)
        outer = jnp.where(iota((1, n), 1) < V, aw, ae)
        both = spread(dot_nt(eye, beyond[:, 0:H]) * outer)
        old = jnp.concatenate([s[0:n, :] for s in sent], axis=0)
        new = jnp.concatenate([s[n : 2 * n, :] for s in sent], axis=0)
        row_effect, col_effect = edge_effect(old, new, params, row_tent(), col_tent())
        by_row = dot_right(sum(row_effect), mean_matrix()) * (1.0 / 9.0)
        thirds = iota((PH, H), 1) - 3 * iota((PH, H), 0)
        thirds = jnp.where((thirds >= 0) & (thirds <= 2), 1.0, 0.0).astype(BF16)
        by_col = dot_left(thirds, sum(col_effect)) * (1.0 / 9.0)
        line, lane = iota((PH, PW), 0), iota((PH, PW), 1)
        fetch.wait()
        patches = []
        for member in range(3):
            nest = row + member - 1
            entry = role_entry(entries, row, column, member, count)
            slot = lax.rem(entry, 9)
            patches.append(
                (
                    (nest >= 0) & (nest < count) & (lax.div(entry, 9) == row),
                    pl.multiple_of(lax.div(slot, 3) * PH, PH),
                    pl.multiple_of(lax.rem(slot, 3) * PW, PW),
                )
            )
        for f in range(V):
            put_sides(tile, stepped, f, both)
            for member, (valid, at_row, at_col) in enumerate(patches):
                up = member * n + f
                patch = (
                    means[member][f]
                    + jnp.where(line == 0, by_row[up : up + 1], 0.0)
                    + jnp.where(line == PH - 1, by_row[up + V : up + V + 1], 0.0)
                    + jnp.where(lane == 0, by_col[:, up : up + 1], 0.0)
                    + jnp.where(lane == PW - 1, by_col[:, up + V : up + V + 1], 0.0)
                )

                @pl.when(valid)
                def _(at_row=at_row, at_col=at_col, patch=patch):
                    tile[f, pl.ds(at_row, PH), pl.ds(at_col, PW)] = patch

            send(f).start()

        for f in range(V):
            send(f).wait()


def parents(nest_patch, *arrays):
    return pl.pallas_call(
        parents_kernel,
        in_specs=[ANY] + [VMEM] * 9,
        out_specs=ANY,
        out_shape=jax.ShapeDtypeStruct((V, H, W), F32),
        scratch_shapes=[
            pltpu.VMEM((V, H, W), F32),
            pltpu.SMEM(nest_patch.shape, jnp.int32),
            pltpu.SemaphoreType.DMA((V + 1,)),
        ],
        compiler_params=SMALL,
        name="parents",
    )(*far(nest_patch), *near(*arrays))


def last_kernel(done, params, y, tent_row, tent_col, got_0, got_1, got_2, out, tile, sems):
    del done
    got = (got_0, got_1, got_2)
    n = 2 * V

    def send(f):
        return pltpu.make_async_copy(tile.at[f], out.at[f], sems.at[f])

    @pl.when(position()[0] != 0)
    def _():
        member = params[MEMBER : MEMBER + 1, 0:256]
        u = jnp.where(
            member == 0.0, got[0][...], jnp.where(member == 1.0, got[1][...], got[2][...])
        )
        row_effect, col_effect = edge_effect(
            u[0:n], u[n : 2 * n], params, tent_row[...], tent_col[...]
        )
        depth = iota(col_effect[0].shape, 1) >> 3
        both = spread(
            jnp.where(
                depth == 0, col_effect[0], jnp.where(depth == 1, col_effect[1], col_effect[2])
            )
        )
        for f in range(V):
            put_sides(tile, y, f, both)
            for depth in range(3):
                bottom = H - 1 - depth
                tile[f, depth : depth + 1, :] = (
                    tile[f, depth : depth + 1, :] + row_effect[depth][f : f + 1]
                )
                tile[f, bottom : bottom + 1, :] = (
                    tile[f, bottom : bottom + 1, :] + row_effect[depth][V + f : V + f + 1]
                )
            send(f).start()

        for f in range(V):
            send(f).wait()


def last(done, *arrays):
    return pl.pallas_call(
        last_kernel,
        in_specs=[ANY] + [VMEM] * 7,
        out_specs=ANY,
        out_shape=jax.ShapeDtypeStruct((V, H, W), F32),
        input_output_aliases={0: 0},
        scratch_shapes=[pltpu.VMEM((V, H, W), F32), pltpu.SemaphoreType.DMA((V,))],
        compiler_params=SMALL,
        name="last",
    )(done, *near(*arrays))


def routes(sizes, source, move):
    _, n_rows, n_cols = sizes
    out = []
    for r in range(n_rows):
        for c in range(n_cols):
            to_sec, to_r, to_c = move(r, c)
            if 0 <= to_r < n_rows and 0 <= to_c < n_cols:
                out.append(
                    (
                        (source * n_rows + r) * n_cols + c,
                        (to_sec * n_rows + to_r) * n_cols + to_c,
                    )
                )
    return out


def on_device(sizes, *arrays):
    return compute(sizes, *arrays)


def compute(sizes, fields, forcing, courant, diffusion, nest_patch):
    x = fields.reshape(V, H, W)
    drive = forcing.reshape(V, H, W)
    courant = courant.reshape(2)

    def shift(value, source, move):
        return lax.ppermute(value, AXES, routes(sizes, source, move))

    def partner(index, first):
        return index + 1 if index % 2 == first else index - 1

    rows_one, rows_two, params = edge(x, drive, courant, diffusion, nest_patch)
    rows_one = shift(rows_one, 0, lambda r, c: (0, partner(r, 0), c))
    rows_two = shift(rows_two, 0, lambda r, c: (0, partner(r, 1), c))
    y, mean, ends, *tents = nests(params, x, drive)
    means = [shift(mean, 1, lambda r, c, m=m: (0, r + 1 - m, c)) for m in range(3)]
    cols_one, cols_two, north, south = pack(ends, rows_one, rows_two)
    cols_one = shift(cols_one, 0, lambda r, c: (0, r, partner(c, 0)))
    cols_two = shift(cols_two, 0, lambda r, c: (0, r, partner(c, 1)))
    rows, cols, stepped = banks(params, x, drive, north, south)
    *sent, beyond = rims(
        sizes[1:], params, rows, cols, ends, north, south, cols_one, cols_two
    )
    got = [shift(sent[m], 0, lambda r, c, m=m: (1, r + m - 1, c)) for m in range(3)]
    done = parents(nest_patch, params, stepped, beyond, *sent, *means)
    out = last(done, params, y, *tents, *got)
    return out.reshape(fields.shape)


def solution(mesh):
    sizes = tuple(mesh.shape[axis] for axis in AXES)
    spec = P("sec", None, None, "gy", "gx")
    return jax.shard_map(
        functools.partial(on_device, sizes),
        mesh=mesh,
        in_specs=(spec, spec, P(), P(), P()),
        out_specs=spec,
        check_vma=False,
    )
```

```python
import functools

import jax
import jax.numpy as jnp
from jax import lax
from jax.experimental import pallas as pl
from jax.experimental.pallas import tpu as pltpu
from jax.sharding import PartitionSpec as P


F32 = jnp.float32
BF16 = jnp.bfloat16
V, H, W = 4, 192, 384
PH, PW = H // 3, W // 3
CHUNK = 16
OFF = 160


def inner(n):
    lines = (n - 1, n, 2 * n - 1, 2 * n)
    return lines, (n - 2, n - 1, n, n + 1, 2 * n - 2, 2 * n - 1, 2 * n, 2 * n + 1)


IN_ROWS, BANK_ROWS = inner(PH)
IN_COLS, BANK_COLS = inner(PW)
WIDE = W + 256
COURANT, PATCH_ROW, PATCH_COL, MEMBER = V, V + 2, V + 5, V + 8
AXES = ("sec", "gy", "gx")
VMEM = pl.BlockSpec(memory_space=pltpu.VMEM)
ANY = pl.BlockSpec(memory_space=pl.ANY)
SMALL = pltpu.CompilerParams(vmem_limit_bytes=16 << 20)
PACKED = pltpu.CompilerParams(vmem_limit_bytes=16 << 20)


def iota(shape, dim):
    return lax.broadcasted_iota(jnp.int32, shape, dim)


def split2(a):
    high = a.astype(BF16)
    return high, (a - high.astype(F32)).astype(BF16)


def dot_right(a, m):
    return sum(jnp.dot(part, m, preferred_element_type=F32) for part in split2(a))


def dot_nt(m, a):
    dims = (((1,), (1,)), ((), ()))
    return sum(lax.dot_general(m, part, dims, preferred_element_type=F32) for part in split2(a))


def dot_left(m, a):
    return sum(jnp.dot(m, part, preferred_element_type=F32) for part in split2(a))


def select_rows(picks, width):
    row, lane = iota((16, width), 0), iota((16, width), 1)
    wanted = jnp.full((16, width), -1, jnp.int32)
    for i, pick in enumerate(picks):
        wanted = jnp.where(row == i, pick, wanted)
    return jnp.where(lane == wanted, 1.0, 0.0).astype(BF16)


def weights(k, params):
    width = k.shape[1]
    half_x = 0.5 * params[COURANT : COURANT + 1, 0:width]
    half_y = 0.5 * params[COURANT + 1 : COURANT + 2, 0:width]
    return 1.0 - 4.0 * k, k - half_x, k + half_x, k - half_y, k + half_y


def per_field(params, shape, dim):
    index = iota(shape, dim) & (V - 1)
    out = jnp.broadcast_to(params[0:1, 0:1], shape)
    for f in range(1, V):
        out = jnp.where(index == f, params[f : f + 1, 0:1], out)
    return out


def weights_of(k, params):
    half_x = 0.5 * params[COURANT : COURANT + 1, 0:1]
    half_y = 0.5 * params[COURANT + 1 : COURANT + 2, 0:1]
    return 1.0 - 4.0 * k, k - half_x, k + half_x, k - half_y, k + half_y


def closed(k, params):
    a0, east, west, south, north = weights(k, params)
    lane = iota((1, W), 1)
    return a0, jnp.where(lane == W - 1, 0.0, east), jnp.where(lane == 0, 0.0, west), south, north


def step_rows(get, r, coefs, force):
    a0, east, west, south, north = coefs
    centre = get(r)
    return (
        a0 * centre
        + east * pltpu.roll(centre, W - 1, 1)
        + west * pltpu.roll(centre, 1, 1)
        + south * get(r + 1)
        + north * get(r - 1)
        + force
    )


def padded(ref):
    return lambda r: ref[8 + r : 8 + r + CHUNK, :]


def between(before, ref, after):
    def get(r):
        if r < 0:
            return jnp.concatenate([before, ref[0 : CHUNK - 1, :]], axis=0)
        if r + CHUNK > H:
            return jnp.concatenate([ref[r:H, :], after], axis=0)
        return ref[r : r + CHUNK, :]

    return get


def near(*values):
    return [pltpu.with_memory_space_constraint(v, pltpu.VMEM) for v in values]


def far(*values):
    return [pltpu.with_memory_space_constraint(v, pltpu.HBM) for v in values]


def position():
    return [lax.axis_index(axis) for axis in AXES]


def by_parity(index, even, odd):
    pl.when(lax.rem(index, 2) == 0)(even)
    pl.when(lax.rem(index, 2) == 1)(odd)


def edge_kernel(
    x, drive, courant, diffusion, nest_patch, one, two, params,
    x_top, x_bottom, d_top, d_bottom, c_now, k_now, entries, sems,
):
    copies = [
        pltpu.make_async_copy(source, target, sems.at[i])
        for i, (source, target) in enumerate(
            (
                (x.at[:, 0:8, :], x_top),
                (x.at[:, H - 8 : H, :], x_bottom),
                (drive.at[:, 0:16, :], d_top),
                (drive.at[:, H - 16 : H, :], d_bottom),
                (courant, c_now),
                (diffusion, k_now),
                (nest_patch, entries),
            )
        )
    ]
    for copy in copies:
        copy.start()
    for copy in copies:
        copy.wait()
    _, row, column = position()

    def fill(down, up):
        for f in range(V):
            down[0, f : f + 1] = x_bottom[f, 7:8, :]
            down[1, f : f + 1] = x_bottom[f, 6:7, :]
            down[2, f : f + 1] = d_bottom[f].astype(F32)[15:16]
            up[0, f : f + 1] = x_top[f, 0:1, :]
            up[1, f : f + 1] = x_top[f, 1:2, :]
            up[2, f : f + 1] = d_top[f].astype(F32)[0:1]

    by_parity(row, lambda: fill(one, two), lambda: fill(two, one))

    def put(at, value):
        params[at : at + 1, :] = jnp.full((1, WIDE), value, F32)

    for f in range(V):
        put(f, k_now[f])
    put(COURANT, c_now[0])
    put(COURANT + 1, c_now[1])
    count = nest_patch.shape[0]
    for member in range(3):
        slot = lax.rem(role_entry(entries, row, column, member, count), 9)
        put(PATCH_ROW + member, lax.div(slot, 3).astype(F32))
        put(PATCH_COL + member, lax.rem(slot, 3).astype(F32))
    put(MEMBER, (row - lax.div(entries[row, column], 9) + 1).astype(F32))


def edge(x, drive, courant, diffusion, nest_patch):
    return pl.pallas_call(
        edge_kernel,
        in_specs=[ANY] * 5,
        out_specs=[VMEM] * 3,
        out_shape=[
            pltpu.VMEM((3, V, W), F32),
            pltpu.VMEM((3, V, W), F32),
            pltpu.VMEM((16, WIDE), F32),
        ],
        scratch_shapes=[
            pltpu.VMEM((V, 8, W), F32),
            pltpu.VMEM((V, 8, W), F32),
            pltpu.VMEM((V, 16, W), BF16),
            pltpu.VMEM((V, 16, W), BF16),
            pltpu.SMEM((2,), F32),
            pltpu.SMEM((V,), F32),
            pltpu.SMEM(nest_patch.shape, jnp.int32),
            pltpu.SemaphoreType.DMA((7,)),
        ],
        compiler_params=SMALL,
        name="edge",
    )(*far(x, drive, courant, diffusion, nest_patch))


def role_entry(entries, row, column, member, count):
    nest = jnp.clip(row + member - 1, 0, count - 1)
    return entries[nest, column]


NT = (((1,), (1,)), ((), ()))


def nests_kernel(
    params, x, drive, y, mean, ends, tent_row, tent_col, two, three, force, thirds
):
    parent = position()[0] == 0

    @pl.when(parent)
    def _():
        ends[...] = jnp.zeros(ends.shape, F32)
        none = -1
        x_west, x_east = select_rows((0, 1), 128), select_rows((none, none, none, 127, 126), 128)
        d_west = select_rows((none, none, 0), 128)
        d_east = select_rows((none, none, none, none, none, 127), 128)
        picks = jnp.concatenate([x_west, x_west, x_east, x_east, d_west, d_east], axis=1)
        for f in range(V):
            parts = (
                *split2(x[f, :, 0:128]),
                *split2(x[f, :, W - 128 : W]),
                drive[f, :, 0:128],
                drive[f, :, W - 128 : W],
            )
            values = lax.dot_general(
                picks, jnp.concatenate(parts, axis=1), NT, preferred_element_type=F32
            )
            for i in range(6):
                ends[i, f : f + 1, 0:H] = values[i : i + 1]

    @pl.when(jnp.logical_not(parent))
    def _():
        for buffer in (two, three):
            buffer[0:8, :] = jnp.zeros((8, W), F32)
            buffer[H + 8 : H + 16, :] = jnp.zeros((8, W), F32)
        blocks = mean_matrix()
        zero = jnp.zeros((1, W), F32)
        tent_row[...] = row_tent()
        tent_col[...] = col_tent()

        @pl.loop(0, V)
        def _(f):
            coefs = closed(3.0 * params[pl.ds(f, 1), :][:, 0:W], params)

            def step(get, new, at):
                for r in range(0, H, CHUNK):
                    new[at + r : at + r + CHUNK, :] = step_rows(
                        get, r, coefs, force[r : r + CHUNK, :]
                    )

            force[...] = drive[f].astype(F32) * (1.0 / 3.0)
            step(between(zero, x.at[f], zero), two, 8)
            step(padded(two), three, 8)
            step(padded(three), y.at[f], 0)
            thirds[...] = dot_right(y[f], blocks)
            total = (
                thirds[pl.ds(0, PH, stride=3), :]
                + thirds[pl.ds(1, PH, stride=3), :]
                + thirds[pl.ds(2, PH, stride=3), :]
            )
            mean[f] = total * (1.0 / 9.0)


def mean_matrix():
    gap = iota((W, PW), 0) - 3 * iota((W, PW), 1)
    return jnp.where((gap >= 0) & (gap <= 2), 1.0, 0.0).astype(BF16)


def row_tent():
    tent = jnp.maximum(3 - jnp.abs(iota((256, W), 1) - 3 * iota((256, W), 0) + 2), 0)
    return tent.astype(F32).astype(BF16)


def col_tent():
    tent = jnp.maximum(3 - jnp.abs(iota((H, 256), 0) - 3 * (iota((H, 256), 1) - OFF) + 2), 0)
    return tent.astype(F32).astype(BF16)


def nests(params, x, drive):
    return pl.pallas_call(
        nests_kernel,
        in_specs=[VMEM] * 3,
        out_specs=[VMEM] * 5,
        out_shape=[
            pltpu.VMEM((V, H, W), F32),
            pltpu.VMEM((V, PH, PW), F32),
            pltpu.VMEM((6, V, 256), F32),
            pltpu.VMEM((256, W), BF16),
            pltpu.VMEM((H, 256), BF16),
        ],
        scratch_shapes=[
            pltpu.VMEM((H + 16, W), F32),
            pltpu.VMEM((H + 16, W), F32),
            pltpu.VMEM((H, W), F32),
            pltpu.VMEM((H, PW), F32),
        ],
        compiler_params=SMALL,
        name="nests",
    )(*near(params, x, drive))


def bank_kernel(params, x, drive, north, south, rows, cols, y):
    @pl.when(position()[0] == 0)
    def _():
        cols[...] = jnp.zeros(cols.shape, F32)
        picks, force_picks = select_rows(BANK_COLS, W), select_rows(IN_COLS, W)
        for f in range(V):
            for i, r in enumerate((0, *BANK_ROWS, H - 1)):
                rows[i, f : f + 1] = x[f, r : r + 1, :]
            for i, r in enumerate(IN_ROWS):
                band = drive[f, r // 16 * 16 : r // 16 * 16 + 16, :].astype(F32)
                rows[10 + i, f : f + 1] = band[r % 16 : r % 16 + 1]
            from_x = dot_nt(picks, x[f])
            from_drive = lax.dot_general(force_picks, drive[f], NT, preferred_element_type=F32)
            for i in range(8):
                cols[i, f : f + 1, 0:H] = from_x[i : i + 1]
            for i in range(4):
                cols[8 + i, f : f + 1, 0:H] = from_drive[i : i + 1]
            coefs = closed(params[f : f + 1, 0:W], params)
            get = between(north[0, f : f + 1, :], x.at[f], south[0, f : f + 1, :])
            for r in range(0, H, CHUNK):
                end = r + CHUNK
                y[f, r:end, :] = step_rows(get, r, coefs, drive[f, r:end, :].astype(F32))


def banks(params, x, drive, north, south):
    return pl.pallas_call(
        bank_kernel,
        in_specs=[VMEM] * 5,
        out_specs=[VMEM] * 3,
        out_shape=[
            pltpu.VMEM((14, V, W), F32),
            pltpu.VMEM((12, V, 256), F32),
            pltpu.VMEM((V, H, W), F32),
        ],
        compiler_params=PACKED,
        name="banks",
    )(*near(params, x, drive, north, south))


def pack_kernel(ends, from_one, from_two, one, two, north, south):
    section, row, column = position()

    def sort(up, down):
        north[...] = up[...]
        south[...] = down[...]

    lane = iota((V, 128), 1)

    def fill(to_west, to_east):
        for i in range(3):
            to_west[i, :, 0:128] = ends[i, :, 0:128]
            above = pltpu.roll(north[i, :, 0:128], H - 128, 1)
            below = pltpu.roll(south[i, :, 0:128], H - 126, 1)
            to_west[i, :, 128:256] = jnp.where(
                lane < H - 128, ends[i, :, 128:256], jnp.where(lane < H - 126, above, below)
            )
            to_east[i, :, 0:128] = ends[3 + i, :, 0:128]
            above = north[i, :, W - 128 : W]
            below = pltpu.roll(south[i, :, W - 128 : W], 126, 1)
            to_east[i, :, 128:256] = jnp.where(
                lane < H - 128, ends[3 + i, :, 128:256], jnp.where(lane >= 126, above, below)
            )

    @pl.when(section == 0)
    def _():
        by_parity(row, lambda: sort(from_two, from_one), lambda: sort(from_one, from_two))
        by_parity(column, lambda: fill(two, one), lambda: fill(one, two))


def pack(ends, from_one, from_two):
    flank, row = pltpu.VMEM((3, V, 256), F32), pltpu.VMEM((3, V, W), F32)
    return pl.pallas_call(
        pack_kernel,
        in_specs=[VMEM] * 3,
        out_specs=[VMEM] * 4,
        out_shape=[flank, flank, row, row],
        compiler_params=SMALL,
        name="pack",
    )(*near(ends, from_one, from_two))


def rims_kernel(
    params, shape, rows, cols, ends, north, south, from_one, from_two, *out
):
    *out, beyond, west, east = out
    section, row, column = position()
    count, columns = shape

    def sort(left, right):
        west[...] = left[...]
        east[...] = right[...]

    @pl.when(section == 0)
    def _():
        by_parity(column, lambda: sort(from_two, from_one), lambda: sort(from_one, from_two))
        beyond[0:V] = west[0]
        beyond[V : 2 * V] = east[0]
        k = per_field(params, (V, 1), 0)
        a0, ae, aw, as_, an = weights_of(k, params)
        has_n = jnp.where(row > 0, 1.0, 0.0)
        has_s = jnp.where(row < count - 1, 1.0, 0.0)
        has_w = jnp.where(column > 0, 1.0, 0.0)
        has_e = jnp.where(column < columns - 1, 1.0, 0.0)
        lane128 = iota((V, 128), 1)
        lane256 = iota((V, 256), 1)
        wide = WIDE
        lane_wide = iota((V, wide), 1)
        keep = jnp.where(lane_wide < 128, has_w, jnp.where(lane_wide >= 128 + W, has_e, 1.0))
        near_w, near_e = west[0], east[0]

        def join(before, middle, after):
            return jnp.concatenate([before, middle, after], axis=1)

        def with_sides(middle, left, right):
            return join(
                jnp.where(lane128 == 127, left, 0.0), middle, jnp.where(lane128 == 0, right, 0.0)
            )

        def lanes(value, at):
            return value[:, at : at + 1]

        def halo_row(near, far, force, inner, a_far, a_inner, exists):
            value = (
                a0 * near
                + ae * pltpu.roll(near, wide - 1, 1)
                + aw * pltpu.roll(near, 1, 1)
                + a_far * far
                + a_inner * inner
                + force
            )
            return value * keep * exists

        def beyond_rows(values, to_west, to_east):
            out = []
            for i in range(3):
                before = pltpu.roll(west[i, :, 128:256], to_west, 1)
                after = pltpu.roll(east[i, :, 128:256], to_east, 1)
                out.append(join(before, values[i], after))
            return out

        north_1, north_2, north_f = beyond_rows(north, 0, 256 - H)
        south_1, south_2, south_f = beyond_rows(south, 2, 254 - H)
        top = with_sides(rows[0], lanes(near_w, 0), lanes(near_e, 0))
        bottom = with_sides(rows[9], lanes(near_w, H - 1), lanes(near_e, H - 1))
        new_north = halo_row(north_1, north_2, north_f, top, an, as_, has_n)
        new_south = halo_row(south_1, south_2, south_f, bottom, as_, an, has_s)

        def with_ends(column_values, before, after):
            return jnp.where(
                lane256 == 255, before, jnp.where(lane256 == H, after, column_values)
            )

        def halo_column(near, far, force, inner, a_far, a_inner, exists, at):
            full = with_ends(near, lanes(north_1, at), lanes(south_1, at))
            value = (
                a0 * full
                + as_ * pltpu.roll(full, 255, 1)
                + an * pltpu.roll(full, 1, 1)
                + a_far * far
                + a_inner * inner
                + force
            )
            new = with_ends(value * exists, lanes(new_north, at), lanes(new_south, at))
            return full, new

        at_w, at_e = 127, 128 + W
        old_west, new_west = halo_column(near_w, west[1], west[2], ends[0], aw, ae, has_w, at_w)
        old_east, new_east = halo_column(near_e, east[1], east[2], ends[3], ae, aw, has_e, at_e)

        bank = {(0, 0): north_1, (1, 0): new_north, (0, 5): south_1, (1, 5): new_south}
        side = {(0, 0): old_west, (1, 0): new_west, (0, 5): old_east, (1, 5): new_east}
        blank = jnp.zeros((V, 128), F32)
        for i, r in enumerate(IN_ROWS):
            place, at = (1, 3, 2, 4)[i], 1 + BANK_ROWS.index(r)
            old = with_sides(rows[at], lanes(near_w, r), lanes(near_e, r))
            bank[0, place] = old
            new = (
                a0 * old
                + ae * pltpu.roll(old, wide - 1, 1)
                + aw * pltpu.roll(old, 1, 1)
                + join(blank, an * rows[at - 1] + as_ * rows[at + 1] + rows[10 + i], blank)
            )
            bank[1, place] = jnp.where(
                lane_wide == 127,
                lanes(new_west, r),
                jnp.where(lane_wide == 128 + W, lanes(new_east, r), new),
            )
        for i, c in enumerate(IN_COLS):
            place, at = (1, 3, 2, 4)[i], BANK_COLS.index(c)
            old, new = halo_column(
                cols[at], cols[at - 1], cols[8 + i], cols[at + 1], aw, ae, 1.0, 128 + c
            )
            side[0, place] = old
            side[1, place] = new

        def choose(which, candidates):
            return jnp.where(
                which == 0.0, candidates[0], jnp.where(which == 1.0, candidates[1], candidates[2])
            )

        for member in range(3):
            at = PATCH_ROW + member
            patch_row = params[at : at + 1, :]
            at = PATCH_COL + member
            patch_col = params[at : at + 1, :]
            for time in range(2):
                for half in range(2):
                    line = choose(patch_row, [bank[time, 3 * half + i] for i in range(3)])
                    rim = choose(
                        patch_col[:, 0:W], [line[:, i * PW : i * PW + W] for i in range(3)]
                    )
                    rim = pltpu.roll(rim, W - 127, 1)[:, 0:256]
                    flank = choose(
                        patch_col[:, 0:256], [side[time, 3 * half + i] for i in range(3)]
                    )
                    flank = choose(
                        patch_row[:, 0:256],
                        [pltpu.roll(flank, OFF + 1 - PH * i, 1) for i in range(3)],
                    )
                    flank = jnp.where((lane256 >= OFF) & (lane256 < OFF + PH + 2), flank, 0.0)
                    place = (2 * time + half) * V
                    out[member][place : place + V, :] = jnp.where(lane256 < PW + 2, rim, flank)


def rims(shape, *arrays):
    def kernel(params, *refs):
        rims_kernel(params, shape, *refs)

    return pl.pallas_call(
        kernel,
        in_specs=[VMEM] * 8,
        out_specs=[VMEM] * 4,
        out_shape=[pltpu.VMEM((4 * V, 256), F32)] * 3 + [pltpu.VMEM((2 * V, 256), F32)],
        scratch_shapes=[pltpu.VMEM((3, V, 256), F32)] * 2,
        compiler_params=SMALL,
        name="rims",
    )(*near(*arrays))


def edge_effect(old, new, params, tent_row, tent_col):
    n = old.shape[0]
    k_row = 3.0 * per_field(params, (n, 1), 0)
    a0_row, ae, aw, as_, an = weights_of(k_row, params)
    upper = (iota((n, 1), 0) & V) == 0
    outer, inner = jnp.where(upper, an, as_), jnp.where(upper, as_, an)
    lane = iota((n, W), 1)
    east = jnp.where(lane == W - 1, 0.0, ae)
    west = jnp.where(lane == 0, 0.0, aw)

    def along_row(v):
        return a0_row * v + east * pltpu.roll(v, W - 1, 1) + west * pltpu.roll(v, 1, 1)

    row_effect = depths(
        dot_right(old, tent_row) * (1.0 / 3.0), dot_right(new, tent_row) * (1.0 / 3.0), outer, inner, along_row
    )

    if n == 2 * V:
        old, new, n = jnp.concatenate([old] * 3, axis=0), jnp.concatenate([new] * 3, axis=0), 3 * n
    k_col = 3.0 * per_field(params, (1, n), 1)
    a0_col, ae, aw, as_, an = weights_of(k_col, params)
    left = (iota((1, n), 1) & V) == 0
    outer, inner = jnp.where(left, aw, ae), jnp.where(left, ae, aw)
    down = iota((H, n), 0)
    south = jnp.where(down == H - 1, 0.0, as_)
    north = jnp.where(down == 0, 0.0, an)

    def along_column(v):
        return a0_col * v + south * pltpu.roll(v, H - 1, 0) + north * pltpu.roll(v, 1, 0)

    col_effect = depths(
        dot_nt(tent_col, old) * (1.0 / 3.0), dot_nt(tent_col, new) * (1.0 / 3.0), outer, inner, along_column
    )
    return row_effect, col_effect


def depths(old, new, outer, inner, along):
    third = (new - old) * (1.0 / 3.0)
    first_0 = outer * old
    second_0 = along(first_0) + outer * (old + third)
    second_1 = outer * first_0
    third_0 = along(second_0) + inner * second_1 + outer * (old + 2.0 * third)
    third_1 = along(second_1) + outer * second_0
    third_2 = outer * second_1
    return third_0, third_1, third_2


def spread(values):
    shape = (values.shape[1], 2 * V * 128)
    index, lane = iota(shape, 0), iota(shape, 1)
    block, depth = index & (2 * V - 1), index >> 3
    target = block * 128 + jnp.where(block < V, depth, 127 - depth)
    return dot_right(values, jnp.where(lane == target, 1.0, 0.0).astype(BF16))


def put_sides(tile, base, f, both):
    left, right = f * 128, (V + f) * 128
    tile[f, :, 0:128] = base[f, :, 0:128] + both[:, left : left + 128]
    tile[f, :, 128 : W - 128] = base[f, :, 128 : W - 128]
    tile[f, :, W - 128 : W] = base[f, :, W - 128 : W] + both[:, right : right + 128]


def parents_kernel(
    nest_patch, params, stepped, beyond, sent_0, sent_1, sent_2, mean_0, mean_1, mean_2,
    out, tile, entries, sems,
):
    section, row, column = position()
    count = nest_patch.shape[0]
    sent, means = (sent_0, sent_1, sent_2), (mean_0, mean_1, mean_2)
    n = 2 * V

    def send(f):
        return pltpu.make_async_copy(tile.at[f], out.at[f], sems.at[f])

    @pl.when(section == 0)
    def _():
        fetch = pltpu.make_async_copy(nest_patch, entries, sems.at[V])
        fetch.start()
        _, ae, aw, _, _ = weights_of(per_field(params, (1, n), 1), params)
        eye = jnp.where(iota((H, H), 0) == iota((H, H), 1), 1.0, 0.0).astype(BF16)
        outer = jnp.where(iota((1, n), 1) < V, aw, ae)
        both = spread(dot_nt(eye, beyond[:, 0:H]) * outer)
        old = jnp.concatenate([s[0:n, :] for s in sent], axis=0)
        new = jnp.concatenate([s[n : 2 * n, :] for s in sent], axis=0)
        row_effect, col_effect = edge_effect(old, new, params, row_tent(), col_tent())
        by_row = dot_right(sum(row_effect), mean_matrix()) * (1.0 / 9.0)
        thirds = iota((PH, H), 1) - 3 * iota((PH, H), 0)
        thirds = jnp.where((thirds >= 0) & (thirds <= 2), 1.0, 0.0).astype(BF16)
        by_col = dot_left(thirds, sum(col_effect)) * (1.0 / 9.0)
        line, lane = iota((PH, PW), 0), iota((PH, PW), 1)
        fetch.wait()
        patches = []
        for member in range(3):
            nest = row + member - 1
            entry = role_entry(entries, row, column, member, count)
            slot = lax.rem(entry, 9)
            patches.append(
                (
                    (nest >= 0) & (nest < count) & (lax.div(entry, 9) == row),
                    pl.multiple_of(lax.div(slot, 3) * PH, PH),
                    pl.multiple_of(lax.rem(slot, 3) * PW, PW),
                )
            )
        for f in range(V):
            put_sides(tile, stepped, f, both)
            for member, (valid, at_row, at_col) in enumerate(patches):
                up = member * n + f

                @pl.when(valid)
                def _(member=member, f=f, up=up, at_row=at_row, at_col=at_col):
                    tile[f, pl.ds(at_row, PH), pl.ds(at_col, PW)] = (
                        means[member][f]
                        + jnp.where(line == 0, by_row[up : up + 1], 0.0)
                        + jnp.where(line == PH - 1, by_row[up + V : up + V + 1], 0.0)
                        + jnp.where(lane == 0, by_col[:, up : up + 1], 0.0)
                        + jnp.where(lane == PW - 1, by_col[:, up + V : up + V + 1], 0.0)
                    )

            send(f).start()

        for f in range(V):
            send(f).wait()


def parents(nest_patch, *arrays):
    return pl.pallas_call(
        parents_kernel,
        in_specs=[ANY] + [VMEM] * 9,
        out_specs=ANY,
        out_shape=jax.ShapeDtypeStruct((V, H, W), F32),
        scratch_shapes=[
            pltpu.VMEM((V, H, W), F32),
            pltpu.SMEM(nest_patch.shape, jnp.int32),
            pltpu.SemaphoreType.DMA((V + 1,)),
        ],
        compiler_params=SMALL,
        name="parents",
    )(*far(nest_patch), *near(*arrays))


def last_kernel(done, params, y, tent_row, tent_col, got_0, got_1, got_2, out, tile, sems):
    del done
    got = (got_0, got_1, got_2)
    n = 2 * V

    def send(f):
        return pltpu.make_async_copy(tile.at[f], out.at[f], sems.at[f])

    @pl.when(position()[0] != 0)
    def _():
        member = params[MEMBER : MEMBER + 1, 0:256]
        u = jnp.where(
            member == 0.0, got[0][...], jnp.where(member == 1.0, got[1][...], got[2][...])
        )
        row_effect, col_effect = edge_effect(
            u[0:n], u[n : 2 * n], params, tent_row[...], tent_col[...]
        )
        depth = iota(col_effect[0].shape, 1) >> 3
        both = spread(
            jnp.where(
                depth == 0, col_effect[0], jnp.where(depth == 1, col_effect[1], col_effect[2])
            )
        )
        for f in range(V):
            put_sides(tile, y, f, both)
            for depth in range(3):
                bottom = H - 1 - depth
                tile[f, depth : depth + 1, :] = (
                    tile[f, depth : depth + 1, :] + row_effect[depth][f : f + 1]
                )
                tile[f, bottom : bottom + 1, :] = (
                    tile[f, bottom : bottom + 1, :] + row_effect[depth][V + f : V + f + 1]
                )
            send(f).start()

        for f in range(V):
            send(f).wait()


def last(done, *arrays):
    return pl.pallas_call(
        last_kernel,
        in_specs=[ANY] + [VMEM] * 7,
        out_specs=ANY,
        out_shape=jax.ShapeDtypeStruct((V, H, W), F32),
        input_output_aliases={0: 0},
        scratch_shapes=[pltpu.VMEM((V, H, W), F32), pltpu.SemaphoreType.DMA((V,))],
        compiler_params=PACKED,
        name="last",
    )(done, *near(*arrays))


def routes(sizes, source, move):
    _, n_rows, n_cols = sizes
    out = []
    for r in range(n_rows):
        for c in range(n_cols):
            to_sec, to_r, to_c = move(r, c)
            if 0 <= to_r < n_rows and 0 <= to_c < n_cols:
                out.append(
                    (
                        (source * n_rows + r) * n_cols + c,
                        (to_sec * n_rows + to_r) * n_cols + to_c,
                    )
                )
    return out


def on_device(sizes, *arrays):
    return compute(sizes, *arrays)


def compute(sizes, fields, forcing, courant, diffusion, nest_patch):
    x = fields.reshape(V, H, W)
    drive = forcing.reshape(V, H, W)
    courant = courant.reshape(2)

    def shift(value, source, move):
        return lax.ppermute(value, AXES, routes(sizes, source, move))

    def partner(index, first):
        return index + 1 if index % 2 == first else index - 1

    rows_one, rows_two, params = edge(x, drive, courant, diffusion, nest_patch)
    rows_one = shift(rows_one, 0, lambda r, c: (0, partner(r, 0), c))
    rows_two = shift(rows_two, 0, lambda r, c: (0, partner(r, 1), c))
    y, mean, ends, *tents = nests(params, x, drive)
    means = [shift(mean, 1, lambda r, c, m=m: (0, r + 1 - m, c)) for m in range(3)]
    cols_one, cols_two, north, south = pack(ends, rows_one, rows_two)
    cols_one = shift(cols_one, 0, lambda r, c: (0, r, partner(c, 0)))
    cols_two = shift(cols_two, 0, lambda r, c: (0, r, partner(c, 1)))
    rows, cols, stepped = banks(params, x, drive, north, south)
    *sent, beyond = rims(
        sizes[1:], params, rows, cols, ends, north, south, cols_one, cols_two
    )
    got = [shift(sent[m], 0, lambda r, c, m=m: (1, r + m - 1, c)) for m in range(3)]
    done = parents(nest_patch, params, stepped, beyond, *sent, *means)
    out = last(done, params, y, *tents, *got)
    return out.reshape(fields.shape)


def solution(mesh):
    sizes = tuple(mesh.shape[axis] for axis in AXES)
    spec = P("sec", None, None, "gy", "gx")
    return jax.shard_map(
        functools.partial(on_device, sizes),
        mesh=mesh,
        in_specs=(spec, spec, P(), P(), P()),
        out_specs=spec,
        check_vma=False,
    )
```
